128 devices in a mesh: gx: 32 (over x_hi, z, y), gy: 4 (over x_lo, core).
Axes of the slice: x: 4 (x_hi: 2, x_lo: 2; x = x_hi * 2 + x_lo), y: 4, z: 4, core: 2. Of those that a mesh axis runs over, the one named last changes fastest.
Arguments:
- populations: float32 [27, 256, 128, 128], P(None, 'gx', 'gy'), may hold values from 0.49 to 1.69
- precursor: float32 [27, 64, 128, 128], P(None, 'gx', 'gy'), may hold values from 0.49 to 1.69
- pairing: int32 [32], replicated, may hold values from 0 to 31, each once
- rates: float32 [27], replicated, may hold values from 0.5 to 1.9
- loading: float32 [32], replicated, may hold values from 4 to 32
- disc_cols: int32 [512], replicated, may hold values from 0 to 32767, as said below
- disc_turb: int32 [512], replicated, may hold values from -1 to 31, as said below
Outputs:
- read: float32 [27, 256, 128, 128], P(None, 'gx', 'gy')
- disc_speed: float32 [32], replicated
The draws below stay inside these ranges and needn't reach their ends.
Inputs may be any that keep to these rules, and one draw needn't show every extreme that they name: `disc_cols`: each turbine's used slots name 8 to 16 spanwise-adjacent columns (periodic in y) of one streamwise plane; unused slots hold column 0. `disc_turb`: every turbine id 0..31 has 8 to 16 used slots, both counts reached; -1 marks an unused slot; slots are in no particular order.
All inputs are finite; a program needn't handle non-finite values.
Results may differ from the reference program's by a relative error of at most 0.00009.
Values sent between devices are 32-bit elements; how exact they have to be, the bound alone decides.
No kernel may reach another device: no remote copies, remote signals or barrier semaphores. Data moves between devices by JAX's collectives and lax.ppermute only.
A program may use at most 128 MiB of HBM per device.

```python
import math
import jax
import jax.numpy as jnp
import numpy as np
from jax import lax

CX = 8
FR = 2
NT = 32
DMAX = 16
NX = 256
NY = 128
NZ = 128
FRX = 64
NR = 512
N_GX = 32


def flow_factor():
    steps = (jnp.arange(27, dtype=jnp.int32) // 9 - 1).astype(jnp.float32)
    return (1.0 + 0.3 * steps).reshape(27, 1, 1, 1)


def draw_populations(key, part):
    shape = (27, NX, NY, NZ)
    noise = jax.random.uniform(key, shape, jnp.float32, -0.3, 0.3)
    return flow_factor() * (1.0 + noise)


def draw_precursor(key, part):
    shape = (27, FRX, NY, NZ)
    inner = jax.random.fold_in(key, 5)
    noise = jax.random.uniform(inner, shape, jnp.float32, -0.3, 0.3)
    return flow_factor() * (1.0 + noise)


def disc_layout(key):
    inner = jax.random.fold_in(key, 11)
    key_a, key_b, key_c, key_d = jax.random.split(inner, 4)
    planes = jax.random.randint(key_a, (NT,), 0, NX)
    centres = jax.random.randint(key_b, (NT,), 0, NY)
    spans = jax.random.randint(key_c, (NT,), DMAX // 2, DMAX + 1)
    spans = spans.at[0].set(DMAX // 2).at[1].set(DMAX)
    slots = jnp.arange(NR, dtype=jnp.int32)
    owner = slots // DMAX
    offset = slots % DMAX
    used = offset < spans[owner]
    column = planes[owner] * NY + (centres[owner] - spans[owner] // 2 + offset) % NY
    turbine = jnp.where(used, owner, -1)
    column = jnp.where(used, column, 0)
    order = jax.random.permutation(key_d, NR)
    return (column[order].astype(jnp.int32), turbine[order].astype(jnp.int32))


def draw_disc_cols(key, part):
    return disc_layout(key)[0]


def draw_disc_turb(key, part):
    return disc_layout(key)[1]


def setup_inputs(seed: int = 0) -> dict:
    key_list = jax.random.split(jax.random.key(seed), 8)
    populations = draw_populations(jax.random.fold_in(key_list[7], 71), 0)
    precursor = draw_precursor(jax.random.fold_in(key_list[7], 71), 0)
    pairing = jax.random.permutation(key_list[2], N_GX).astype(jnp.int32)
    rates = jnp.clip(jnp.exp(jax.random.uniform(key_list[3], (27,), jnp.float32, math.log(0.5), math.log(1.9))), 0.5, 1.9)
    loading = jnp.clip(jnp.exp(jax.random.uniform(key_list[4], (NT,), jnp.float32, math.log(4.0), math.log(32.0))), 4.0, 32.0)
    disc_cols = draw_disc_cols(jax.random.fold_in(key_list[7], 71), 0)
    disc_turb = draw_disc_turb(jax.random.fold_in(key_list[7], 71), 0)
    return {"populations": populations, "precursor": precursor, "pairing": pairing, "rates": rates, "loading": loading, "disc_cols": disc_cols, "disc_turb": disc_turb}


FULL_PRECISION = lax.Precision.HIGHEST


def lattice_tables():
    steps_one = np.array([-1.0, 0.0, 1.0])
    weight_one = np.array([1.0 / 6.0, 2.0 / 3.0, 1.0 / 6.0])
    grid_x, grid_y, grid_z = np.meshgrid(np.arange(3), np.arange(3), np.arange(3), indexing="ij")
    grid_x = grid_x.ravel()
    grid_y = grid_y.ravel()
    grid_z = grid_z.ravel()
    shift_x = steps_one[grid_x]
    shift_y = steps_one[grid_y]
    shift_z = steps_one[grid_z]
    weights = weight_one[grid_x] * weight_one[grid_y] * weight_one[grid_z]
    vander = np.array([[1.0, 1.0, 1.0], [-1.0, 0.0, 1.0], [1.0, 0.0, 1.0]])
    inverse = np.array([[0.0, -0.5, 0.5], [1.0, 0.0, -1.0], [0.0, 0.5, 0.5]])
    moment_map = np.kron(np.kron(vander, vander), vander) * weights[None, :]
    back_map = np.kron(np.kron(inverse, inverse), inverse) / weights[:, None]
    third = 1.0 / 3.0
    fringe_map = np.stack([weights, weights * shift_x, weights * shift_y, weights * shift_z,
                           weights * shift_x * shift_x, weights * shift_y * shift_y, weights * shift_z * shift_z,
                           weights * shift_x * shift_y, weights * shift_x * shift_z, weights * shift_y * shift_z])
    quad_x = shift_x * shift_x - third
    quad_y = shift_y * shift_y - third
    quad_z = shift_z * shift_z - third
    rebuild_map = np.stack([1.0 - 1.5 * (quad_x + quad_y + quad_z), 3.0 * shift_x, 3.0 * shift_y, 3.0 * shift_z,
                            4.5 * quad_x, 4.5 * quad_y, 4.5 * quad_z,
                            9.0 * shift_x * shift_y, 9.0 * shift_x * shift_z, 9.0 * shift_y * shift_z], axis=1)
    tables = (shift_x, shift_y, shift_z, moment_map, back_map, fringe_map, rebuild_map)
    return tuple(jnp.asarray(table, dtype=jnp.float32) for table in tables)


def disc_profile(depth):
    heights = jnp.arange(depth).astype(jnp.float32)
    return jnp.exp(-jnp.square((heights - depth / 3.0) / (depth / 6.0)))


def relax_cells(tables, moments, rates, force):
    shift_x, shift_y, shift_z, moment_map, back_map = tables[:5]
    density = moments[0]
    velocity_x = moments[9] / density
    velocity_y = moments[3] / density
    velocity_z = moments[1] / density
    projected = shift_x[:, None] * velocity_x[None, :] + shift_y[:, None] * velocity_y[None, :] + shift_z[:, None] * velocity_z[None, :]
    speed_sq = velocity_x * velocity_x + velocity_y * velocity_y + velocity_z * velocity_z
    balance = density[None, :] * (1.0 + 3.0 * projected + 4.5 * projected * projected - 1.5 * speed_sq[None, :])
    balance_moments = jnp.dot(moment_map, balance, precision=FULL_PRECISION)
    relaxed = moments - rates[:, None] * (moments - balance_moments)
    return jnp.dot(back_map, relaxed, precision=FULL_PRECISION) + 3.0 * shift_x[:, None] * force[None, :]


def reference(populations, precursor, pairing, rates, loading, disc_cols, disc_turb):
    tables = lattice_tables()
    flat = populations.reshape(27, NX * NY * NZ)
    moments = jnp.dot(tables[3], flat, precision=FULL_PRECISION)
    velocity_x = moments[9] / moments[0]
    profile = disc_profile(NZ)
    columns = velocity_x.reshape(NX * NY, NZ)[disc_cols]
    row_values = jnp.dot(columns, profile, precision=FULL_PRECISION)
    owner_table = (disc_turb[None, :] == jnp.arange(NT, dtype=jnp.int32)[:, None]).astype(jnp.float32)
    totals = jnp.dot(owner_table, row_values, precision=FULL_PRECISION)
    counts = jnp.sum(owner_table, axis=1)
    disc_speed = totals / (counts * jnp.sum(profile))
    thrust = 0.5 * loading * disc_speed * jnp.abs(disc_speed)
    row_thrust = jnp.dot(thrust, owner_table, precision=FULL_PRECISION)
    column_force = jnp.zeros((NX * NY,), jnp.float32).at[disc_cols].add(row_thrust)
    force = -(column_force[:, None] * profile[None, :]).reshape(NX * NY * NZ)
    post = relax_cells(tables, moments, rates, force).reshape(27, NX, NY, NZ)
    reduced = jnp.dot(tables[5], precursor.reshape(27, FRX * NY * NZ), precision=FULL_PRECISION)
    rebuilt = jnp.dot(tables[6], reduced, precision=FULL_PRECISION).reshape(27, FRX, NY, NZ)
    planes = jnp.arange(FR, dtype=jnp.int32)
    targets = (jnp.arange(N_GX, dtype=jnp.int32)[:, None] * CX + planes[None, :]).reshape(-1)
    sources = (pairing[:, None] * FR + planes[None, :]).reshape(-1)
    blend = jnp.tile(0.5 / (planes.astype(jnp.float32) + 1.0), N_GX)[None, :, None, None]
    mixed = (1.0 - blend) * post[:, targets] + blend * rebuilt[:, sources]
    post = post.at[:, targets].set(mixed)
    pieces = []
    for slot in range(27):
        step_x = slot // 9 - 1
        step_y = (slot // 3) % 3 - 1
        step_z = slot % 3 - 1
        moved = jnp.roll(post[slot], (step_x, step_y), axis=(0, 1))
        if step_z == 1:
            moved = jnp.concatenate([post[26 - slot][:, :, :1], moved[:, :, :-1]], axis=2)
        elif step_z == -1:
            moved = jnp.concatenate([moved[:, :, 1:], post[26 - slot][:, :, -1:]], axis=2)
        pieces.append(moved)
    return jnp.stack(pieces), disc_speed
```

```python
import jax
import jax.numpy as jnp
import numpy as np
from jax import lax
from jax.experimental import pallas as pl
from jax.experimental.pallas import tpu as pltpu
from jax.sharding import PartitionSpec as P

GX, GY = 32, 4
NDEV = GX * GY
XW, YW, Z = 8, 32, 128
NY_ALL, NX_ALL = 128, 256
SLOTS = 512
TURBINES = 32
F32 = jnp.float32

OWN, NEXT, LO_OWN, HI_OWN, LO_NEXT, HI_NEXT, DISC, CORNER = 0, 80, 104, 107, 110, 111, 112, 113
CORNERS = ((-1, -1), (-1, 1), (1, -1), (1, 1))
W_ROWS = 360
BLEND = (0.5, 0.25)

HEIGHTS = np.arange(Z).astype(np.float32)
PROFILE_SUM = float(np.sum(np.exp(-np.square((np.arange(Z) - Z / 3.0) / (Z / 6.0)))))


def slot(cx, cy, cz):
    return 9 * (cx + 1) + 3 * (cy + 1) + (cz + 1)


def profile_row():
    heights = lax.broadcasted_iota(jnp.int32, (8, Z), 1).astype(F32)
    return jnp.exp(-jnp.square((heights - Z / 3.0) * (6.0 / Z)))


def forward(g):
    for stride in (1, 3, 9):
        out = list(g)
        for i in range(27):
            if (i // stride) % 3 == 0:
                a, b, c = g[i], g[i + stride], g[i + 2 * stride]
                s = c + a
                out[i] = s + 4.0 * b
                out[i + stride] = c - a
                out[i + 2 * stride] = s
        g = out
    return g


def backward(m):
    for stride in (9, 3, 1):
        out = list(m)
        for i in range(27):
            if (i // stride) % 3 == 0:
                a, b, c = m[i], m[i + stride], m[i + 2 * stride]
                out[i] = c - b
                out[i + stride] = 0.5 * (a - c)
                out[i + 2 * stride] = c + b
        m = out
    return m


def collide(g, rates):
    m = forward(g)
    density = m[0] * (1.0 / 216.0)
    inv = 1.0 / m[0]
    u = (m[9] * inv, m[3] * inv, m[1] * inv)
    j = (m[9] * (1.0 / 216.0), m[3] * (1.0 / 216.0), m[1] * (1.0 / 216.0))
    ju = {}
    for a in range(3):
        for b in range(a, 3):
            ju[(a, b)] = j[a] * u[b]
    out = []
    for i in range(27):
        order = (i // 9, i // 3 % 3, i % 3)
        ones = [d for d in range(3) if order[d] == 1]
        twos = [d for d in range(3) if order[d] == 2]
        if i in (0, 1, 3, 9):
            out.append(m[i] * 0.125)
            continue
        r = rates(i)
        keep = m[i] * ((1.0 - r) * 0.125)
        if len(ones) == 3:
            out.append(keep)
            continue
        scale = r * (27.0 / 3.0 ** len(twos))
        if len(ones) == 0:
            eq = ju[(twos[0], twos[0])]
            for d in twos[1:]:
                eq = eq + ju[(d, d)]
            eq = density + 3.0 * eq
        elif len(ones) == 1:
            eq = j[ones[0]]
        else:
            eq = ju[(ones[0], ones[1])]
        out.append(keep + eq * scale)
    return backward(out)


def z_stream(p, lane):
    out = []
    for i in range(27):
        cz = i % 3 - 1
        if cz == 0:
            out.append(p[i])
        elif cz == 1:
            out.append(jnp.where(lane == 0, p[26 - i], pltpu.roll(p[i], 1, 1)))
        else:
            out.append(jnp.where(lane == Z - 1, p[26 - i], pltpu.roll(p[i], Z - 1, 1)))
    return out


def precursor_coefficients(g):
    m = forward(g)
    rho, jx, jy, jz = m[0], m[9], m[3], m[1]
    xx, yy, zz, xy, xz, yz = m[18], m[6], m[2], m[12], m[10], m[4]
    third = rho * (1.0 / 3.0)
    pxx, pyy, pzz = xx - third, yy - third, zz - third
    s = 1.0 / 216.0
    k0 = (rho - 1.5 * (pxx + pyy + pzz)) * s
    return [k0, jx * (3 * s), jy * (3 * s), jz * (3 * s), pxx * (4.5 * s), pyy * (4.5 * s), pzz * (4.5 * s),
            xy * (9 * s), xz * (9 * s), yz * (9 * s)]


def next_coefficients(c):
    return [c[0] - c[1] + c[4], c[2] - c[7], c[3] - c[8], c[5], c[6], c[9]]


def rebuild_next(c):
    out = []
    for cy in (-1, 0, 1):
        base = c[0] + (cy * c[1] + c[3] if cy else 0.0)
        lin = c[2] + cy * c[5] if cy else c[2]
        for cz in (-1, 0, 1):
            out.append(base + cz * lin + c[4] if cz else base)
    return out


def rebuild(c):
    out = []
    for cx in (-1, 0, 1):
        base = c[0] + cx * c[1] + c[4] if cx else c[0]
        liny = c[2] + cx * c[7] if cx else c[2]
        linz = c[3] + cx * c[8] if cx else c[3]
        out += rebuild_next([base, liny, linz, c[5], c[6], c[9]])
    return out


K1_PLANES = 2


def first_kernel(rates_ref, pop_ref, pre_ref, cols_ref, turb_ref, send_ref, w_ref, corner_scr, acc_scr):
    step = pl.program_id(0)
    gx = lax.axis_index("gx")
    gy = lax.axis_index("gy")

    @pl.when(step == 0)
    def _():
        rows = lax.broadcasted_iota(jnp.int32, (W_ROWS, SLOTS), 0)
        lo = rows - 320
        main = rows < 320
        xx = jnp.where(main, rows >> 5, jnp.where(lo < 16, lo, lo - 16))
        yy = jnp.where(main, rows & 31, jnp.where(lo < 16, -1, YW))
        col = ((gx * XW + xx - 1) & (NX_ALL - 1)) * NY_ALL + ((gy * YW + yy) & (NY_ALL - 1))
        valid = main | ((lo & 15) < 10)
        hit = ((col == cols_ref[...]) & valid & (lo < 32)) | (lo >= 32)
        owner = lax.broadcasted_iota(jnp.int32, (128, SLOTS), 0) == turb_ref[...]
        w_ref[...] = lax.dot_general(
            jnp.where(hit, 1.0, 0.0).astype(jnp.bfloat16),
            jnp.where(owner, 1.0, 0.0).astype(jnp.bfloat16),
            (((1,), (1,)), ((), ())), preferred_element_type=F32)
        acc_scr[...] = jnp.zeros_like(acc_scr)
        send_ref[LO_OWN:, :, :] = jnp.zeros((NDEV - LO_OWN, 8, Z), F32)
        for p in range(2):
            for q in range(4):
                g = [pre_ref[i, p, 8 * q:8 * q + 8, :] for i in range(27)]
                c = precursor_coefficients(g)
                for k in range(10):
                    send_ref[OWN + (2 * k + p) * 4 + q, :, :] = c[k]
                    row = 2 * k + p
                    if q == 3:
                        send_ref[LO_OWN + row // 8, row % 8:row % 8 + 1, :] = c[k][7:8, :]
                    if q == 0:
                        send_ref[HI_OWN + row // 8, row % 8:row % 8 + 1, :] = c[k][0:1, :]
                if p == 0:
                    n = next_coefficients(c)
                    for k in range(6):
                        send_ref[NEXT + 4 * k + q, :, :] = n[k]
                        if q == 3:
                            send_ref[LO_NEXT, k:k + 1, :] = n[k][7:8, :]
                        if q == 0:
                            send_ref[HI_NEXT, k:k + 1, :] = n[k][0:1, :]
        corner_scr[...] = jnp.ones_like(corner_scr)
        for i in range(27):
            corner_scr[i, 0:1, :] = pop_ref[i, 0, 0:1, :]
            corner_scr[i, 1:2, :] = pop_ref[i, 0, YW - 1:YW, :]

    profile = profile_row()
    for a in range(K1_PLANES):
        for q in range(4):
            rows = slice(8 * q, 8 * q + 8)
            part = []
            for cx in range(3):
                total = None
                for cy in range(3):
                    b = 9 * cx + 3 * cy
                    t = pop_ref[b, a, rows, :] + pop_ref[b + 2, a, rows, :] + 4.0 * pop_ref[b + 1, a, rows, :]
                    t = 4.0 * t if cy == 1 else t
                    total = t if total is None else total + t
                part.append(total)
            ends = part[0] + part[2]
            ux = (part[2] - part[0]) / (ends + 4.0 * part[1])
            sums = jnp.sum(ux * profile, axis=1, keepdims=True)
            base = pl.multiple_of((step * K1_PLANES + a + 1) * YW, YW) + 8 * q
            acc_scr[...] += sums * w_ref[pl.ds(base, 8), :]

    @pl.when(step == XW // K1_PLANES - 1)
    def _():
        a = K1_PLANES - 1
        for i in range(27):
            corner_scr[i, 2:3, :] = pop_ref[i, a, 0:1, :]
            corner_scr[i, 3:4, :] = pop_ref[i, a, YW - 1:YW, :]
        lane = lax.broadcasted_iota(jnp.int32, (8, Z), 1)
        post = z_stream(collide([corner_scr[i] for i in range(27)], lambda i: rates_ref[i]), lane)
        for n, (cx, cy) in enumerate(CORNERS):
            row = 2 * (cx > 0) + (cy > 0)
            for cz in (-1, 0, 1):
                send_ref[CORNER + n, cz + 1:cz + 2, :] = post[slot(cx, cy, cz)][row:row + 1, :]
        send_ref[DISC, 0:1, :] = jnp.sum(acc_scr[...], axis=0, keepdims=True)


def before_exchange(rates, populations, precursor, cols, turb):
    return pl.pallas_call(
        first_kernel,
        grid=(XW // K1_PLANES,),
        in_specs=[
            pl.BlockSpec(memory_space=pltpu.SMEM),
            pl.BlockSpec((27, K1_PLANES, YW, Z), lambda x: (0, x, 0, 0)),
            pl.BlockSpec((27, 2, YW, Z), lambda x: (0, 0, 0, 0)),
            pl.BlockSpec((1, SLOTS), lambda x: (0, 0)),
            pl.BlockSpec((1, SLOTS), lambda x: (0, 0)),
        ],
        out_specs=[
            pl.BlockSpec((NDEV, 8, Z), lambda x: (0, 0, 0)),
            pl.BlockSpec((W_ROWS, 128), lambda x: (0, 0)),
        ],
        out_shape=[jax.ShapeDtypeStruct((NDEV, 8, Z), F32), jax.ShapeDtypeStruct((W_ROWS, 128), F32)],
        scratch_shapes=[pltpu.VMEM((27, 8, Z), F32), pltpu.VMEM((8, 128), F32)],
        name="before_exchange",
    )(rates, populations, precursor, cols, turb)


def collide_kernel(rates_ref, pop_ref, out_ref, xm_ref, xp_ref, ym_ref, yp_ref):
    x = pl.program_id(0)
    lane = lax.broadcasted_iota(jnp.int32, (8, Z), 1)
    for q in range(4):
        rows = slice(8 * q, 8 * q + 8)
        post = collide([pop_ref[i, 0, rows, :] for i in range(27)], lambda i: rates_ref[i])
        post = z_stream(post, lane)
        for i in range(27):
            out_ref[i, 0, rows, :] = post[i]
        for cx in (-1, 0, 1):
            for cz in (-1, 0, 1):
                k = 3 * (cx + 1) + cz + 1
                if q == 0:
                    ym_ref[k, pl.ds(x, 1), :] = post[slot(cx, -1, cz)][0:1, :]
                if q == 3:
                    yp_ref[k, pl.ds(x, 1), :] = post[slot(cx, 1, cz)][7:8, :]

    @pl.when(x == 0)
    def _():
        for k in range(9):
            xm_ref[k, :, :] = out_ref[k, 0, :, :]

    @pl.when(x == XW - 1)
    def _():
        for k in range(9):
            xp_ref[k, :, :] = out_ref[18 + k, 0, :, :]


def collision(rates, populations):
    whole = lambda x: (0, 0, 0)
    return pl.pallas_call(
        collide_kernel,
        grid=(XW,),
        in_specs=[
            pl.BlockSpec(memory_space=pltpu.SMEM),
            pl.BlockSpec((27, 1, YW, Z), lambda x: (0, x, 0, 0)),
        ],
        out_specs=[
            pl.BlockSpec((27, 1, YW, Z), lambda x: (0, x, 0, 0)),
            pl.BlockSpec((9, YW, Z), whole),
            pl.BlockSpec((9, YW, Z), whole),
            pl.BlockSpec((9, XW, Z), whole),
            pl.BlockSpec((9, XW, Z), whole),
        ],
        out_shape=[
            jax.ShapeDtypeStruct((27, XW, YW, Z), F32),
            jax.ShapeDtypeStruct((9, YW, Z), F32),
            jax.ShapeDtypeStruct((9, YW, Z), F32),
            jax.ShapeDtypeStruct((9, XW, Z), F32),
            jax.ShapeDtypeStruct((9, XW, Z), F32),
        ],
        name="collision",
    )(rates, populations)


def route_kernel(pairing_ref, got_ref, send_ref):
    me = lax.axis_index("gx") * GY + lax.axis_index("gy")
    is_next = ((me >= NEXT) & (me < LO_OWN)) | (me == LO_NEXT) | (me == HI_NEXT)
    corner = me - CORNER
    is_corner = (corner >= 0) & (corner < 4)
    low = ((me >= LO_OWN) & (me < HI_OWN)) | (me == LO_NEXT)
    high = ((me >= HI_OWN) & (me < LO_NEXT)) | (me == HI_NEXT)
    from_x = jnp.where(corner < 2, 1, -1)
    from_y = jnp.where(is_corner, jnp.where((corner & 1) == 0, 1, -1), jnp.where(low, -1, jnp.where(high, 1, 0)))
    ahead = jnp.where(is_next, 1, 0)
    lanes = [(t + from_y) & (GY - 1) for t in range(GY)]

    @pl.when(me != DISC)
    def _():
        for d in range(GX):
            tile = pairing_ref[(d + ahead) & (GX - 1)]
            tile = jnp.where(is_corner, (d + from_x) & (GX - 1), tile) * GY
            for t in range(GY):
                send_ref[d * GY + t, :, :] = got_ref[tile + lanes[t], :, :]

    @pl.when(me == DISC)
    def _():
        total = got_ref[0, :, :]
        for n in range(1, NDEV):
            total = total + got_ref[n, :, :]
        for n in range(NDEV):
            send_ref[n, :, :] = total


def route(pairing, got):
    return pl.pallas_call(
        route_kernel,
        in_specs=[pl.BlockSpec(memory_space=pltpu.SMEM), pl.BlockSpec(memory_space=pltpu.VMEM)],
        out_specs=pl.BlockSpec(memory_space=pltpu.VMEM),
        out_shape=jax.ShapeDtypeStruct((NDEV, 8, Z), F32),
        name="route",
    )(pairing, got)


def last_kernel(got_ref, w_ref, loading_ref, r_ref, xm_ref, xp_ref, ym_ref, yp_ref, out_ref, speed_ref,
                rp, force, load_scr, lo_scr, hi_scr, yp_scr, ym_scr):
    x = pl.program_id(0)
    lane = lax.broadcasted_iota(jnp.int32, (8, Z), 1)
    profile = profile_row()
    up = jnp.where(lane == 0, -profile, pltpu.roll(profile, 1, 1))
    down = jnp.where(lane == Z - 1, -profile, pltpu.roll(profile, Z - 1, 1))
    along = (3.0 * down, 3.0 * profile, 3.0 * up)

    def pushed(value, i, f):
        cx = i // 9 - 1
        if cx == 0:
            return value
        term = f * along[i % 3]
        return value + term if cx > 0 else value - term

    def pushes(f):
        return [f * a for a in along]

    def push(value, i, fs):
        cx = i // 9 - 1
        return value if cx == 0 else (value + fs[i % 3] if cx > 0 else value - fs[i % 3])

    @pl.when(x == 0)
    def _():
        load_scr[...] = jnp.zeros_like(load_scr)
        load_scr[0:1, 0:TURBINES] = loading_ref[...]
        counts = w_ref[352:360, :]
        totals = jnp.broadcast_to(got_ref[DISC, 0:1, :], (8, 128))
        k = lax.broadcasted_iota(jnp.int32, (8, 128), 1)
        speed = jnp.where(k < TURBINES, totals / (jnp.where(k < TURBINES, counts, 1.0) * PROFILE_SUM), 0.0)
        speed_ref[...] = speed[0:1, 0:TURBINES]
        thrust = (0.5 * jnp.broadcast_to(load_scr[0:1, :], (8, 128))) * speed * jnp.abs(speed)
        force[...] = -lax.dot_general(
            w_ref[0:352, :] * thrust[0:1, :], jnp.ones((128, Z), F32), (((1,), (0,)), ((), ())),
            precision=lax.Precision.HIGHEST, preferred_element_type=F32)
        for scr, tile, nxt, halo, frow, cy, out in (
            (lo_scr, LO_OWN, LO_NEXT, yp_ref, 320, 1, yp_scr),
            (hi_scr, HI_OWN, HI_NEXT, ym_ref, 336, -1, ym_scr),
        ):
            scr[...] = jnp.zeros_like(scr)
            for c in range(10):
                r = 2 * c
                scr[c, 0:2, :] = got_ref[tile + r // 8, r % 8:r % 8 + 2, :]
            built = rebuild([scr[c] for c in range(10)])
            ahead = rebuild_next([got_ref[nxt, c:c + 1, :] for c in range(6)])
            row = lax.broadcasted_iota(jnp.int32, (8, Z), 0)
            blend = jnp.where(row == 0, BLEND[0], jnp.where(row == 1, BLEND[1], 0.0))
            f = force[frow + 1:frow + 9, :]
            fs = pushes(f)
            for cx in (-1, 0, 1):
                for cz in (-1, 0, 1):
                    k = 3 * (cx + 1) + cz + 1
                    i = slot(cx, cy, cz)
                    b = built[i]
                    b = b if cz == 0 else pltpu.roll(b, cz % Z, 1)
                    out[k, 1:9, :] = (1.0 - blend) * push(halo[k], i, fs) + blend * b
            for cz in (-1, 0, 1):
                i = slot(1, cy, cz)
                n = CORNERS.index((1, cy))
                out[6 + cz + 1, 0:1, :] = got_ref[CORNER + n, cz + 1:cz + 2, :] + (
                    force[frow:frow + 1, :] * along[cz + 1][0:1, :])
                n = CORNERS.index((-1, cy))
                value = got_ref[CORNER + n, cz + 1:cz + 2, :] - force[frow + 9:frow + 10, :] * along[cz + 1][0:1, :]
                b = ahead[3 * (cy + 1) + cz + 1]
                b = b if cz == 0 else pltpu.roll(jnp.broadcast_to(b, (8, Z)), cz % Z, 1)[0:1, :]
                out[cz + 1, 9:10, :] = (1.0 - BLEND[0]) * value + BLEND[0] * b
        for q in range(4):
            rows = slice(8 * q, 8 * q + 8)
            into = slice(8 * q + 8, 8 * q + 16)
            fs = pushes(force[rows, :])
            for k in range(9):
                rp[18 + k, 0, into, :] = push(xp_ref[k, rows, :], 18 + k, fs)
            for p in range(2):
                c = [got_ref[OWN + (2 * k + p) * 4 + q, :, :] for k in range(10)]
                built = z_stream(rebuild(c), lane)
                fs = pushes(force[YW * (p + 1) + 8 * q:YW * (p + 1) + 8 * q + 8, :])
                for i in range(27):
                    rp[i, p + 1, into, :] = (1.0 - BLEND[p]) * push(r_ref[i, p, rows, :], i, fs) + BLEND[p] * built[i]

    @pl.when((x >= 1) & (x < XW - 1))
    def _():
        for q in range(4):
            rows = slice(8 * q, 8 * q + 8)
            into = slice(8 * q + 8, 8 * q + 16)
            fs = pushes(force[pl.ds(pl.multiple_of((x + 2) * YW, YW) + 8 * q, 8), :])
            for i in range(27):
                rp[i, x + 2, into, :] = push(r_ref[i, x + 1, rows, :], i, fs)

    @pl.when(x == XW - 1)
    def _():
        for q in range(4):
            rows = slice(8 * q, 8 * q + 8)
            into = slice(8 * q + 8, 8 * q + 16)
            fs = pushes(force[YW * (XW + 1) + 8 * q:YW * (XW + 1) + 8 * q + 8, :])
            built = rebuild_next([got_ref[NEXT + 4 * k + q, :, :] for k in range(6)])
            for k in range(9):
                cz = k % 3 - 1
                b = built[k] if cz == 0 else pltpu.roll(built[k], cz % Z, 1)
                rp[k, XW + 1, into, :] = (1.0 - BLEND[0]) * push(xm_ref[k, rows, :], k, fs) + BLEND[0] * b

    lane = lax.broadcasted_iota(jnp.int32, (YW, Z), 1)
    row = lax.broadcasted_iota(jnp.int32, (YW, Z), 0)
    for i in range(27):
        cx, cy, cz = i // 9 - 1, i // 3 % 3 - 1, i % 3 - 1
        at = x + 1 - cx
        k = 3 * (cx + 1) + cz + 1
        value = rp[i, at, 8 - cy:40 - cy, :]
        if cy == 1:
            value = jnp.where(row == 0, yp_scr[k, pl.ds(at, 1), :], value)
        elif cy == -1:
            value = jnp.where(row == YW - 1, ym_scr[k, pl.ds(at, 1), :], value)
        if cz != 0 and (cx != 0 or cy != 0):
            value = jnp.where(lane == (0 if cz == 1 else Z - 1), rp[i, x + 1, 8:40, :], value)
        out_ref[i, 0, :, :] = value


def after_exchange(got, w, loading, r, xm, xp, ym, yp):
    full = lambda a: pl.BlockSpec(a.shape, lambda x: (0,) * a.ndim)
    return pl.pallas_call(
        last_kernel,
        grid=(XW,),
        in_specs=[full(a) for a in (got, w, loading, r, xm, xp, ym, yp)],
        out_specs=[
            pl.BlockSpec((27, 1, YW, Z), lambda x: (0, x, 0, 0)),
            pl.BlockSpec((1, TURBINES), lambda x: (0, 0)),
        ],
        out_shape=[jax.ShapeDtypeStruct((27, XW, YW, Z), F32), jax.ShapeDtypeStruct((1, TURBINES), F32)],
        scratch_shapes=[
            pltpu.VMEM((27, XW + 2, 48, Z), F32),
            pltpu.VMEM((352, Z), F32),
            pltpu.VMEM((8, 128), F32),
            pltpu.VMEM((10, 8, Z), F32),
            pltpu.VMEM((10, 8, Z), F32),
            pltpu.VMEM((9, 16, Z), F32),
            pltpu.VMEM((9, 16, Z), F32),
        ],
        name="after_exchange",
    )(got, w, loading, r, xm, xp, ym, yp)


def body(populations, precursor, pairing, rates, loading, disc_cols, disc_turb):
    both = ("gx", "gy")
    ring = lambda n, s: [(i, (i + s) % n) for i in range(n)]
    send, w = before_exchange(rates, populations, precursor, disc_cols.reshape(1, SLOTS), disc_turb.reshape(1, SLOTS))
    got = lax.all_to_all(send, both, 0, 0, tiled=True)
    r, xm, xp, ym, yp = collision(rates, populations)
    xm = lax.ppermute(xm, "gx", ring(GX, -1))
    xp = lax.ppermute(xp, "gx", ring(GX, 1))
    ym = lax.ppermute(ym, "gy", ring(GY, -1))
    yp = lax.ppermute(yp, "gy", ring(GY, 1))
    got = lax.all_to_all(route(pairing, got), both, 0, 0, tiled=True)
    read, speed = after_exchange(got, w, loading.reshape(1, TURBINES), r, xm, xp, ym, yp)
    return read, speed.reshape(TURBINES)


def solution(mesh):
    in_specs = (P(None, "gx", "gy", None), P(None, "gx", "gy", None), P(), P(), P(), P(), P())
    out_specs = (P(None, "gx", "gy", None), P())
    return jax.shard_map(body, mesh=mesh, in_specs=in_specs, out_specs=out_specs, check_vma=False)
```

```python
import jax
import jax.numpy as jnp
import numpy as np
from jax import lax
from jax.experimental import pallas as pl
from jax.experimental.pallas import tpu as pltpu
from jax.sharding import PartitionSpec as P

GX, GY = 32, 4
NDEV = GX * GY
XW, YW, Z = 8, 32, 128
NY_ALL, NX_ALL = 128, 256
SLOTS = 512
TURBINES = 32
F32 = jnp.float32

OWN, NEXT, LO_OWN, HI_OWN, LO_NEXT, HI_NEXT, CORNER = 0, 80, 104, 107, 110, 111, 112
PIECE = 9
CORNERS = ((-1, -1), (-1, 1), (1, -1), (1, 1))
W_ROWS = 360
BLEND = (0.5, 0.25)

PROFILE_SUM = float(np.sum(np.exp(-np.square((np.arange(Z) - Z / 3.0) / (Z / 6.0)))))


HBM = pl.BlockSpec(memory_space=pltpu.HBM)
SMEM = pl.BlockSpec(memory_space=pltpu.SMEM)
VMEM = pl.BlockSpec(memory_space=pltpu.VMEM)


def near(array):
    return pltpu.with_memory_space_constraint(array, pltpu.VMEM)


def far(array):
    return pltpu.with_memory_space_constraint(array, pltpu.HBM)


def slot(cx, cy, cz):
    return 9 * (cx + 1) + 3 * (cy + 1) + (cz + 1)


def profile_row():
    heights = lax.broadcasted_iota(jnp.int32, (8, Z), 1).astype(F32)
    return jnp.exp(-jnp.square((heights - Z / 3.0) * (6.0 / Z)))


def forward(g):
    for stride in (1, 3, 9):
        out = list(g)
        for i in range(27):
            if (i // stride) % 3 == 0:
                a, b, c = g[i], g[i + stride], g[i + 2 * stride]
                s = c + a
                out[i] = s + 4.0 * b
                out[i + stride] = c - a
                out[i + 2 * stride] = s
        g = out
    return g


def backward(m):
    for stride in (9, 3, 1):
        out = list(m)
        for i in range(27):
            if (i // stride) % 3 == 0:
                a, b, c = m[i], m[i + stride], m[i + 2 * stride]
                out[i] = c - b
                out[i + stride] = 0.5 * (a - c)
                out[i + 2 * stride] = c + b
        m = out
    return m


def collide(g, rates):
    return relax(forward(g), rates)


def relax(m, rates):
    density = m[0] * (1.0 / 216.0)
    inv = 1.0 / m[0]
    u = (m[9] * inv, m[3] * inv, m[1] * inv)
    j = (m[9] * (1.0 / 216.0), m[3] * (1.0 / 216.0), m[1] * (1.0 / 216.0))
    ju = {}
    for a in range(3):
        for b in range(a, 3):
            ju[(a, b)] = j[a] * u[b]
    out = []
    for i in range(27):
        order = (i // 9, i // 3 % 3, i % 3)
        ones = [d for d in range(3) if order[d] == 1]
        twos = [d for d in range(3) if order[d] == 2]
        if i in (0, 1, 3, 9):
            out.append(m[i] * 0.125)
            continue
        r = rates(i)
        keep = m[i] * ((1.0 - r) * 0.125)
        if len(ones) == 3:
            out.append(keep)
            continue
        scale = r * (27.0 / 3.0 ** len(twos))
        if len(ones) == 0:
            eq = ju[(twos[0], twos[0])]
            for d in twos[1:]:
                eq = eq + ju[(d, d)]
            eq = density + 3.0 * eq
        elif len(ones) == 1:
            eq = j[ones[0]]
        else:
            eq = ju[(ones[0], ones[1])]
        out.append(keep + eq * scale)
    return backward(out)


def z_stream(p, lane):
    out = []
    for i in range(27):
        cz = i % 3 - 1
        if cz == 0:
            out.append(p[i])
        elif cz == 1:
            out.append(jnp.where(lane == 0, p[26 - i], pltpu.roll(p[i], 1, 1)))
        else:
            out.append(jnp.where(lane == Z - 1, p[26 - i], pltpu.roll(p[i], Z - 1, 1)))
    return out


def precursor_coefficients(g):
    m = forward(g)
    rho, jx, jy, jz = m[0], m[9], m[3], m[1]
    xx, yy, zz, xy, xz, yz = m[18], m[6], m[2], m[12], m[10], m[4]
    third = rho * (1.0 / 3.0)
    pxx, pyy, pzz = xx - third, yy - third, zz - third
    s = 1.0 / 216.0
    k0 = (rho - 1.5 * (pxx + pyy + pzz)) * s
    return [k0, jx * (3 * s), jy * (3 * s), jz * (3 * s), pxx * (4.5 * s), pyy * (4.5 * s), pzz * (4.5 * s),
            xy * (9 * s), xz * (9 * s), yz * (9 * s)]


def next_coefficients(c):
    return [c[0] - c[1] + c[4], c[2] - c[7], c[3] - c[8], c[5], c[6], c[9]]


def rebuild_next(c):
    out = []
    for cy in (-1, 0, 1):
        base = c[0] + (cy * c[1] + c[3] if cy else 0.0)
        lin = c[2] + cy * c[5] if cy else c[2]
        for cz in (-1, 0, 1):
            out.append(base + cz * lin + c[4] if cz else base)
    return out


def rebuild(c):
    out = []
    for cx in (-1, 0, 1):
        base = c[0] + cx * c[1] + c[4] if cx else c[0]
        liny = c[2] + cx * c[7] if cx else c[2]
        linz = c[3] + cx * c[8] if cx else c[3]
        out += rebuild_next([base, liny, linz, c[5], c[6], c[9]])
    return out


def first_kernel(rates_hbm, pop_hbm, pre_hbm, send_ref, pre_ref, corner_scr, rates_ref, sems):
    planes = [pltpu.make_async_copy(pre_hbm.at[:, p], pre_ref.at[:, p], sems.at[p]) for p in range(2)]
    columns = []
    for n, (x, y) in enumerate(((0, 0), (0, YW - 8), (XW - 1, 0), (XW - 1, YW - 8))):
        columns.append(pltpu.make_async_copy(pop_hbm.at[:, x, y:y + 8, :], corner_scr.at[n], sems.at[2 + n]))
    columns.append(pltpu.make_async_copy(rates_hbm, rates_ref, sems.at[6]))
    for copy in planes + columns:
        copy.start()
    send_ref[LO_OWN:, :, :] = jnp.zeros((NDEV - LO_OWN, 8, Z), F32)
    for p in range(2):
        planes[p].wait()
        for q in range(4):
            c = precursor_coefficients([pre_ref[i, p, 8 * q:8 * q + 8, :] for i in range(27)])
            for k in range(10):
                send_ref[OWN + (2 * k + p) * 4 + q, :, :] = c[k]
                row = 2 * k + p
                if q == 3:
                    send_ref[LO_OWN + row // 8, row % 8:row % 8 + 1, :] = c[k][7:8, :]
                if q == 0:
                    send_ref[HI_OWN + row // 8, row % 8:row % 8 + 1, :] = c[k][0:1, :]
            if p == 0:
                c = next_coefficients(c)
                for k in range(6):
                    send_ref[NEXT + 4 * k + q, :, :] = c[k]
                    if q == 3:
                        send_ref[LO_NEXT, k:k + 1, :] = c[k][7:8, :]
                    if q == 0:
                        send_ref[HI_NEXT, k:k + 1, :] = c[k][0:1, :]
    for copy in columns:
        copy.wait()
    row = lax.broadcasted_iota(jnp.int32, (8, Z), 0)
    g = []
    for i in range(27):
        rows = [corner_scr[n, i, y:y + 1, :] for n, y in enumerate((0, 7, 0, 7))]
        g.append(jnp.where(row == 0, rows[0], jnp.where(row == 1, rows[1], jnp.where(row == 2, rows[2], rows[3]))))
    lane = lax.broadcasted_iota(jnp.int32, (8, Z), 1)
    post = z_stream(collide(g, lambda i: rates_ref[i]), lane)
    for n, (cx, cy) in enumerate(CORNERS):
        at = 2 * (cx > 0) + (cy > 0)
        for cz in (-1, 0, 1):
            send_ref[CORNER + n, cz + 1:cz + 2, :] = post[slot(cx, cy, cz)][at:at + 1, :]


def before_exchange(rates, populations, precursor):
    return pl.pallas_call(
        first_kernel,
        in_specs=[HBM, HBM, HBM],
        out_specs=VMEM,
        out_shape=pltpu.VMEM((NDEV, 8, Z), F32),
        scratch_shapes=[
            pltpu.VMEM((27, 2, YW, Z), F32),
            pltpu.VMEM((4, 27, 8, Z), F32),
            pltpu.SMEM((27,), F32),
            pltpu.SemaphoreType.DMA((7,)),
        ],
        name="before_exchange",
        compiler_params=pltpu.CompilerParams(vmem_limit_bytes=4 << 20),
    )(far(rates), far(populations), far(precursor))


def collide_kernel(rates_ref, cols_ref, turb_ref, pop_hbm, out_hbm, xa_ref, xb_ref, ya_ref, yb_ref, w_ref, disc_ref,
                   pop_ref, out_ref, ym_ref, yp_ref, in_sems, out_sems):
    def copy_in(x):
        return pltpu.make_async_copy(pop_hbm.at[:, x], pop_ref.at[:, x], in_sems.at[x])

    def copy_out(x):
        return pltpu.make_async_copy(out_ref.at[:, x], out_hbm.at[:, x], out_sems.at[x])

    for x in range(XW):
        copy_in(x).start()
    gx = lax.axis_index("gx")
    gy = lax.axis_index("gy")
    rows = lax.broadcasted_iota(jnp.int32, (W_ROWS, SLOTS), 0)
    lo = rows - 320
    main = rows < 320
    xx = jnp.where(main, rows >> 5, jnp.where(lo < 16, lo, lo - 16))
    yy = jnp.where(main, rows & 31, jnp.where(lo < 16, -1, YW))
    col = ((gx * XW + xx - 1) & (NX_ALL - 1)) * NY_ALL + ((gy * YW + yy) & (NY_ALL - 1))
    valid = main | ((lo & 15) < 10)
    hit = ((col == cols_ref[...]) & valid & (lo < 32)) | (lo >= 32)
    owner = lax.broadcasted_iota(jnp.int32, (128, SLOTS), 0) == turb_ref[...]
    w_ref[...] = lax.dot_general(
        jnp.where(hit, 1.0, 0.0).astype(jnp.bfloat16),
        jnp.where(owner, 1.0, 0.0).astype(jnp.bfloat16),
        (((1,), (1,)), ((), ())), preferred_element_type=F32)
    disc_ref[...] = jnp.zeros_like(disc_ref)
    lane = lax.broadcasted_iota(jnp.int32, (8, Z), 1)
    profile = profile_row()

    def plane(x, carry):
        copy_in(x).wait()
        for q in range(4):
            rows = slice(8 * q, 8 * q + 8)
            m = forward([pop_ref[i, x, rows, :] for i in range(27)])
            sums = jnp.sum(m[9] / m[0] * profile, axis=1, keepdims=True)
            disc_ref[...] += sums * w_ref[pl.ds(pl.multiple_of((x + 1) * YW + 8 * q, 8), 8), :]
            post = z_stream(relax(m, lambda i: rates_ref[i]), lane)
            for i in range(27):
                out_ref[i, x, rows, :] = post[i]
            for cx in (-1, 0, 1):
                for cz in (-1, 0, 1):
                    k = 3 * (cx + 1) + cz + 1
                    if q == 0:
                        ym_ref[k, pl.ds(x, 1), :] = post[slot(cx, -1, cz)][0:1, :]
                    if q == 3:
                        yp_ref[k, pl.ds(x, 1), :] = post[slot(cx, 1, cz)][7:8, :]
        copy_out(x).start()
        return carry

    lax.fori_loop(0, XW, plane, 0)
    odd_x = (gx & 1) == 1
    odd_y = (gy & 1) == 1
    for k in range(9):
        low, high = out_ref[k, 0, :, :], out_ref[18 + k, XW - 1, :, :]
        xa_ref[k, :, :] = jnp.where(odd_x, low, high)
        xb_ref[k, :, :] = jnp.where(odd_x, high, low)
        low, high = ym_ref[k, :, :], yp_ref[k, :, :]
        ya_ref[k, :, :] = jnp.where(odd_y, low, high)
        yb_ref[k, :, :] = jnp.where(odd_y, high, low)
    for x in range(XW):
        copy_out(x).wait()


def collision(rates, cols, turb, populations):
    shapes = ((27, XW, YW, Z), (9, YW, Z), (9, YW, Z), (9, XW, Z), (9, XW, Z), (W_ROWS, 128), (8, 128))
    return pl.pallas_call(
        collide_kernel,
        in_specs=[SMEM, VMEM, VMEM, HBM],
        out_specs=[HBM] + [VMEM] * (len(shapes) - 1),
        out_shape=[pltpu.HBM(shapes[0], F32)] + [pltpu.VMEM(shape, F32) for shape in shapes[1:]],
        scratch_shapes=[
            pltpu.VMEM(shapes[0], F32),
            pltpu.VMEM(shapes[0], F32),
            pltpu.VMEM((9, XW, Z), F32),
            pltpu.VMEM((9, XW, Z), F32),
            pltpu.SemaphoreType.DMA((XW,)),
            pltpu.SemaphoreType.DMA((XW,)),
        ],
        name="collision",
        compiler_params=pltpu.CompilerParams(vmem_limit_bytes=12 << 20),
    )(rates, cols, turb, far(populations))


def route_kernel(pairing_ref, got_ref, disc_ref, send_ref):
    me = lax.axis_index("gx") * GY + lax.axis_index("gy")
    is_next = ((me >= NEXT) & (me < LO_OWN)) | (me == LO_NEXT) | (me == HI_NEXT)
    corner = me - CORNER
    is_corner = (corner >= 0) & (corner < 4)
    low = ((me >= LO_OWN) & (me < HI_OWN)) | (me == LO_NEXT)
    high = ((me >= HI_OWN) & (me < LO_NEXT)) | (me == HI_NEXT)
    from_x = jnp.where(corner < 2, 1, -1)
    from_y = jnp.where(is_corner, jnp.where((corner & 1) == 0, 1, -1), jnp.where(low, -1, jnp.where(high, 1, 0)))
    ahead = jnp.where(is_next, 1, 0)
    lanes = [(t + from_y) & (GY - 1) for t in range(GY)]
    part = jnp.sum(disc_ref[...], axis=0, keepdims=True)
    for d in range(GX):
        tile = pairing_ref[(d + ahead) & (GX - 1)]
        tile = jnp.where(is_corner, (d + from_x) & (GX - 1), tile) * GY
        for t in range(GY):
            at = (d * GY + t) * PIECE
            send_ref[at:at + 8, :] = got_ref[tile + lanes[t], :, :]
            send_ref[at + 8:at + 9, :] = part


def route(pairing, got, disc):
    return pl.pallas_call(
        route_kernel,
        in_specs=[SMEM, VMEM, VMEM],
        out_specs=VMEM,
        out_shape=pltpu.VMEM((NDEV * PIECE, Z), F32),
        name="route",
        compiler_params=pltpu.CompilerParams(vmem_limit_bytes=3 << 20),
    )(pairing, near(got), near(disc))


def last_kernel(got_ref, w_ref, loading_ref, r_hbm, xa_ref, xb_ref, ya_ref, yb_ref, out_hbm, speed_ref,
                rp, force, load_scr, lo_scr, hi_scr, yp_scr, ym_scr, r_ref, out_scr, in_sems, sems):
    def copy_in(x):
        return pltpu.make_async_copy(r_hbm.at[:, x], r_ref.at[:, x], in_sems.at[x])

    for x in range(XW):
        copy_in(x).start()
    lane = lax.broadcasted_iota(jnp.int32, (8, Z), 1)
    profile = profile_row()
    up = jnp.where(lane == 0, -profile, pltpu.roll(profile, 1, 1))
    down = jnp.where(lane == Z - 1, -profile, pltpu.roll(profile, Z - 1, 1))
    along = (3.0 * down, 3.0 * profile, 3.0 * up)

    odd_x = (lax.axis_index("gx") & 1) == 1
    odd_y = (lax.axis_index("gy") & 1) == 1

    def got(tile, a=0, b=8):
        return got_ref[PIECE * tile + a:PIECE * tile + b, :]

    def pushes(f):
        return [f * a for a in along]

    def push(value, i, fs):
        cx = i // 9 - 1
        return value if cx == 0 else (value + fs[i % 3] if cx > 0 else value - fs[i % 3])

    load_scr[...] = jnp.zeros_like(load_scr)
    load_scr[0:1, 0:TURBINES] = loading_ref[...]
    counts = w_ref[352:360, :]
    totals = jnp.broadcast_to(jnp.sum(got_ref[pl.ds(8, NDEV, stride=PIECE), :], axis=0, keepdims=True), (8, 128))
    k = lax.broadcasted_iota(jnp.int32, (8, 128), 1)
    speed = jnp.where(k < TURBINES, totals / (jnp.where(k < TURBINES, counts, 1.0) * PROFILE_SUM), 0.0)
    speed_ref[...] = speed[0:1, 0:TURBINES]
    thrust = (0.5 * jnp.broadcast_to(load_scr[0:1, :], (8, 128))) * speed * jnp.abs(speed)
    force[...] = -lax.dot_general(
        w_ref[0:352, :] * thrust[0:1, :], jnp.ones((128, Z), F32), (((1,), (0,)), ((), ())),
        precision=lax.Precision.HIGHEST, preferred_element_type=F32)
    for scr, tile, nxt, halo, frow, cy, out in (
        (lo_scr, LO_OWN, LO_NEXT, (ya_ref, yb_ref), 320, 1, yp_scr),
        (hi_scr, HI_OWN, HI_NEXT, (yb_ref, ya_ref), 336, -1, ym_scr),
    ):
        scr[...] = jnp.zeros_like(scr)
        for c in range(10):
            r = 2 * c
            scr[c, 0:2, :] = got(tile + r // 8, r % 8, r % 8 + 2)
        built = rebuild([scr[c] for c in range(10)])
        ahead = rebuild_next([got(nxt, c, c + 1) for c in range(6)])
        row = lax.broadcasted_iota(jnp.int32, (8, Z), 0)
        blend = jnp.where(row == 0, BLEND[0], jnp.where(row == 1, BLEND[1], 0.0))
        fs = pushes(force[frow + 1:frow + 9, :])
        for cx in (-1, 0, 1):
            for cz in (-1, 0, 1):
                k = 3 * (cx + 1) + cz + 1
                i = slot(cx, cy, cz)
                b = built[i]
                b = b if cz == 0 else pltpu.roll(b, cz % Z, 1)
                out[k, 1:9, :] = (1.0 - blend) * push(jnp.where(odd_y, halo[0][k], halo[1][k]), i, fs) + blend * b
        for cz in (-1, 0, 1):
            n = CORNERS.index((1, cy))
            out[6 + cz + 1, 0:1, :] = got(CORNER + n, cz + 1, cz + 2) + (
                force[frow:frow + 1, :] * along[cz + 1][0:1, :])
            n = CORNERS.index((-1, cy))
            value = got(CORNER + n, cz + 1, cz + 2) - force[frow + 9:frow + 10, :] * along[cz + 1][0:1, :]
            b = ahead[3 * (cy + 1) + cz + 1]
            b = b if cz == 0 else pltpu.roll(jnp.broadcast_to(b, (8, Z)), cz % Z, 1)[0:1, :]
            out[cz + 1, 9:10, :] = (1.0 - BLEND[0]) * value + BLEND[0] * b

    copy_in(0).wait()
    copy_in(1).wait()
    for q in range(4):
        rows = slice(8 * q, 8 * q + 8)
        into = slice(8 * q + 8, 8 * q + 16)
        fs = pushes(force[rows, :])
        for k in range(9):
            rp[18 + k, 0, into, :] = push(jnp.where(odd_x, xa_ref[k, rows, :], xb_ref[k, rows, :]), 18 + k, fs)
        for p in range(2):
            built = z_stream(rebuild([got(OWN + (2 * k + p) * 4 + q) for k in range(10)]), lane)
            fs = pushes(force[YW * (p + 1) + 8 * q:YW * (p + 1) + 8 * q + 8, :])
            for i in range(27):
                rp[i, p + 1, into, :] = (1.0 - BLEND[p]) * push(r_ref[i, p, rows, :], i, fs) + BLEND[p] * built[i]
        fs = pushes(force[YW * (XW + 1) + 8 * q:YW * (XW + 1) + 8 * q + 8, :])
        built = rebuild_next([got(NEXT + 4 * k + q) for k in range(6)])
        for k in range(9):
            cz = k % 3 - 1
            b = built[k] if cz == 0 else pltpu.roll(built[k], cz % Z, 1)
            rp[k, XW + 1, into, :] = (1.0 - BLEND[0]) * push(jnp.where(odd_x, xb_ref[k, rows, :], xa_ref[k, rows, :]), k, fs) + BLEND[0] * b

    wide_lane = lax.broadcasted_iota(jnp.int32, (YW, Z), 1)
    wide_row = lax.broadcasted_iota(jnp.int32, (YW, Z), 0)

    def copy_out(x):
        return pltpu.make_async_copy(out_scr.at[:, x], out_hbm.at[:, x], sems.at[x])

    def plane(x, carry):
        @pl.when(x < XW - 2)
        def _():
            copy_in(x + 2).wait()
            for q in range(4):
                rows = slice(8 * q, 8 * q + 8)
                into = slice(8 * q + 8, 8 * q + 16)
                fs = pushes(force[pl.ds(pl.multiple_of((x + 3) * YW + 8 * q, 8), 8), :])
                for i in range(27):
                    rp[i, x + 3, into, :] = push(r_ref[i, x + 2, rows, :], i, fs)

        for i in range(27):
            cx, cy, cz = i // 9 - 1, i // 3 % 3 - 1, i % 3 - 1
            at = x + 1 - cx
            k = 3 * (cx + 1) + cz + 1
            value = rp[i, at, 8 - cy:40 - cy, :]
            if cy == 1:
                value = jnp.where(wide_row == 0, yp_scr[k, pl.ds(at, 1), :], value)
            elif cy == -1:
                value = jnp.where(wide_row == YW - 1, ym_scr[k, pl.ds(at, 1), :], value)
            if cz != 0 and (cx != 0 or cy != 0):
                value = jnp.where(wide_lane == (0 if cz == 1 else Z - 1), rp[i, x + 1, 8:40, :], value)
            out_scr[i, x, :, :] = value
        copy_out(x).start()
        return carry

    lax.fori_loop(0, XW, plane, 0)
    for x in range(XW):
        copy_out(x).wait()


def after_exchange(*args):
    return pl.pallas_call(
        last_kernel,
        in_specs=[HBM if n == 3 else VMEM for n in range(len(args))],
        out_specs=[HBM, VMEM],
        out_shape=[pltpu.HBM((27, XW, YW, Z), F32), jax.ShapeDtypeStruct((1, TURBINES), F32)],
        scratch_shapes=[
            pltpu.VMEM((27, XW + 2, 48, Z), F32),
            pltpu.VMEM((352, Z), F32),
            pltpu.VMEM((8, 128), F32),
            pltpu.VMEM((10, 8, Z), F32),
            pltpu.VMEM((10, 8, Z), F32),
            pltpu.VMEM((9, 16, Z), F32),
            pltpu.VMEM((9, 16, Z), F32),
            pltpu.VMEM((27, XW, YW, Z), F32),
            pltpu.VMEM((27, XW, YW, Z), F32),
            pltpu.SemaphoreType.DMA((XW,)),
            pltpu.SemaphoreType.DMA((XW,)),
        ],
        name="after_exchange",
        compiler_params=pltpu.CompilerParams(vmem_limit_bytes=24 << 20),
    )(*[far(a) if n == 3 else near(a) for n, a in enumerate(args)])


def body(populations, precursor, pairing, rates, loading, disc_cols, disc_turb):
    both = ("gx", "gy")
    inner = lambda n: [(i, i ^ 1) for i in range(n)]
    outer = lambda n: [(i, (i + (1 if i % 2 else -1)) % n) for i in range(n)]
    send = before_exchange(rates, populations, precursor)
    got = lax.all_to_all(send, both, 0, 0, tiled=True)
    r, xa, xb, ya, yb, w, disc = collision(
        rates, disc_cols.reshape(1, SLOTS), disc_turb.reshape(1, SLOTS), populations)
    xb = lax.ppermute(xb, "gx", outer(GX))
    xa = lax.ppermute(xa, "gx", inner(GX))
    yb = lax.ppermute(yb, "gy", outer(GY))
    ya = lax.ppermute(ya, "gy", inner(GY))
    send = route(pairing, got, disc).reshape(NDEV, PIECE, 1, Z)
    got = lax.all_to_all(send, both, 0, 0, tiled=True).reshape(NDEV * PIECE, Z)
    read, speed = after_exchange(got, w, loading.reshape(1, TURBINES), r, xa, xb, ya, yb)
    return read, speed.reshape(TURBINES)


def solution(mesh):
    in_specs = (P(None, "gx", "gy", None), P(None, "gx", "gy", None), P(), P(), P(), P(), P())
    out_specs = (P(None, "gx", "gy", None), P())
    return jax.shard_map(body, mesh=mesh, in_specs=in_specs, out_specs=out_specs, check_vma=False)
```

```python
import jax
import jax.numpy as jnp
import numpy as np
from jax import lax
from jax.experimental import pallas as pl
from jax.experimental.pallas import tpu as pltpu
from jax.sharding import PartitionSpec as P

GX, GY = 32, 4
NDEV = GX * GY
XW, YW, Z = 8, 32, 128
NY_ALL, NX_ALL = 128, 256
SLOTS = 512
TURBINES = 32
F32 = jnp.float32

OWN, NEXT, LO_OWN, HI_OWN, LO_NEXT, HI_NEXT, CORNER = 0, 80, 104, 107, 110, 111, 112
PIECE = 9
CORNERS = ((-1, -1), (-1, 1), (1, -1), (1, 1))
W_ROWS = 360
BLEND = (0.5, 0.25)

PROFILE_SUM = float(np.sum(np.exp(-np.square((np.arange(Z) - Z / 3.0) / (Z / 6.0)))))


HBM = pl.BlockSpec(memory_space=pltpu.HBM)
SMEM = pl.BlockSpec(memory_space=pltpu.SMEM)
VMEM = pl.BlockSpec(memory_space=pltpu.VMEM)


def near(array):
    return pltpu.with_memory_space_constraint(array, pltpu.VMEM)


def far(array):
    return pltpu.with_memory_space_constraint(array, pltpu.HBM)


def slot(cx, cy, cz):
    return 9 * (cx + 1) + 3 * (cy + 1) + (cz + 1)


def profile_row():
    heights = lax.broadcasted_iota(jnp.int32, (8, Z), 1).astype(F32)
    return jnp.exp(-jnp.square((heights - Z / 3.0) * (6.0 / Z)))


def forward(g):
    for stride in (1, 3, 9):
        out = list(g)
        for i in range(27):
            if (i // stride) % 3 == 0:
                a, b, c = g[i], g[i + stride], g[i + 2 * stride]
                s = c + a
                out[i] = s + 4.0 * b
                out[i + stride] = c - a
                out[i + 2 * stride] = s
        g = out
    return g


def backward(m):
    for stride in (9, 3, 1):
        out = list(m)
        for i in range(27):
            if (i // stride) % 3 == 0:
                a, b, c = m[i], m[i + stride], m[i + 2 * stride]
                out[i] = c - b
                out[i + stride] = 0.5 * (a - c)
                out[i + 2 * stride] = c + b
        m = out
    return m


def collide(g, rates):
    return relax(forward(g), rates)


def relax(m, rates):
    density = m[0] * (1.0 / 216.0)
    inv = 1.0 / m[0]
    u = (m[9] * inv, m[3] * inv, m[1] * inv)
    j = (m[9] * (1.0 / 216.0), m[3] * (1.0 / 216.0), m[1] * (1.0 / 216.0))
    ju = {}
    for a in range(3):
        for b in range(a, 3):
            ju[(a, b)] = j[a] * u[b]
    out = []
    for i in range(27):
        order = (i // 9, i // 3 % 3, i % 3)
        ones = [d for d in range(3) if order[d] == 1]
        twos = [d for d in range(3) if order[d] == 2]
        if i in (0, 1, 3, 9):
            out.append(m[i] * 0.125)
            continue
        r = rates(i)
        keep = m[i] * ((1.0 - r) * 0.125)
        if len(ones) == 3:
            out.append(keep)
            continue
        scale = r * (27.0 / 3.0 ** len(twos))
        if len(ones) == 0:
            eq = ju[(twos[0], twos[0])]
            for d in twos[1:]:
                eq = eq + ju[(d, d)]
            eq = density + 3.0 * eq
        elif len(ones) == 1:
            eq = j[ones[0]]
        else:
            eq = ju[(ones[0], ones[1])]
        out.append(keep + eq * scale)
    return backward(out)


def z_stream(p, lane):
    out = []
    for i in range(27):
        cz = i % 3 - 1
        if cz == 0:
            out.append(p[i])
        elif cz == 1:
            out.append(jnp.where(lane == 0, p[26 - i], pltpu.roll(p[i], 1, 1)))
        else:
            out.append(jnp.where(lane == Z - 1, p[26 - i], pltpu.roll(p[i], Z - 1, 1)))
    return out


def precursor_coefficients(g):
    m = forward(g)
    rho, jx, jy, jz = m[0], m[9], m[3], m[1]
    xx, yy, zz, xy, xz, yz = m[18], m[6], m[2], m[12], m[10], m[4]
    third = rho * (1.0 / 3.0)
    pxx, pyy, pzz = xx - third, yy - third, zz - third
    s = 1.0 / 216.0
    k0 = (rho - 1.5 * (pxx + pyy + pzz)) * s
    return [k0, jx * (3 * s), jy * (3 * s), jz * (3 * s), pxx * (4.5 * s), pyy * (4.5 * s), pzz * (4.5 * s),
            xy * (9 * s), xz * (9 * s), yz * (9 * s)]


def next_coefficients(c):
    return [c[0] - c[1] + c[4], c[2] - c[7], c[3] - c[8], c[5], c[6], c[9]]


def rebuild_next(c):
    out = []
    for cy in (-1, 0, 1):
        base = c[0] + (cy * c[1] + c[3] if cy else 0.0)
        lin = c[2] + cy * c[5] if cy else c[2]
        for cz in (-1, 0, 1):
            out.append(base + cz * lin + c[4] if cz else base)
    return out


def rebuild(c):
    out = []
    for cx in (-1, 0, 1):
        base = c[0] + cx * c[1] + c[4] if cx else c[0]
        liny = c[2] + cx * c[7] if cx else c[2]
        linz = c[3] + cx * c[8] if cx else c[3]
        out += rebuild_next([base, liny, linz, c[5], c[6], c[9]])
    return out


def first_kernel(rates_hbm, pop_hbm, pre_hbm, send_ref, xa_ref, xb_ref, ya_ref, yb_ref, pre_ref, edge_ref, side_ref,
                 rates_ref, sems):
    copies = [pltpu.make_async_copy(pre_hbm.at[:, p], pre_ref.at[:, p], sems.at[p]) for p in range(2)]
    for n, x in enumerate((0, XW - 1)):
        copies.append(pltpu.make_async_copy(pop_hbm.at[:, x], edge_ref.at[:, n], sems.at[2 + n]))
    copies.append(pltpu.make_async_copy(rates_hbm, rates_ref, sems.at[4]))
    for n, y in enumerate((0, YW - 1)):
        copies.append(pltpu.make_async_copy(pop_hbm.at[:, :, y, :], side_ref.at[n], sems.at[5 + n]))
    for copy in copies:
        copy.start()
    send_ref[LO_OWN:, :, :] = jnp.zeros((NDEV - LO_OWN, 8, Z), F32)
    for p in range(2):
        copies[p].wait()
        for q in range(4):
            c = precursor_coefficients([pre_ref[i, p, 8 * q:8 * q + 8, :] for i in range(27)])
            for k in range(10):
                send_ref[OWN + (2 * k + p) * 4 + q, :, :] = c[k]
                row = 2 * k + p
                if q == 3:
                    send_ref[LO_OWN + row // 8, row % 8:row % 8 + 1, :] = c[k][7:8, :]
                if q == 0:
                    send_ref[HI_OWN + row // 8, row % 8:row % 8 + 1, :] = c[k][0:1, :]
            if p == 0:
                c = next_coefficients(c)
                for k in range(6):
                    send_ref[NEXT + 4 * k + q, :, :] = c[k]
                    if q == 3:
                        send_ref[LO_NEXT, k:k + 1, :] = c[k][7:8, :]
                    if q == 0:
                        send_ref[HI_NEXT, k:k + 1, :] = c[k][0:1, :]
    copies[4].wait()
    lane = lax.broadcasted_iota(jnp.int32, (8, Z), 1)
    odd_x = (lax.axis_index("gx") & 1) == 1
    for n, cx in enumerate((-1, 1)):
        copies[2 + n].wait()
        for q in range(4):
            rows = slice(8 * q, 8 * q + 8)
            post = z_stream(collide([edge_ref[i, n, rows, :] for i in range(27)], lambda i: rates_ref[i]), lane)
            for k in range(9):
                value = post[9 * (cx + 1) + k]
                if cx < 0:
                    xa_ref[k, rows, :] = value
                else:
                    keep = xa_ref[k, rows, :]
                    xa_ref[k, rows, :] = jnp.where(odd_x, keep, value)
                    xb_ref[k, rows, :] = jnp.where(odd_x, value, keep)
    odd_y = (lax.axis_index("gy") & 1) == 1
    for n, cy in enumerate((-1, 1)):
        copies[5 + n].wait()
        post = z_stream(collide([side_ref[n, i] for i in range(27)], lambda i: rates_ref[i]), lane)
        for cx in (-1, 0, 1):
            for cz in (-1, 0, 1):
                k = 3 * (cx + 1) + cz + 1
                value = post[slot(cx, cy, cz)]
                if cy < 0:
                    ya_ref[k, :, :] = value
                else:
                    keep = ya_ref[k, :, :]
                    ya_ref[k, :, :] = jnp.where(odd_y, keep, value)
                    yb_ref[k, :, :] = jnp.where(odd_y, value, keep)
                if cx:
                    at = 0 if cx < 0 else XW - 1
                    send_ref[CORNER + CORNERS.index((cx, cy)), cz + 1:cz + 2, :] = value[at:at + 1, :]


def before_exchange(rates, populations, precursor):
    return pl.pallas_call(
        first_kernel,
        in_specs=[HBM, HBM, HBM],
        out_specs=[VMEM] * 5,
        out_shape=[pltpu.VMEM((NDEV, 8, Z), F32)] + [pltpu.VMEM((9, n, Z), F32) for n in (YW, YW, XW, XW)],
        scratch_shapes=[
            pltpu.VMEM((27, 2, YW, Z), F32),
            pltpu.VMEM((27, 2, YW, Z), F32),
            pltpu.VMEM((2, 27, XW, Z), F32),
            pltpu.SMEM((27,), F32),
            pltpu.SemaphoreType.DMA((7,)),
        ],
        name="before_exchange",
        compiler_params=pltpu.CompilerParams(vmem_limit_bytes=4 << 20),
    )(far(rates), far(populations), far(precursor))


def collide_kernel(rates_ref, cols_ref, turb_ref, pop_hbm, out_hbm, w_ref, disc_ref,
                   pop_ref, out_ref, in_sems, out_sems):
    def copy_in(x):
        return pltpu.make_async_copy(pop_hbm.at[:, x], pop_ref.at[:, x], in_sems.at[x])

    def copy_out(x):
        return pltpu.make_async_copy(out_ref.at[:, x], out_hbm.at[:, x], out_sems.at[x])

    for x in range(XW):
        copy_in(x).start()
    gx = lax.axis_index("gx")
    gy = lax.axis_index("gy")
    rows = lax.broadcasted_iota(jnp.int32, (W_ROWS, SLOTS), 0)
    lo = rows - 320
    main = rows < 320
    xx = jnp.where(main, rows >> 5, jnp.where(lo < 16, lo, lo - 16))
    yy = jnp.where(main, rows & 31, jnp.where(lo < 16, -1, YW))
    col = ((gx * XW + xx - 1) & (NX_ALL - 1)) * NY_ALL + ((gy * YW + yy) & (NY_ALL - 1))
    valid = main | ((lo & 15) < 10)
    hit = ((col == cols_ref[...]) & valid & (lo < 32)) | (lo >= 32)
    owner = lax.broadcasted_iota(jnp.int32, (128, SLOTS), 0) == turb_ref[...]
    w_ref[...] = lax.dot_general(
        jnp.where(hit, 1.0, 0.0).astype(jnp.bfloat16),
        jnp.where(owner, 1.0, 0.0).astype(jnp.bfloat16),
        (((1,), (1,)), ((), ())), preferred_element_type=F32)
    disc_ref[...] = jnp.zeros_like(disc_ref)
    lane = lax.broadcasted_iota(jnp.int32, (8, Z), 1)
    profile = profile_row()

    def plane(x, carry):
        copy_in(x).wait()
        for q in range(4):
            rows = slice(8 * q, 8 * q + 8)
            m = forward([pop_ref[i, x, rows, :] for i in range(27)])
            sums = jnp.sum(m[9] / m[0] * profile, axis=1, keepdims=True)
            disc_ref[...] += sums * w_ref[pl.ds(pl.multiple_of((x + 1) * YW + 8 * q, 8), 8), :]
            post = z_stream(relax(m, lambda i: rates_ref[i]), lane)
            for i in range(27):
                out_ref[i, x, rows, :] = post[i]
        copy_out(x).start()
        return carry

    lax.fori_loop(0, XW, plane, 0)
    for x in range(XW):
        copy_out(x).wait()


def collision(rates, cols, turb, populations):
    shapes = ((27, XW, YW, Z), (W_ROWS, 128), (8, 128))
    return pl.pallas_call(
        collide_kernel,
        in_specs=[SMEM, VMEM, VMEM, HBM],
        out_specs=[HBM] + [VMEM] * (len(shapes) - 1),
        out_shape=[pltpu.HBM(shapes[0], F32)] + [pltpu.VMEM(shape, F32) for shape in shapes[1:]],
        scratch_shapes=[
            pltpu.VMEM(shapes[0], F32),
            pltpu.VMEM(shapes[0], F32),
            pltpu.SemaphoreType.DMA((XW,)),
            pltpu.SemaphoreType.DMA((XW,)),
        ],
        name="collision",
        compiler_params=pltpu.CompilerParams(vmem_limit_bytes=12 << 20),
    )(rates, cols, turb, far(populations))


def route_kernel(pairing_ref, got_ref, disc_ref, send_ref):
    me = lax.axis_index("gx") * GY + lax.axis_index("gy")
    is_next = ((me >= NEXT) & (me < LO_OWN)) | (me == LO_NEXT) | (me == HI_NEXT)
    corner = me - CORNER
    is_corner = (corner >= 0) & (corner < 4)
    low = ((me >= LO_OWN) & (me < HI_OWN)) | (me == LO_NEXT)
    high = ((me >= HI_OWN) & (me < LO_NEXT)) | (me == HI_NEXT)
    from_x = jnp.where(corner < 2, 1, -1)
    from_y = jnp.where(is_corner, jnp.where((corner & 1) == 0, 1, -1), jnp.where(low, -1, jnp.where(high, 1, 0)))
    ahead = jnp.where(is_next, 1, 0)
    lanes = [(t + from_y) & (GY - 1) for t in range(GY)]
    part = jnp.sum(disc_ref[...], axis=0, keepdims=True)
    for d in range(GX):
        tile = pairing_ref[(d + ahead) & (GX - 1)]
        tile = jnp.where(is_corner, (d + from_x) & (GX - 1), tile) * GY
        for t in range(GY):
            at = (d * GY + t) * PIECE
            send_ref[at:at + 8, :] = got_ref[tile + lanes[t], :, :]
            send_ref[at + 8:at + 9, :] = part


def route(pairing, got, disc):
    return pl.pallas_call(
        route_kernel,
        in_specs=[SMEM, VMEM, VMEM],
        out_specs=VMEM,
        out_shape=pltpu.VMEM((NDEV * PIECE, Z), F32),
        name="route",
        compiler_params=pltpu.CompilerParams(vmem_limit_bytes=3 << 20),
    )(pairing, near(got), near(disc))


def last_kernel(got_ref, w_ref, loading_ref, r_hbm, xa_ref, xb_ref, ya_ref, yb_ref, out_hbm, speed_ref,
                rp, force, load_scr, lo_scr, hi_scr, yp_scr, ym_scr, r_ref, out_scr, in_sems, sems):
    def copy_in(x):
        return pltpu.make_async_copy(r_hbm.at[:, x], r_ref.at[:, x], in_sems.at[x])

    for x in range(XW):
        copy_in(x).start()
    lane = lax.broadcasted_iota(jnp.int32, (8, Z), 1)
    profile = profile_row()
    up = jnp.where(lane == 0, -profile, pltpu.roll(profile, 1, 1))
    down = jnp.where(lane == Z - 1, -profile, pltpu.roll(profile, Z - 1, 1))
    along = (3.0 * down, 3.0 * profile, 3.0 * up)

    odd_x = (lax.axis_index("gx") & 1) == 1
    odd_y = (lax.axis_index("gy") & 1) == 1

    def got(tile, a=0, b=8):
        return got_ref[PIECE * tile + a:PIECE * tile + b, :]

    def pushes(f):
        return [f * a for a in along]

    def push(value, i, fs):
        cx = i // 9 - 1
        return value if cx == 0 else (value + fs[i % 3] if cx > 0 else value - fs[i % 3])

    load_scr[...] = jnp.zeros_like(load_scr)
    load_scr[0:1, 0:TURBINES] = loading_ref[...]
    counts = w_ref[352:360, :]
    totals = jnp.broadcast_to(jnp.sum(got_ref[pl.ds(8, NDEV, stride=PIECE), :], axis=0, keepdims=True), (8, 128))
    k = lax.broadcasted_iota(jnp.int32, (8, 128), 1)
    speed = jnp.where(k < TURBINES, totals / (jnp.where(k < TURBINES, counts, 1.0) * PROFILE_SUM), 0.0)
    speed_ref[...] = speed[0:1, 0:TURBINES]
    thrust = (0.5 * jnp.broadcast_to(load_scr[0:1, :], (8, 128))) * speed * jnp.abs(speed)
    force[...] = -lax.dot_general(
        w_ref[0:352, :] * thrust[0:1, :], jnp.ones((128, Z), F32), (((1,), (0,)), ((), ())),
        precision=lax.Precision.HIGHEST, preferred_element_type=F32)
    for scr, tile, nxt, halo, frow, cy, out in (
        (lo_scr, LO_OWN, LO_NEXT, (ya_ref, yb_ref), 320, 1, yp_scr),
        (hi_scr, HI_OWN, HI_NEXT, (yb_ref, ya_ref), 336, -1, ym_scr),
    ):
        scr[...] = jnp.zeros_like(scr)
        for c in range(10):
            r = 2 * c
            scr[c, 0:2, :] = got(tile + r // 8, r % 8, r % 8 + 2)
        built = rebuild([scr[c] for c in range(10)])
        ahead = rebuild_next([got(nxt, c, c + 1) for c in range(6)])
        row = lax.broadcasted_iota(jnp.int32, (8, Z), 0)
        blend = jnp.where(row == 0, BLEND[0], jnp.where(row == 1, BLEND[1], 0.0))
        fs = pushes(force[frow + 1:frow + 9, :])
        for cx in (-1, 0, 1):
            for cz in (-1, 0, 1):
                k = 3 * (cx + 1) + cz + 1
                i = slot(cx, cy, cz)
                b = built[i]
                b = b if cz == 0 else pltpu.roll(b, cz % Z, 1)
                out[k, 1:9, :] = (1.0 - blend) * push(jnp.where(odd_y, halo[0][k], halo[1][k]), i, fs) + blend * b
        for cz in (-1, 0, 1):
            n = CORNERS.index((1, cy))
            out[6 + cz + 1, 0:1, :] = got(CORNER + n, cz + 1, cz + 2) + (
                force[frow:frow + 1, :] * along[cz + 1][0:1, :])
            n = CORNERS.index((-1, cy))
            value = got(CORNER + n, cz + 1, cz + 2) - force[frow + 9:frow + 10, :] * along[cz + 1][0:1, :]
            b = ahead[3 * (cy + 1) + cz + 1]
            b = b if cz == 0 else pltpu.roll(jnp.broadcast_to(b, (8, Z)), cz % Z, 1)[0:1, :]
            out[cz + 1, 9:10, :] = (1.0 - BLEND[0]) * value + BLEND[0] * b

    copy_in(0).wait()
    copy_in(1).wait()
    for q in range(4):
        rows = slice(8 * q, 8 * q + 8)
        into = slice(8 * q + 8, 8 * q + 16)
        fs = pushes(force[rows, :])
        for k in range(9):
            rp[18 + k, 0, into, :] = push(jnp.where(odd_x, xa_ref[k, rows, :], xb_ref[k, rows, :]), 18 + k, fs)
        for p in range(2):
            built = z_stream(rebuild([got(OWN + (2 * k + p) * 4 + q) for k in range(10)]), lane)
            fs = pushes(force[YW * (p + 1) + 8 * q:YW * (p + 1) + 8 * q + 8, :])
            for i in range(27):
                rp[i, p + 1, into, :] = (1.0 - BLEND[p]) * push(r_ref[i, p, rows, :], i, fs) + BLEND[p] * built[i]
        fs = pushes(force[YW * (XW + 1) + 8 * q:YW * (XW + 1) + 8 * q + 8, :])
        built = rebuild_next([got(NEXT + 4 * k + q) for k in range(6)])
        for k in range(9):
            cz = k % 3 - 1
            b = built[k] if cz == 0 else pltpu.roll(built[k], cz % Z, 1)
            rp[k, XW + 1, into, :] = (1.0 - BLEND[0]) * push(jnp.where(odd_x, xb_ref[k, rows, :], xa_ref[k, rows, :]), k, fs) + BLEND[0] * b

    wide_lane = lax.broadcasted_iota(jnp.int32, (YW, Z), 1)
    wide_row = lax.broadcasted_iota(jnp.int32, (YW, Z), 0)

    def copy_out(x):
        return pltpu.make_async_copy(out_scr.at[:, x], out_hbm.at[:, x], sems.at[x])

    def plane(x, carry):
        @pl.when(x < XW - 2)
        def _():
            copy_in(x + 2).wait()
            for q in range(4):
                rows = slice(8 * q, 8 * q + 8)
                into = slice(8 * q + 8, 8 * q + 16)
                fs = pushes(force[pl.ds(pl.multiple_of((x + 3) * YW + 8 * q, 8), 8), :])
                for i in range(27):
                    rp[i, x + 3, into, :] = push(r_ref[i, x + 2, rows, :], i, fs)

        for i in range(27):
            cx, cy, cz = i // 9 - 1, i // 3 % 3 - 1, i % 3 - 1
            at = x + 1 - cx
            k = 3 * (cx + 1) + cz + 1
            value = rp[i, at, 8 - cy:40 - cy, :]
            if cy == 1:
                value = jnp.where(wide_row == 0, yp_scr[k, pl.ds(at, 1), :], value)
            elif cy == -1:
                value = jnp.where(wide_row == YW - 1, ym_scr[k, pl.ds(at, 1), :], value)
            if cz != 0 and (cx != 0 or cy != 0):
                value = jnp.where(wide_lane == (0 if cz == 1 else Z - 1), rp[i, x + 1, 8:40, :], value)
            out_scr[i, x, :, :] = value
        copy_out(x).start()
        return carry

    lax.fori_loop(0, XW, plane, 0)
    for x in range(XW):
        copy_out(x).wait()


def after_exchange(*args):
    return pl.pallas_call(
        last_kernel,
        in_specs=[HBM if n == 3 else VMEM for n in range(len(args))],
        out_specs=[HBM, VMEM],
        out_shape=[pltpu.HBM((27, XW, YW, Z), F32), jax.ShapeDtypeStruct((1, TURBINES), F32)],
        scratch_shapes=[
            pltpu.VMEM((27, XW + 2, 48, Z), F32),
            pltpu.VMEM((352, Z), F32),
            pltpu.VMEM((8, 128), F32),
            pltpu.VMEM((10, 8, Z), F32),
            pltpu.VMEM((10, 8, Z), F32),
            pltpu.VMEM((9, 16, Z), F32),
            pltpu.VMEM((9, 16, Z), F32),
            pltpu.VMEM((27, XW, YW, Z), F32),
            pltpu.VMEM((27, XW, YW, Z), F32),
            pltpu.SemaphoreType.DMA((XW,)),
            pltpu.SemaphoreType.DMA((XW,)),
        ],
        name="after_exchange",
        compiler_params=pltpu.CompilerParams(vmem_limit_bytes=24 << 20),
    )(*[far(a) if n == 3 else near(a) for n, a in enumerate(args)])


def body(populations, precursor, pairing, rates, loading, disc_cols, disc_turb):
    both = ("gx", "gy")
    inner = lambda n: [(i, i ^ 1) for i in range(n)]
    outer = lambda n: [(i, (i + (1 if i % 2 else -1)) % n) for i in range(n)]
    send, xa, xb, ya, yb = before_exchange(rates, populations, precursor)
    got = lax.all_to_all(send, both, 0, 0, tiled=True)
    r, w, disc = collision(
        rates, disc_cols.reshape(1, SLOTS), disc_turb.reshape(1, SLOTS), populations)
    xb = lax.ppermute(xb, "gx", outer(GX))
    xa = lax.ppermute(xa, "gx", inner(GX))
    yb = lax.ppermute(yb, "gy", outer(GY))
    ya = lax.ppermute(ya, "gy", inner(GY))
    send, xa, xb, ya, yb = lax.optimization_barrier((route(pairing, got, disc), xa, xb, ya, yb))
    send = send.reshape(NDEV, PIECE, 1, Z)
    got = lax.all_to_all(send, both, 0, 0, tiled=True).reshape(NDEV * PIECE, Z)
    read, speed = after_exchange(got, w, loading.reshape(1, TURBINES), r, xa, xb, ya, yb)
    return read, speed.reshape(TURBINES)


def solution(mesh):
    in_specs = (P(None, "gx", "gy", None), P(None, "gx", "gy", None), P(), P(), P(), P(), P())
    out_specs = (P(None, "gx", "gy", None), P())
    return jax.shard_map(body, mesh=mesh, in_specs=in_specs, out_specs=out_specs, check_vma=False)
```

```python
import jax
import jax.numpy as jnp
import numpy as np
from jax import lax
from jax.experimental import pallas as pl
from jax.experimental.pallas import tpu as pltpu
from jax.sharding import PartitionSpec as P

GX, GY = 32, 4
NDEV = GX * GY
XW, YW, Z = 8, 32, 128
NY_ALL, NX_ALL = 128, 256
SLOTS = 512
TURBINES = 32
F32 = jnp.float32

OWN, NEXT, LO_OWN, HI_OWN, LO_NEXT, HI_NEXT, CORNER = 0, 80, 104, 107, 110, 111, 112
PIECE = 9
CORNERS = ((-1, -1), (-1, 1), (1, -1), (1, 1))
W_ROWS = 360
BLEND = (0.5, 0.25)

PROFILE_SUM = float(np.sum(np.exp(-np.square((np.arange(Z) - Z / 3.0) / (Z / 6.0)))))


HBM = pl.BlockSpec(memory_space=pltpu.HBM)
SMEM = pl.BlockSpec(memory_space=pltpu.SMEM)
VMEM = pl.BlockSpec(memory_space=pltpu.VMEM)


def near(array):
    return pltpu.with_memory_space_constraint(array, pltpu.VMEM)


def far(array):
    return pltpu.with_memory_space_constraint(array, pltpu.HBM)


def slot(cx, cy, cz):
    return 9 * (cx + 1) + 3 * (cy + 1) + (cz + 1)


def profile_row():
    heights = lax.broadcasted_iota(jnp.int32, (8, Z), 1).astype(F32)
    return jnp.exp(-jnp.square((heights - Z / 3.0) * (6.0 / Z)))


def forward(g):
    for stride in (1, 3, 9):
        out = list(g)
        for i in range(27):
            if (i // stride) % 3 == 0:
                a, b, c = g[i], g[i + stride], g[i + 2 * stride]
                s = c + a
                out[i] = s + 4.0 * b
                out[i + stride] = c - a
                out[i + 2 * stride] = s
        g = out
    return g


def backward(m):
    for stride in (9, 3, 1):
        out = list(m)
        for i in range(27):
            if (i // stride) % 3 == 0:
                a, b, c = m[i], m[i + stride], m[i + 2 * stride]
                out[i] = c - b
                out[i + stride] = 0.5 * (a - c)
                out[i + 2 * stride] = c + b
        m = out
    return m


def collide(g, rates):
    return relax(forward(g), rates)


def relax(m, rates):
    density = m[0] * (1.0 / 216.0)
    inv = 1.0 / m[0]
    u = (m[9] * inv, m[3] * inv, m[1] * inv)
    j = (m[9] * (1.0 / 216.0), m[3] * (1.0 / 216.0), m[1] * (1.0 / 216.0))
    ju = {}
    for a in range(3):
        for b in range(a, 3):
            ju[(a, b)] = j[a] * u[b]
    out = []
    for i in range(27):
        order = (i // 9, i // 3 % 3, i % 3)
        ones = [d for d in range(3) if order[d] == 1]
        twos = [d for d in range(3) if order[d] == 2]
        if i in (0, 1, 3, 9):
            out.append(m[i] * 0.125)
            continue
        r = rates(i)
        keep = m[i] * ((1.0 - r) * 0.125)
        if len(ones) == 3:
            out.append(keep)
            continue
        scale = r * (27.0 / 3.0 ** len(twos))
        if len(ones) == 0:
            eq = ju[(twos[0], twos[0])]
            for d in twos[1:]:
                eq = eq + ju[(d, d)]
            eq = density + 3.0 * eq
        elif len(ones) == 1:
            eq = j[ones[0]]
        else:
            eq = ju[(ones[0], ones[1])]
        out.append(keep + eq * scale)
    return backward(out)


def z_stream(p, lane):
    out = []
    for i in range(27):
        cz = i % 3 - 1
        if cz == 0:
            out.append(p[i])
        elif cz == 1:
            out.append(jnp.where(lane == 0, p[26 - i], pltpu.roll(p[i], 1, 1)))
        else:
            out.append(jnp.where(lane == Z - 1, p[26 - i], pltpu.roll(p[i], Z - 1, 1)))
    return out


def precursor_coefficients(g):
    m = forward(g)
    rho, jx, jy, jz = m[0], m[9], m[3], m[1]
    xx, yy, zz, xy, xz, yz = m[18], m[6], m[2], m[12], m[10], m[4]
    third = rho * (1.0 / 3.0)
    pxx, pyy, pzz = xx - third, yy - third, zz - third
    s = 1.0 / 216.0
    k0 = (rho - 1.5 * (pxx + pyy + pzz)) * s
    return [k0, jx * (3 * s), jy * (3 * s), jz * (3 * s), pxx * (4.5 * s), pyy * (4.5 * s), pzz * (4.5 * s),
            xy * (9 * s), xz * (9 * s), yz * (9 * s)]


def next_coefficients(c):
    return [c[0] - c[1] + c[4], c[2] - c[7], c[3] - c[8], c[5], c[6], c[9]]


def rebuild_next(c):
    out = []
    for cy in (-1, 0, 1):
        base = c[0] + (cy * c[1] + c[3] if cy else 0.0)
        lin = c[2] + cy * c[5] if cy else c[2]
        for cz in (-1, 0, 1):
            out.append(base + cz * lin + c[4] if cz else base)
    return out


def rebuild(c):
    out = []
    for cx in (-1, 0, 1):
        base = c[0] + cx * c[1] + c[4] if cx else c[0]
        liny = c[2] + cx * c[7] if cx else c[2]
        linz = c[3] + cx * c[8] if cx else c[3]
        out += rebuild_next([base, liny, linz, c[5], c[6], c[9]])
    return out


def first_kernel(rates_hbm, pop_hbm, pre_hbm, send_hbm, xa_ref, xb_ref, ya_ref, yb_ref, pre_ref, edge_ref, side_ref,
                 rates_ref, send_ref, sems):
    copies = [pltpu.make_async_copy(pre_hbm.at[:, p], pre_ref.at[:, p], sems.at[p]) for p in range(2)]
    for n, x in enumerate((0, XW - 1)):
        copies.append(pltpu.make_async_copy(pop_hbm.at[:, x], edge_ref.at[:, n], sems.at[2 + n]))
    copies.append(pltpu.make_async_copy(rates_hbm, rates_ref, sems.at[4]))
    for n, y in enumerate((0, YW - 1)):
        copies.append(pltpu.make_async_copy(pop_hbm.at[:, :, y, :], side_ref.at[n], sems.at[5 + n]))
    for copy in copies:
        copy.start()
    send_ref[LO_OWN:, :, :] = jnp.zeros((NDEV - LO_OWN, 8, Z), F32)
    for p in range(2):
        copies[p].wait()
        for q in range(4):
            c = precursor_coefficients([pre_ref[i, p, 8 * q:8 * q + 8, :] for i in range(27)])
            for k in range(10):
                send_ref[OWN + (2 * k + p) * 4 + q, :, :] = c[k]
                row = 2 * k + p
                if q == 3:
                    send_ref[LO_OWN + row // 8, row % 8:row % 8 + 1, :] = c[k][7:8, :]
                if q == 0:
                    send_ref[HI_OWN + row // 8, row % 8:row % 8 + 1, :] = c[k][0:1, :]
            if p == 0:
                c = next_coefficients(c)
                for k in range(6):
                    send_ref[NEXT + 4 * k + q, :, :] = c[k]
                    if q == 3:
                        send_ref[LO_NEXT, k:k + 1, :] = c[k][7:8, :]
                    if q == 0:
                        send_ref[HI_NEXT, k:k + 1, :] = c[k][0:1, :]
    sends = [pltpu.make_async_copy(send_ref.at[0:LO_OWN], send_hbm.at[0:LO_OWN], sems.at[7]),
             pltpu.make_async_copy(send_ref.at[LO_OWN:NDEV], send_hbm.at[LO_OWN:NDEV], sems.at[8])]
    sends[0].start()
    copies[4].wait()
    lane = lax.broadcasted_iota(jnp.int32, (8, Z), 1)
    odd_x = (lax.axis_index("gx") & 1) == 1
    for n, cx in enumerate((-1, 1)):
        copies[2 + n].wait()
        for q in range(4):
            rows = slice(8 * q, 8 * q + 8)
            post = z_stream(collide([edge_ref[i, n, rows, :] for i in range(27)], lambda i: rates_ref[i]), lane)
            for k in range(9):
                value = post[9 * (cx + 1) + k]
                if cx < 0:
                    xa_ref[k, rows, :] = value
                else:
                    keep = xa_ref[k, rows, :]
                    xa_ref[k, rows, :] = jnp.where(odd_x, keep, value)
                    xb_ref[k, rows, :] = jnp.where(odd_x, value, keep)
    odd_y = (lax.axis_index("gy") & 1) == 1
    for n, cy in enumerate((-1, 1)):
        copies[5 + n].wait()
        post = z_stream(collide([side_ref[n, i] for i in range(27)], lambda i: rates_ref[i]), lane)
        for cx in (-1, 0, 1):
            for cz in (-1, 0, 1):
                k = 3 * (cx + 1) + cz + 1
                value = post[slot(cx, cy, cz)]
                if cy < 0:
                    ya_ref[k, :, :] = value
                else:
                    keep = ya_ref[k, :, :]
                    ya_ref[k, :, :] = jnp.where(odd_y, keep, value)
                    yb_ref[k, :, :] = jnp.where(odd_y, value, keep)
                if cx:
                    at = 0 if cx < 0 else XW - 1
                    send_ref[CORNER + CORNERS.index((cx, cy)), cz + 1:cz + 2, :] = value[at:at + 1, :]
    sends[1].start()
    for copy in sends:
        copy.wait()


def before_exchange(rates, populations, precursor):
    return pl.pallas_call(
        first_kernel,
        in_specs=[HBM, HBM, HBM],
        out_specs=[HBM] + [VMEM] * 4,
        out_shape=[pltpu.HBM((NDEV, 8, Z), F32)] + [pltpu.VMEM((9, n, Z), F32) for n in (YW, YW, XW, XW)],
        scratch_shapes=[
            pltpu.VMEM((27, 2, YW, Z), F32),
            pltpu.VMEM((27, 2, YW, Z), F32),
            pltpu.VMEM((2, 27, XW, Z), F32),
            pltpu.SMEM((27,), F32),
            pltpu.VMEM((NDEV, 8, Z), F32),
            pltpu.SemaphoreType.DMA((9,)),
        ],
        name="before_exchange",
        compiler_params=pltpu.CompilerParams(vmem_limit_bytes=4 << 20),
    )(far(rates), far(populations), far(precursor))


def collide_kernel(rates_ref, cols_ref, turb_ref, pop_hbm, out_hbm, w_ref, disc_ref,
                   pop_ref, out_ref, in_sems, out_sems):
    def copy_in(x):
        return pltpu.make_async_copy(pop_hbm.at[:, x], pop_ref.at[:, x], in_sems.at[x])

    def copy_out(x):
        return pltpu.make_async_copy(out_ref.at[:, x], out_hbm.at[:, x], out_sems.at[x])

    for x in range(XW):
        copy_in(x).start()
    gx = lax.axis_index("gx")
    gy = lax.axis_index("gy")
    rows = lax.broadcasted_iota(jnp.int32, (W_ROWS, SLOTS), 0)
    lo = rows - 320
    main = rows < 320
    xx = jnp.where(main, rows >> 5, jnp.where(lo < 16, lo, lo - 16))
    yy = jnp.where(main, rows & 31, jnp.where(lo < 16, -1, YW))
    col = ((gx * XW + xx - 1) & (NX_ALL - 1)) * NY_ALL + ((gy * YW + yy) & (NY_ALL - 1))
    valid = main | ((lo & 15) < 10)
    hit = ((col == cols_ref[...]) & valid & (lo < 32)) | (lo >= 32)
    owner = lax.broadcasted_iota(jnp.int32, (128, SLOTS), 0) == turb_ref[...]
    w_ref[...] = lax.dot_general(
        jnp.where(hit, 1.0, 0.0).astype(jnp.bfloat16),
        jnp.where(owner, 1.0, 0.0).astype(jnp.bfloat16),
        (((1,), (1,)), ((), ())), preferred_element_type=F32)
    disc_ref[...] = jnp.zeros_like(disc_ref)
    lane = lax.broadcasted_iota(jnp.int32, (8, Z), 1)
    profile = profile_row()

    def plane(x, carry):
        copy_in(x).wait()
        for q in range(4):
            rows = slice(8 * q, 8 * q + 8)
            m = forward([pop_ref[i, x, rows, :] for i in range(27)])
            sums = jnp.sum(m[9] / m[0] * profile, axis=1, keepdims=True)
            disc_ref[...] += sums * w_ref[pl.ds(pl.multiple_of((x + 1) * YW + 8 * q, 8), 8), :]
            post = z_stream(relax(m, lambda i: rates_ref[i]), lane)
            for i in range(27):
                out_ref[i, x, rows, :] = post[i]
        copy_out(x).start()
        return carry

    lax.fori_loop(0, XW, plane, 0)
    for x in range(XW):
        copy_out(x).wait()


def collision(rates, cols, turb, populations):
    shapes = ((27, XW, YW, Z), (W_ROWS, 128), (8, 128))
    return pl.pallas_call(
        collide_kernel,
        in_specs=[SMEM, VMEM, VMEM, HBM],
        out_specs=[HBM] + [VMEM] * (len(shapes) - 1),
        out_shape=[pltpu.HBM(shapes[0], F32)] + [pltpu.VMEM(shape, F32) for shape in shapes[1:]],
        scratch_shapes=[
            pltpu.VMEM(shapes[0], F32),
            pltpu.VMEM(shapes[0], F32),
            pltpu.SemaphoreType.DMA((XW,)),
            pltpu.SemaphoreType.DMA((XW,)),
        ],
        name="collision",
        compiler_params=pltpu.CompilerParams(vmem_limit_bytes=12 << 20),
    )(rates, cols, turb, far(populations))


def route_kernel(pairing_ref, got_ref, disc_ref, send_hbm, send_ref, sems):
    me = lax.axis_index("gx") * GY + lax.axis_index("gy")
    is_next = ((me >= NEXT) & (me < LO_OWN)) | (me == LO_NEXT) | (me == HI_NEXT)
    corner = me - CORNER
    is_corner = (corner >= 0) & (corner < 4)
    low = ((me >= LO_OWN) & (me < HI_OWN)) | (me == LO_NEXT)
    high = ((me >= HI_OWN) & (me < LO_NEXT)) | (me == HI_NEXT)
    from_x = jnp.where(corner < 2, 1, -1)
    from_y = jnp.where(is_corner, jnp.where((corner & 1) == 0, 1, -1), jnp.where(low, -1, jnp.where(high, 1, 0)))
    ahead = jnp.where(is_next, 1, 0)
    lanes = [(t + from_y) & (GY - 1) for t in range(GY)]
    part = jnp.sum(disc_ref[...], axis=0, keepdims=True)
    copies = []
    for d in range(GX):
        tile = pairing_ref[(d + ahead) & (GX - 1)]
        tile = jnp.where(is_corner, (d + from_x) & (GX - 1), tile) * GY
        for t in range(GY):
            at = (d * GY + t) * PIECE
            send_ref[at:at + 8, :] = got_ref[tile + lanes[t], :, :]
            send_ref[at + 8:at + 9, :] = part
        if d % 8 == 7:
            rows = slice((d - 7) * GY * PIECE, (d + 1) * GY * PIECE)
            copies.append(pltpu.make_async_copy(send_ref.at[rows], send_hbm.at[rows], sems.at[d // 8]))
            copies[-1].start()
    for copy in copies:
        copy.wait()


def route(pairing, got, disc):
    return pl.pallas_call(
        route_kernel,
        in_specs=[SMEM, VMEM, VMEM],
        out_specs=HBM,
        out_shape=pltpu.HBM((NDEV * PIECE, Z), F32),
        scratch_shapes=[pltpu.VMEM((NDEV * PIECE, Z), F32), pltpu.SemaphoreType.DMA((GX // 8,))],
        name="route",
        compiler_params=pltpu.CompilerParams(vmem_limit_bytes=3 << 20),
    )(pairing, near(got), near(disc))


def side_kernel(xa_ref, xb_ref, ya_ref, yb_ref, xm_ref, xp_ref, ym_ref, yp_ref):
    odd_x = (lax.axis_index("gx") & 1) == 1
    odd_y = (lax.axis_index("gy") & 1) == 1
    for k in range(9):
        xm_ref[k] = jnp.where(odd_x, xb_ref[k], xa_ref[k])
        xp_ref[k] = jnp.where(odd_x, xa_ref[k], xb_ref[k])
        ym_ref[k] = jnp.where(odd_y, yb_ref[k], ya_ref[k])
        yp_ref[k] = jnp.where(odd_y, ya_ref[k], yb_ref[k])


def sides(*borders):
    return pl.pallas_call(
        side_kernel,
        in_specs=[VMEM] * 4,
        out_specs=[VMEM] * 4,
        out_shape=[pltpu.VMEM(b.shape, F32) for b in borders],
        name="sides",
        compiler_params=pltpu.CompilerParams(vmem_limit_bytes=2 << 20),
        cost_estimate=pl.CostEstimate(flops=7 * 10**9, transcendentals=0, bytes_accessed=10**6),
    )(*[near(b) for b in borders])


def last_kernel(got_ref, w_ref, loading_ref, r_hbm, xm_ref, xp_ref, ym_ref, yp_ref, out_hbm, speed_ref,
                rp, force, load_scr, lo_scr, hi_scr, yp_scr, ym_scr, r_ref, out_scr, in_sems, sems):
    def copy_in(x):
        return pltpu.make_async_copy(r_hbm.at[:, x], r_ref.at[:, x], in_sems.at[x])

    for x in range(XW):
        copy_in(x).start()
    lane = lax.broadcasted_iota(jnp.int32, (8, Z), 1)
    profile = profile_row()
    up = jnp.where(lane == 0, -profile, pltpu.roll(profile, 1, 1))
    down = jnp.where(lane == Z - 1, -profile, pltpu.roll(profile, Z - 1, 1))
    along = (3.0 * down, 3.0 * profile, 3.0 * up)

    def got(tile, a=0, b=8):
        return got_ref[PIECE * tile + a:PIECE * tile + b, :]

    def pushes(f):
        return [f * a for a in along]

    def push(value, i, fs):
        cx = i // 9 - 1
        return value if cx == 0 else (value + fs[i % 3] if cx > 0 else value - fs[i % 3])

    load_scr[...] = jnp.zeros_like(load_scr)
    load_scr[0:1, 0:TURBINES] = loading_ref[...]
    counts = w_ref[352:360, :]
    totals = jnp.broadcast_to(jnp.sum(got_ref[pl.ds(8, NDEV, stride=PIECE), :], axis=0, keepdims=True), (8, 128))
    k = lax.broadcasted_iota(jnp.int32, (8, 128), 1)
    speed = jnp.where(k < TURBINES, totals / (jnp.where(k < TURBINES, counts, 1.0) * PROFILE_SUM), 0.0)
    speed_ref[...] = speed[0:1, 0:TURBINES]
    thrust = (0.5 * jnp.broadcast_to(load_scr[0:1, :], (8, 128))) * speed * jnp.abs(speed)
    force[...] = -lax.dot_general(
        w_ref[0:352, :] * thrust[0:1, :], jnp.ones((128, Z), F32), (((1,), (0,)), ((), ())),
        precision=lax.Precision.HIGHEST, preferred_element_type=F32)
    for scr, tile, nxt, halo, frow, cy, out in (
        (lo_scr, LO_OWN, LO_NEXT, yp_ref, 320, 1, yp_scr),
        (hi_scr, HI_OWN, HI_NEXT, ym_ref, 336, -1, ym_scr),
    ):
        scr[...] = jnp.zeros_like(scr)
        for c in range(10):
            r = 2 * c
            scr[c, 0:2, :] = got(tile + r // 8, r % 8, r % 8 + 2)
        built = rebuild([scr[c] for c in range(10)])
        ahead = rebuild_next([got(nxt, c, c + 1) for c in range(6)])
        row = lax.broadcasted_iota(jnp.int32, (8, Z), 0)
        blend = jnp.where(row == 0, BLEND[0], jnp.where(row == 1, BLEND[1], 0.0))
        fs = pushes(force[frow + 1:frow + 9, :])
        for cx in (-1, 0, 1):
            for cz in (-1, 0, 1):
                k = 3 * (cx + 1) + cz + 1
                i = slot(cx, cy, cz)
                b = built[i]
                b = b if cz == 0 else pltpu.roll(b, cz % Z, 1)
                out[k, 1:9, :] = (1.0 - blend) * push(halo[k], i, fs) + blend * b
        for cz in (-1, 0, 1):
            n = CORNERS.index((1, cy))
            out[6 + cz + 1, 0:1, :] = got(CORNER + n, cz + 1, cz + 2) + (
                force[frow:frow + 1, :] * along[cz + 1][0:1, :])
            n = CORNERS.index((-1, cy))
            value = got(CORNER + n, cz + 1, cz + 2) - force[frow + 9:frow + 10, :] * along[cz + 1][0:1, :]
            b = ahead[3 * (cy + 1) + cz + 1]
            b = b if cz == 0 else pltpu.roll(jnp.broadcast_to(b, (8, Z)), cz % Z, 1)[0:1, :]
            out[cz + 1, 9:10, :] = (1.0 - BLEND[0]) * value + BLEND[0] * b

    copy_in(0).wait()
    copy_in(1).wait()
    for q in range(4):
        rows = slice(8 * q, 8 * q + 8)
        into = slice(8 * q + 8, 8 * q + 16)
        fs = pushes(force[rows, :])
        for k in range(9):
            rp[18 + k, 0, into, :] = push(xp_ref[k, rows, :], 18 + k, fs)
        for p in range(2):
            built = z_stream(rebuild([got(OWN + (2 * k + p) * 4 + q) for k in range(10)]), lane)
            fs = pushes(force[YW * (p + 1) + 8 * q:YW * (p + 1) + 8 * q + 8, :])
            for i in range(27):
                rp[i, p + 1, into, :] = (1.0 - BLEND[p]) * push(r_ref[i, p, rows, :], i, fs) + BLEND[p] * built[i]
        fs = pushes(force[YW * (XW + 1) + 8 * q:YW * (XW + 1) + 8 * q + 8, :])
        built = rebuild_next([got(NEXT + 4 * k + q) for k in range(6)])
        for k in range(9):
            cz = k % 3 - 1
            b = built[k] if cz == 0 else pltpu.roll(built[k], cz % Z, 1)
            rp[k, XW + 1, into, :] = (1.0 - BLEND[0]) * push(xm_ref[k, rows, :], k, fs) + BLEND[0] * b

    wide_lane = lax.broadcasted_iota(jnp.int32, (YW, Z), 1)
    wide_row = lax.broadcasted_iota(jnp.int32, (YW, Z), 0)

    def copy_out(x):
        return pltpu.make_async_copy(out_scr.at[:, x], out_hbm.at[:, x], sems.at[x])

    def plane(x, carry):
        @pl.when(x < XW - 2)
        def _():
            copy_in(x + 2).wait()
            for q in range(4):
                rows = slice(8 * q, 8 * q + 8)
                into = slice(8 * q + 8, 8 * q + 16)
                fs = pushes(force[pl.ds(pl.multiple_of((x + 3) * YW + 8 * q, 8), 8), :])
                for i in range(27):
                    rp[i, x + 3, into, :] = push(r_ref[i, x + 2, rows, :], i, fs)

        for i in range(27):
            cx, cy, cz = i // 9 - 1, i // 3 % 3 - 1, i % 3 - 1
            at = x + 1 - cx
            k = 3 * (cx + 1) + cz + 1
            value = rp[i, at, 8 - cy:40 - cy, :]
            if cy == 1:
                value = jnp.where(wide_row == 0, yp_scr[k, pl.ds(at, 1), :], value)
            elif cy == -1:
                value = jnp.where(wide_row == YW - 1, ym_scr[k, pl.ds(at, 1), :], value)
            if cz != 0 and (cx != 0 or cy != 0):
                value = jnp.where(wide_lane == (0 if cz == 1 else Z - 1), rp[i, x + 1, 8:40, :], value)
            out_scr[i, x, :, :] = value
        copy_out(x).start()
        return carry

    lax.fori_loop(0, XW, plane, 0)
    for x in range(XW):
        copy_out(x).wait()


def after_exchange(*args):
    return pl.pallas_call(
        last_kernel,
        in_specs=[HBM if n == 3 else VMEM for n in range(len(args))],
        out_specs=[HBM, VMEM],
        out_shape=[pltpu.HBM((27, XW, YW, Z), F32), jax.ShapeDtypeStruct((1, TURBINES), F32)],
        scratch_shapes=[
            pltpu.VMEM((27, XW + 2, 48, Z), F32),
            pltpu.VMEM((352, Z), F32),
            pltpu.VMEM((8, 128), F32),
            pltpu.VMEM((10, 8, Z), F32),
            pltpu.VMEM((10, 8, Z), F32),
            pltpu.VMEM((9, 16, Z), F32),
            pltpu.VMEM((9, 16, Z), F32),
            pltpu.VMEM((27, XW, YW, Z), F32),
            pltpu.VMEM((27, XW, YW, Z), F32),
            pltpu.SemaphoreType.DMA((XW,)),
            pltpu.SemaphoreType.DMA((XW,)),
        ],
        name="after_exchange",
        compiler_params=pltpu.CompilerParams(vmem_limit_bytes=24 << 20),
    )(*[far(a) if n == 3 else near(a) for n, a in enumerate(args)])


def body(populations, precursor, pairing, rates, loading, disc_cols, disc_turb):
    both = ("gx", "gy")
    inner = lambda n: [(i, i ^ 1) for i in range(n)]
    outer = lambda n: [(i, (i + (1 if i % 2 else -1)) % n) for i in range(n)]
    send, xa, xb, ya, yb = before_exchange(rates, populations, precursor)
    got = lax.all_to_all(send, both, 0, 0, tiled=True)
    r, w, disc = collision(
        rates, disc_cols.reshape(1, SLOTS), disc_turb.reshape(1, SLOTS), populations)
    xb = lax.ppermute(xb, "gx", outer(GX))
    xa = lax.ppermute(xa, "gx", inner(GX))
    yb = lax.ppermute(yb, "gy", outer(GY))
    ya = lax.ppermute(ya, "gy", inner(GY))
    send = route(pairing, got, disc).reshape(NDEV, PIECE, 1, Z)
    got = lax.all_to_all(send, both, 0, 0, tiled=True).reshape(NDEV * PIECE, Z)
    read, speed = after_exchange(got, w, loading.reshape(1, TURBINES), r, *sides(xa, xb, ya, yb))
    return read, speed.reshape(TURBINES)


def solution(mesh):
    in_specs = (P(None, "gx", "gy", None), P(None, "gx", "gy", None), P(), P(), P(), P(), P())
    out_specs = (P(None, "gx", "gy", None), P())
    return jax.shard_map(body, mesh=mesh, in_specs=in_specs, out_specs=out_specs, check_vma=False)
```

```python
import jax
import jax.numpy as jnp
import numpy as np
from jax import lax
from jax.experimental import pallas as pl
from jax.experimental.pallas import tpu as pltpu
from jax.sharding import PartitionSpec as P

GX, GY = 32, 4
NDEV = GX * GY
XW, YW, Z = 8, 32, 128
NY_ALL, NX_ALL = 128, 256
SLOTS = 512
TURBINES = 32
F32 = jnp.float32

OWN, NEXT, LO_OWN, HI_OWN, LO_NEXT, HI_NEXT, CORNER = 0, 80, 104, 107, 110, 111, 112
PIECE = 9
CORNERS = ((-1, -1), (-1, 1), (1, -1), (1, 1))
W_ROWS = 360
BLEND = (0.5, 0.25)

PROFILE_SUM = float(np.sum(np.exp(-np.square((np.arange(Z) - Z / 3.0) / (Z / 6.0)))))


HBM = pl.BlockSpec(memory_space=pltpu.HBM)
SMEM = pl.BlockSpec(memory_space=pltpu.SMEM)
VMEM = pl.BlockSpec(memory_space=pltpu.VMEM)


def near(array):
    return pltpu.with_memory_space_constraint(array, pltpu.VMEM)


def far(array):
    return pltpu.with_memory_space_constraint(array, pltpu.HBM)


def slot(cx, cy, cz):
    return 9 * (cx + 1) + 3 * (cy + 1) + (cz + 1)


def profile_row():
    heights = lax.broadcasted_iota(jnp.int32, (8, Z), 1).astype(F32)
    return jnp.exp(-jnp.square((heights - Z / 3.0) * (6.0 / Z)))


def forward(g):
    for stride in (1, 3, 9):
        out = list(g)
        for i in range(27):
            if (i // stride) % 3 == 0:
                a, b, c = g[i], g[i + stride], g[i + 2 * stride]
                s = c + a
                out[i] = s + 4.0 * b
                out[i + stride] = c - a
                out[i + 2 * stride] = s
        g = out
    return g


def backward(m):
    for stride in (9, 3, 1):
        out = list(m)
        for i in range(27):
            if (i // stride) % 3 == 0:
                a, b, c = m[i], m[i + stride], m[i + 2 * stride]
                out[i] = c - b
                out[i + stride] = 0.5 * (a - c)
                out[i + 2 * stride] = c + b
        m = out
    return m


def collide(g, rates):
    return relax(forward(g), rates)


def relax(m, rates):
    density = m[0] * (1.0 / 216.0)
    inv = 1.0 / m[0]
    u = (m[9] * inv, m[3] * inv, m[1] * inv)
    j = (m[9] * (1.0 / 216.0), m[3] * (1.0 / 216.0), m[1] * (1.0 / 216.0))
    ju = {}
    for a in range(3):
        for b in range(a, 3):
            ju[(a, b)] = j[a] * u[b]
    out = []
    for i in range(27):
        order = (i // 9, i // 3 % 3, i % 3)
        ones = [d for d in range(3) if order[d] == 1]
        twos = [d for d in range(3) if order[d] == 2]
        if i in (0, 1, 3, 9):
            out.append(m[i] * 0.125)
            continue
        r = rates(i)
        keep = m[i] * ((1.0 - r) * 0.125)
        if len(ones) == 3:
            out.append(keep)
            continue
        scale = r * (27.0 / 3.0 ** len(twos))
        if len(ones) == 0:
            eq = ju[(twos[0], twos[0])]
            for d in twos[1:]:
                eq = eq + ju[(d, d)]
            eq = density + 3.0 * eq
        elif len(ones) == 1:
            eq = j[ones[0]]
        else:
            eq = ju[(ones[0], ones[1])]
        out.append(keep + eq * scale)
    return backward(out)


def z_stream(p, lane):
    out = []
    for i in range(27):
        cz = i % 3 - 1
        if cz == 0:
            out.append(p[i])
        elif cz == 1:
            out.append(jnp.where(lane == 0, p[26 - i], pltpu.roll(p[i], 1, 1)))
        else:
            out.append(jnp.where(lane == Z - 1, p[26 - i], pltpu.roll(p[i], Z - 1, 1)))
    return out


def precursor_coefficients(g):
    m = forward(g)
    rho, jx, jy, jz = m[0], m[9], m[3], m[1]
    xx, yy, zz, xy, xz, yz = m[18], m[6], m[2], m[12], m[10], m[4]
    third = rho * (1.0 / 3.0)
    pxx, pyy, pzz = xx - third, yy - third, zz - third
    s = 1.0 / 216.0
    k0 = (rho - 1.5 * (pxx + pyy + pzz)) * s
    return [k0, jx * (3 * s), jy * (3 * s), jz * (3 * s), pxx * (4.5 * s), pyy * (4.5 * s), pzz * (4.5 * s),
            xy * (9 * s), xz * (9 * s), yz * (9 * s)]


def next_coefficients(c):
    return [c[0] - c[1] + c[4], c[2] - c[7], c[3] - c[8], c[5], c[6], c[9]]


def rebuild_next(c):
    out = []
    for cy in (-1, 0, 1):
        base = c[0] + (cy * c[1] + c[3] if cy else 0.0)
        lin = c[2] + cy * c[5] if cy else c[2]
        for cz in (-1, 0, 1):
            out.append(base + cz * lin + c[4] if cz else base)
    return out


def rebuild(c):
    out = []
    for cx in (-1, 0, 1):
        base = c[0] + cx * c[1] + c[4] if cx else c[0]
        liny = c[2] + cx * c[7] if cx else c[2]
        linz = c[3] + cx * c[8] if cx else c[3]
        out += rebuild_next([base, liny, linz, c[5], c[6], c[9]])
    return out


def first_kernel(rates_hbm, pop_hbm, pre_hbm, send_hbm, xa_ref, xb_ref, ya_ref, yb_ref, pre_ref, edge_ref, side_ref,
                 rates_ref, send_ref, sems):
    copies = [pltpu.make_async_copy(pre_hbm.at[:, p], pre_ref.at[:, p], sems.at[p]) for p in range(2)]
    for n, x in enumerate((0, XW - 1)):
        copies.append(pltpu.make_async_copy(pop_hbm.at[:, x], edge_ref.at[:, n], sems.at[2 + n]))
    copies.append(pltpu.make_async_copy(rates_hbm, rates_ref, sems.at[4]))
    for n, y in enumerate((0, YW - 1)):
        copies.append(pltpu.make_async_copy(pop_hbm.at[:, :, y, :], side_ref.at[n], sems.at[5 + n]))
    for copy in copies:
        copy.start()
    send_ref[LO_OWN:, :, :] = jnp.zeros((NDEV - LO_OWN, 8, Z), F32)
    for p in range(2):
        copies[p].wait()
        for q in range(4):
            c = precursor_coefficients([pre_ref[i, p, 8 * q:8 * q + 8, :] for i in range(27)])
            for k in range(10):
                send_ref[OWN + (2 * k + p) * 4 + q, :, :] = c[k]
                row = 2 * k + p
                if q == 3:
                    send_ref[LO_OWN + row // 8, row % 8:row % 8 + 1, :] = c[k][7:8, :]
                if q == 0:
                    send_ref[HI_OWN + row // 8, row % 8:row % 8 + 1, :] = c[k][0:1, :]
            if p == 0:
                c = next_coefficients(c)
                for k in range(6):
                    send_ref[NEXT + 4 * k + q, :, :] = c[k]
                    if q == 3:
                        send_ref[LO_NEXT, k:k + 1, :] = c[k][7:8, :]
                    if q == 0:
                        send_ref[HI_NEXT, k:k + 1, :] = c[k][0:1, :]
    sends = [pltpu.make_async_copy(send_ref.at[0:LO_OWN], send_hbm.at[0:LO_OWN], sems.at[7]),
             pltpu.make_async_copy(send_ref.at[LO_OWN:NDEV], send_hbm.at[LO_OWN:NDEV], sems.at[8])]
    sends[0].start()
    copies[4].wait()
    lane = lax.broadcasted_iota(jnp.int32, (8, Z), 1)
    odd_x = (lax.axis_index("gx") & 1) == 1
    for n, cx in enumerate((-1, 1)):
        copies[2 + n].wait()
        for q in range(4):
            rows = slice(8 * q, 8 * q + 8)
            post = z_stream(collide([edge_ref[i, n, rows, :] for i in range(27)], lambda i: rates_ref[i]), lane)
            for k in range(9):
                value = post[9 * (cx + 1) + k]
                if cx < 0:
                    xa_ref[k, rows, :] = value
                else:
                    keep = xa_ref[k, rows, :]
                    xa_ref[k, rows, :] = jnp.where(odd_x, keep, value)
                    xb_ref[k, rows, :] = jnp.where(odd_x, value, keep)
    odd_y = (lax.axis_index("gy") & 1) == 1
    for n, cy in enumerate((-1, 1)):
        copies[5 + n].wait()
        post = z_stream(collide([side_ref[n, i] for i in range(27)], lambda i: rates_ref[i]), lane)
        for cx in (-1, 0, 1):
            for cz in (-1, 0, 1):
                k = 3 * (cx + 1) + cz + 1
                value = post[slot(cx, cy, cz)]
                if cy < 0:
                    ya_ref[k, :, :] = value
                else:
                    keep = ya_ref[k, :, :]
                    ya_ref[k, :, :] = jnp.where(odd_y, keep, value)
                    yb_ref[k, :, :] = jnp.where(odd_y, value, keep)
                if cx:
                    at = 0 if cx < 0 else XW - 1
                    send_ref[CORNER + CORNERS.index((cx, cy)), cz + 1:cz + 2, :] = value[at:at + 1, :]
    sends[1].start()
    for copy in sends:
        copy.wait()


def before_exchange(rates, populations, precursor):
    return pl.pallas_call(
        first_kernel,
        in_specs=[HBM, HBM, HBM],
        out_specs=[HBM] + [VMEM] * 4,
        out_shape=[pltpu.HBM((NDEV, 8, Z), F32)] + [pltpu.VMEM((9, n, Z), F32) for n in (YW, YW, XW, XW)],
        scratch_shapes=[
            pltpu.VMEM((27, 2, YW, Z), F32),
            pltpu.VMEM((27, 2, YW, Z), F32),
            pltpu.VMEM((2, 27, XW, Z), F32),
            pltpu.SMEM((27,), F32),
            pltpu.VMEM((NDEV, 8, Z), F32),
            pltpu.SemaphoreType.DMA((9,)),
        ],
        name="before_exchange",
        compiler_params=pltpu.CompilerParams(vmem_limit_bytes=4 << 20),
    )(far(rates), far(populations), far(precursor))


def collide_kernel(rates_ref, cols_ref, turb_ref, pop_hbm, out_hbm, w_ref, disc_ref,
                   pop_ref, out_ref, in_sems, out_sems):
    def copy_in(x):
        return pltpu.make_async_copy(pop_hbm.at[:, x], pop_ref.at[:, x], in_sems.at[x])

    def copy_out(x):
        return pltpu.make_async_copy(out_ref.at[:, x], out_hbm.at[:, x], out_sems.at[x])

    for x in range(XW):
        copy_in(x).start()
    gx = lax.axis_index("gx")
    gy = lax.axis_index("gy")
    rows = lax.broadcasted_iota(jnp.int32, (W_ROWS, SLOTS), 0)
    lo = rows - 320
    main = rows < 320
    xx = jnp.where(main, rows >> 5, jnp.where(lo < 16, lo, lo - 16))
    yy = jnp.where(main, rows & 31, jnp.where(lo < 16, -1, YW))
    col = ((gx * XW + xx - 1) & (NX_ALL - 1)) * NY_ALL + ((gy * YW + yy) & (NY_ALL - 1))
    valid = main | ((lo & 15) < 10)
    hit = ((col == cols_ref[...]) & valid & (lo < 32)) | (lo >= 32)
    owner = lax.broadcasted_iota(jnp.int32, (128, SLOTS), 0) == turb_ref[...]
    w_ref[...] = lax.dot_general(
        jnp.where(hit, 1.0, 0.0).astype(jnp.bfloat16),
        jnp.where(owner, 1.0, 0.0).astype(jnp.bfloat16),
        (((1,), (1,)), ((), ())), preferred_element_type=F32)
    disc_ref[...] = jnp.zeros_like(disc_ref)
    lane = lax.broadcasted_iota(jnp.int32, (8, Z), 1)
    profile = profile_row()

    def plane(x, carry):
        copy_in(x).wait()
        for q in range(4):
            rows = slice(8 * q, 8 * q + 8)
            m = forward([pop_ref[i, x, rows, :] for i in range(27)])
            sums = jnp.sum(m[9] / m[0] * profile, axis=1, keepdims=True)
            disc_ref[...] += sums * w_ref[pl.ds(pl.multiple_of((x + 1) * YW + 8 * q, 8), 8), :]
            post = z_stream(relax(m, lambda i: rates_ref[i]), lane)
            for i in range(27):
                out_ref[i, x, rows, :] = post[i]
        copy_out(x).start()
        return carry

    lax.fori_loop(0, XW, plane, 0)
    for x in range(XW):
        copy_out(x).wait()


def collision(rates, cols, turb, populations):
    shapes = ((27, XW, YW, Z), (W_ROWS, 128), (8, 128))
    return pl.pallas_call(
        collide_kernel,
        in_specs=[SMEM, VMEM, VMEM, HBM],
        out_specs=[HBM] + [VMEM] * (len(shapes) - 1),
        out_shape=[pltpu.HBM(shapes[0], F32)] + [pltpu.VMEM(shape, F32) for shape in shapes[1:]],
        scratch_shapes=[
            pltpu.VMEM(shapes[0], F32),
            pltpu.VMEM(shapes[0], F32),
            pltpu.SemaphoreType.DMA((XW,)),
            pltpu.SemaphoreType.DMA((XW,)),
        ],
        name="collision",
        compiler_params=pltpu.CompilerParams(vmem_limit_bytes=12 << 20),
    )(rates, cols, turb, far(populations))


def route_kernel(pairing_ref, got_ref, disc_ref, send_hbm, send_ref, sems):
    me = lax.axis_index("gx") * GY + lax.axis_index("gy")
    is_next = ((me >= NEXT) & (me < LO_OWN)) | (me == LO_NEXT) | (me == HI_NEXT)
    corner = me - CORNER
    is_corner = (corner >= 0) & (corner < 4)
    low = ((me >= LO_OWN) & (me < HI_OWN)) | (me == LO_NEXT)
    high = ((me >= HI_OWN) & (me < LO_NEXT)) | (me == HI_NEXT)
    from_x = jnp.where(corner < 2, 1, -1)
    from_y = jnp.where(is_corner, jnp.where((corner & 1) == 0, 1, -1), jnp.where(low, -1, jnp.where(high, 1, 0)))
    ahead = jnp.where(is_next, 1, 0)
    lanes = [(t + from_y) & (GY - 1) for t in range(GY)]
    part = jnp.sum(disc_ref[...], axis=0, keepdims=True)
    copies = []
    for d in range(GX):
        tile = pairing_ref[(d + ahead) & (GX - 1)]
        tile = jnp.where(is_corner, (d + from_x) & (GX - 1), tile) * GY
        for t in range(GY):
            at = (d * GY + t) * PIECE
            send_ref[at:at + 8, :] = got_ref[tile + lanes[t], :, :]
            send_ref[at + 8:at + 9, :] = part
        if d % 8 == 7:
            rows = slice((d - 7) * GY * PIECE, (d + 1) * GY * PIECE)
            copies.append(pltpu.make_async_copy(send_ref.at[rows], send_hbm.at[rows], sems.at[d // 8]))
            copies[-1].start()
    for copy in copies:
        copy.wait()


def route(pairing, got, disc):
    return pl.pallas_call(
        route_kernel,
        in_specs=[SMEM, VMEM, VMEM],
        out_specs=HBM,
        out_shape=pltpu.HBM((NDEV * PIECE, Z), F32),
        scratch_shapes=[pltpu.VMEM((NDEV * PIECE, Z), F32), pltpu.SemaphoreType.DMA((GX // 8,))],
        name="route",
        compiler_params=pltpu.CompilerParams(vmem_limit_bytes=3 << 20),
    )(pairing, near(got), near(disc))


def changed(used_ref, p):
    return (p == 0) | (p == 1) | (p == XW) | (used_ref[p + 1] > 0)


def late(used_ref, x, cx):
    if cx == 0:
        return x < len(BLEND)
    return changed(used_ref, x) | changed(used_ref, x - cx)


def stream_group(rp, low_scr, high_scr, out_scr, x, cx):
    lane = lax.broadcasted_iota(jnp.int32, (YW, Z), 1)
    row = lax.broadcasted_iota(jnp.int32, (YW, Z), 0)
    at = x + 1 - cx
    for cy in (-1, 0, 1):
        for cz in (-1, 0, 1):
            i = slot(cx, cy, cz)
            k = 3 * (cx + 1) + cz + 1
            value = rp[i, at, 8 - cy:40 - cy, :]
            if cy == 1:
                value = jnp.where(row == 0, low_scr[k, pl.ds(at, 1), :], value)
            elif cy == -1:
                value = jnp.where(row == YW - 1, high_scr[k, pl.ds(at, 1), :], value)
            if cz != 0 and (cx != 0 or cy != 0):
                value = jnp.where(lane == (0 if cz == 1 else Z - 1), rp[i, x + 1, 8:40, :], value)
            out_scr[i, x, :, :] = value


def group_copy(out_scr, out_hbm, sems, x, cx):
    group = slice(9 * (cx + 1), 9 * (cx + 2))
    return pltpu.make_async_copy(out_scr.at[group, x], out_hbm.at[group, x], sems.at[x, cx + 1])


HELD = (0, 1, 2, XW - 1)


def early_kernel(w_ref, r_hbm, xa_ref, xb_ref, ya_ref, yb_ref, out_hbm, xm_ref, xp_ref, ym_ref, yp_ref, held_ref,
                 used_ref, rp, low_scr, high_scr, out_scr, in_sems, held_sems, sems):
    first = len(BLEND)

    def copy_in(x):
        return pltpu.make_async_copy(r_hbm.at[:, x], rp.at[:, x + 1, 8:40, :], in_sems.at[x])

    for x in range(first, XW):
        copy_in(x).start()
    holds = [pltpu.make_async_copy(r_hbm.at[:, x], held_ref.at[:, n], held_sems.at[n]) for n, x in enumerate(HELD)]
    for copy in holds:
        copy.start()
    for p in range(XW + 2):
        beside = jnp.max(w_ref[320 + p:321 + p, :] + w_ref[336 + p:337 + p, :])
        used_ref[p] = jnp.where(jnp.max(w_ref[YW * p:YW * p + YW, :]) + beside > 0.0, 1, 0)
    odd_x = (lax.axis_index("gx") & 1) == 1
    odd_y = (lax.axis_index("gy") & 1) == 1
    for k in range(9):
        xm_ref[k] = jnp.where(odd_x, xb_ref[k], xa_ref[k])
        xp_ref[k] = jnp.where(odd_x, xa_ref[k], xb_ref[k])
        high = jnp.where(odd_y, yb_ref[k], ya_ref[k])
        low = jnp.where(odd_y, ya_ref[k], yb_ref[k])
        ym_ref[k] = high
        yp_ref[k] = low
        high_scr[k, 1:9, :] = high
        low_scr[k, 1:9, :] = low
    copy_in(first).wait()

    def plane(x, carry):
        @pl.when(x + 1 < XW)
        def _():
            copy_in(jnp.minimum(x + 1, XW - 1)).wait()

        for cx in (-1, 0, 1):
            @pl.when(jnp.logical_not(late(used_ref, x, cx)))
            def _():
                stream_group(rp, low_scr, high_scr, out_scr, x, cx)
                group_copy(out_scr, out_hbm, sems, x, cx).start()
        return carry

    lax.fori_loop(first, XW, plane, 0)
    for copy in holds:
        copy.wait()
    for x in range(first, XW):
        for cx in (-1, 0, 1):
            @pl.when(jnp.logical_not(late(used_ref, x, cx)))
            def _():
                group_copy(out_scr, out_hbm, sems, x, cx).wait()


def stream_early(w, r, *borders):
    return pl.pallas_call(
        early_kernel,
        in_specs=[VMEM, HBM] + [VMEM] * 4,
        out_specs=[HBM] + [VMEM] * 5 + [SMEM],
        out_shape=[pltpu.HBM((27, XW, YW, Z), F32)] + [pltpu.VMEM(b.shape, F32) for b in borders]
        + [pltpu.VMEM((27, len(HELD), YW, Z), F32), jax.ShapeDtypeStruct((XW + 2,), jnp.int32)],
        scratch_shapes=[
            pltpu.VMEM((27, XW + 2, 48, Z), F32),
            pltpu.VMEM((9, 16, Z), F32),
            pltpu.VMEM((9, 16, Z), F32),
            pltpu.VMEM((27, XW, YW, Z), F32),
            pltpu.SemaphoreType.DMA((XW,)),
            pltpu.SemaphoreType.DMA((len(HELD),)),
            pltpu.SemaphoreType.DMA((XW, 3)),
        ],
        name="stream_early",
        compiler_params=pltpu.CompilerParams(vmem_limit_bytes=16 << 20),
        cost_estimate=pl.CostEstimate(flops=7 * 10**9, transcendentals=0, bytes_accessed=10**6),
    )(near(w), far(r), *[near(b) for b in borders])


def last_kernel(got_ref, w_ref, loading_ref, r_hbm, xm_ref, xp_ref, ym_ref, yp_ref, held_ref, used_ref, early_hbm,
                out_hbm, speed_ref,
                rp, force, load_scr, lo_scr, hi_scr, yp_scr, ym_scr, r_ref, out_scr, in_sems, sems):
    def copy_in(x):
        return pltpu.make_async_copy(r_hbm.at[:, x], r_ref.at[:, x], in_sems.at[x])

    def needed(p):
        return changed(used_ref, p - 1) | changed(used_ref, p) | changed(used_ref, p + 1)

    for x in range(3, XW - 1):
        @pl.when(needed(x))
        def _():
            copy_in(x).start()

    lane = lax.broadcasted_iota(jnp.int32, (8, Z), 1)
    profile = profile_row()
    up = jnp.where(lane == 0, -profile, pltpu.roll(profile, 1, 1))
    down = jnp.where(lane == Z - 1, -profile, pltpu.roll(profile, Z - 1, 1))
    along = (3.0 * down, 3.0 * profile, 3.0 * up)

    def got(tile, a=0, b=8):
        return got_ref[PIECE * tile + a:PIECE * tile + b, :]

    def pushes(f):
        return [f * a for a in along]

    def push(value, i, fs):
        cx = i // 9 - 1
        return value if cx == 0 else (value + fs[i % 3] if cx > 0 else value - fs[i % 3])

    load_scr[...] = jnp.zeros_like(load_scr)
    load_scr[0:1, 0:TURBINES] = loading_ref[...]
    counts = w_ref[352:360, :]
    totals = jnp.broadcast_to(jnp.sum(got_ref[pl.ds(8, NDEV, stride=PIECE), :], axis=0, keepdims=True), (8, 128))
    k = lax.broadcasted_iota(jnp.int32, (8, 128), 1)
    speed = jnp.where(k < TURBINES, totals / (jnp.where(k < TURBINES, counts, 1.0) * PROFILE_SUM), 0.0)
    speed_ref[...] = speed[0:1, 0:TURBINES]
    thrust = (0.5 * jnp.broadcast_to(load_scr[0:1, :], (8, 128))) * speed * jnp.abs(speed)
    force[...] = -lax.dot_general(
        w_ref[0:352, :] * thrust[0:1, :], jnp.ones((128, Z), F32), (((1,), (0,)), ((), ())),
        precision=lax.Precision.HIGHEST, preferred_element_type=F32)
    for scr, tile, nxt, halo, frow, cy, out in (
        (lo_scr, LO_OWN, LO_NEXT, yp_ref, 320, 1, yp_scr),
        (hi_scr, HI_OWN, HI_NEXT, ym_ref, 336, -1, ym_scr),
    ):
        scr[...] = jnp.zeros_like(scr)
        for c in range(10):
            r = 2 * c
            scr[c, 0:2, :] = got(tile + r // 8, r % 8, r % 8 + 2)
        built = rebuild([scr[c] for c in range(10)])
        ahead = rebuild_next([got(nxt, c, c + 1) for c in range(6)])
        row = lax.broadcasted_iota(jnp.int32, (8, Z), 0)
        blend = jnp.where(row == 0, BLEND[0], jnp.where(row == 1, BLEND[1], 0.0))
        fs = pushes(force[frow + 1:frow + 9, :])
        for cx in (-1, 0, 1):
            for cz in (-1, 0, 1):
                k = 3 * (cx + 1) + cz + 1
                i = slot(cx, cy, cz)
                b = built[i]
                b = b if cz == 0 else pltpu.roll(b, cz % Z, 1)
                out[k, 1:9, :] = (1.0 - blend) * push(halo[k], i, fs) + blend * b
        for cz in (-1, 0, 1):
            n = CORNERS.index((1, cy))
            out[6 + cz + 1, 0:1, :] = got(CORNER + n, cz + 1, cz + 2) + (
                force[frow:frow + 1, :] * along[cz + 1][0:1, :])
            n = CORNERS.index((-1, cy))
            value = got(CORNER + n, cz + 1, cz + 2) - force[frow + 9:frow + 10, :] * along[cz + 1][0:1, :]
            b = ahead[3 * (cy + 1) + cz + 1]
            b = b if cz == 0 else pltpu.roll(jnp.broadcast_to(b, (8, Z)), cz % Z, 1)[0:1, :]
            out[cz + 1, 9:10, :] = (1.0 - BLEND[0]) * value + BLEND[0] * b

    for q in range(4):
        rows = slice(8 * q, 8 * q + 8)
        into = slice(8 * q + 8, 8 * q + 16)
        fs = pushes(force[rows, :])
        for k in range(9):
            rp[18 + k, 0, into, :] = push(xp_ref[k, rows, :], 18 + k, fs)
        for p in range(2):
            built = z_stream(rebuild([got(OWN + (2 * k + p) * 4 + q) for k in range(10)]), lane)
            fs = pushes(force[YW * (p + 1) + 8 * q:YW * (p + 1) + 8 * q + 8, :])
            for i in range(27):
                rp[i, p + 1, into, :] = (1.0 - BLEND[p]) * push(held_ref[i, p, rows, :], i, fs) + BLEND[p] * built[i]
        for n in range(2, len(HELD)):
            x = HELD[n]
            fs = pushes(force[YW * (x + 1) + 8 * q:YW * (x + 1) + 8 * q + 8, :])
            for i in range(27):
                rp[i, x + 1, into, :] = push(held_ref[i, n, rows, :], i, fs)
        fs = pushes(force[YW * (XW + 1) + 8 * q:YW * (XW + 1) + 8 * q + 8, :])
        built = rebuild_next([got(NEXT + 4 * k + q) for k in range(6)])
        for k in range(9):
            cz = k % 3 - 1
            b = built[k] if cz == 0 else pltpu.roll(built[k], cz % Z, 1)
            rp[k, XW + 1, into, :] = (1.0 - BLEND[0]) * push(xm_ref[k, rows, :], k, fs) + BLEND[0] * b

    for x in range(3, XW - 1):
        @pl.when(needed(x))
        def _():
            copy_in(x).wait()
            for q in range(4):
                rows = slice(8 * q, 8 * q + 8)
                into = slice(8 * q + 8, 8 * q + 16)
                fs = pushes(force[YW * (x + 1) + 8 * q:YW * (x + 1) + 8 * q + 8, :])
                for i in range(27):
                    rp[i, x + 1, into, :] = push(r_ref[i, x, rows, :], i, fs)

    def plane(x, carry):
        for cx in (-1, 0, 1):
            @pl.when(late(used_ref, x, cx))
            def _():
                stream_group(rp, yp_scr, ym_scr, out_scr, x, cx)
                group_copy(out_scr, out_hbm, sems, x, cx).start()
        return carry

    lax.fori_loop(0, XW, plane, 0)
    for x in range(XW):
        for cx in (-1, 0, 1):
            @pl.when(late(used_ref, x, cx))
            def _():
                group_copy(out_scr, out_hbm, sems, x, cx).wait()


def after_exchange(*args):
    return pl.pallas_call(
        last_kernel,
        in_specs=[HBM if n in (3, 10) else SMEM if n == 9 else VMEM for n in range(len(args))],
        input_output_aliases={10: 0},
        out_specs=[HBM, VMEM],
        out_shape=[pltpu.HBM((27, XW, YW, Z), F32), jax.ShapeDtypeStruct((1, TURBINES), F32)],
        scratch_shapes=[
            pltpu.VMEM((27, XW + 2, 48, Z), F32),
            pltpu.VMEM((352, Z), F32),
            pltpu.VMEM((8, 128), F32),
            pltpu.VMEM((10, 8, Z), F32),
            pltpu.VMEM((10, 8, Z), F32),
            pltpu.VMEM((9, 16, Z), F32),
            pltpu.VMEM((9, 16, Z), F32),
            pltpu.VMEM((27, XW, YW, Z), F32),
            pltpu.VMEM((27, XW, YW, Z), F32),
            pltpu.SemaphoreType.DMA((XW,)),
            pltpu.SemaphoreType.DMA((XW, 3)),
        ],
        name="after_exchange",
        compiler_params=pltpu.CompilerParams(vmem_limit_bytes=24 << 20),
    )(*[far(a) if n in (3, 10) else a if n == 9 else near(a) for n, a in enumerate(args)])


def body(populations, precursor, pairing, rates, loading, disc_cols, disc_turb):
    both = ("gx", "gy")
    inner = lambda n: [(i, i ^ 1) for i in range(n)]
    outer = lambda n: [(i, (i + (1 if i % 2 else -1)) % n) for i in range(n)]
    send, xa, xb, ya, yb = before_exchange(rates, populations, precursor)
    got = lax.all_to_all(send, both, 0, 0, tiled=True)
    r, w, disc = collision(
        rates, disc_cols.reshape(1, SLOTS), disc_turb.reshape(1, SLOTS), populations)
    xb = lax.ppermute(xb, "gx", outer(GX))
    xa = lax.ppermute(xa, "gx", inner(GX))
    yb = lax.ppermute(yb, "gy", outer(GY))
    ya = lax.ppermute(ya, "gy", inner(GY))
    send = route(pairing, got, disc).reshape(NDEV, PIECE, 1, Z)
    got = lax.all_to_all(send, both, 0, 0, tiled=True).reshape(NDEV * PIECE, Z)
    read, *rest = stream_early(w, r, xa, xb, ya, yb)
    read, speed = after_exchange(got, w, loading.reshape(1, TURBINES), r, *rest, read)
    return read, speed.reshape(TURBINES)


def solution(mesh):
    in_specs = (P(None, "gx", "gy", None), P(None, "gx", "gy", None), P(), P(), P(), P(), P())
    out_specs = (P(None, "gx", "gy", None), P())
    return jax.shard_map(body, mesh=mesh, in_specs=in_specs, out_specs=out_specs, check_vma=False)
```

```python
import jax
import jax.numpy as jnp
import numpy as np
from jax import lax
from jax.experimental import pallas as pl
from jax.experimental.pallas import tpu as pltpu
from jax.sharding import PartitionSpec as P

GX, GY = 32, 4
NDEV = GX * GY
XW, YW, Z = 8, 32, 128
NY_ALL, NX_ALL = 128, 256
SLOTS = 512
TURBINES = 32
F32 = jnp.float32

OWN, NEXT, LO_OWN, HI_OWN, LO_NEXT, HI_NEXT, CORNER = 0, 80, 104, 107, 110, 111, 112
PIECE = 9
CORNERS = ((-1, -1), (-1, 1), (1, -1), (1, 1))
W_ROWS = 360
BLEND = (0.5, 0.25)

PROFILE_SUM = float(np.sum(np.exp(-np.square((np.arange(Z) - Z / 3.0) / (Z / 6.0)))))


HBM = pl.BlockSpec(memory_space=pltpu.HBM)
SMEM = pl.BlockSpec(memory_space=pltpu.SMEM)
VMEM = pl.BlockSpec(memory_space=pltpu.VMEM)


def near(array):
    return pltpu.with_memory_space_constraint(array, pltpu.VMEM)


def far(array):
    return pltpu.with_memory_space_constraint(array, pltpu.HBM)


def slot(cx, cy, cz):
    return 9 * (cx + 1) + 3 * (cy + 1) + (cz + 1)


def profile_row():
    heights = lax.broadcasted_iota(jnp.int32, (8, Z), 1).astype(F32)
    return jnp.exp(-jnp.square((heights - Z / 3.0) * (6.0 / Z)))


def forward(g):
    for stride in (1, 3, 9):
        out = list(g)
        for i in range(27):
            if (i // stride) % 3 == 0:
                a, b, c = g[i], g[i + stride], g[i + 2 * stride]
                s = c + a
                out[i] = s + 4.0 * b
                out[i + stride] = c - a
                out[i + 2 * stride] = s
        g = out
    return g


def backward(m):
    for stride in (9, 3, 1):
        out = list(m)
        for i in range(27):
            if (i // stride) % 3 == 0:
                a, b, c = m[i], m[i + stride], m[i + 2 * stride]
                out[i] = c - b
                out[i + stride] = 0.5 * (a - c)
                out[i + 2 * stride] = c + b
        m = out
    return m


def collide(g, rates):
    return relax(forward(g), rates)


def relax(m, rates):
    density = m[0] * (1.0 / 216.0)
    inv = 1.0 / m[0]
    u = (m[9] * inv, m[3] * inv, m[1] * inv)
    j = (m[9] * (1.0 / 216.0), m[3] * (1.0 / 216.0), m[1] * (1.0 / 216.0))
    ju = {}
    for a in range(3):
        for b in range(a, 3):
            ju[(a, b)] = j[a] * u[b]
    out = []
    for i in range(27):
        order = (i // 9, i // 3 % 3, i % 3)
        ones = [d for d in range(3) if order[d] == 1]
        twos = [d for d in range(3) if order[d] == 2]
        if i in (0, 1, 3, 9):
            out.append(m[i] * 0.125)
            continue
        r = rates(i)
        keep = m[i] * ((1.0 - r) * 0.125)
        if len(ones) == 3:
            out.append(keep)
            continue
        scale = r * (27.0 / 3.0 ** len(twos))
        if len(ones) == 0:
            eq = ju[(twos[0], twos[0])]
            for d in twos[1:]:
                eq = eq + ju[(d, d)]
            eq = density + 3.0 * eq
        elif len(ones) == 1:
            eq = j[ones[0]]
        else:
            eq = ju[(ones[0], ones[1])]
        out.append(keep + eq * scale)
    return backward(out)


def z_stream(p, lane):
    out = []
    for i in range(27):
        cz = i % 3 - 1
        if cz == 0:
            out.append(p[i])
        elif cz == 1:
            out.append(jnp.where(lane == 0, p[26 - i], pltpu.roll(p[i], 1, 1)))
        else:
            out.append(jnp.where(lane == Z - 1, p[26 - i], pltpu.roll(p[i], Z - 1, 1)))
    return out


def precursor_coefficients(g):
    m = forward(g)
    rho, jx, jy, jz = m[0], m[9], m[3], m[1]
    xx, yy, zz, xy, xz, yz = m[18], m[6], m[2], m[12], m[10], m[4]
    third = rho * (1.0 / 3.0)
    pxx, pyy, pzz = xx - third, yy - third, zz - third
    s = 1.0 / 216.0
    k0 = (rho - 1.5 * (pxx + pyy + pzz)) * s
    return [k0, jx * (3 * s), jy * (3 * s), jz * (3 * s), pxx * (4.5 * s), pyy * (4.5 * s), pzz * (4.5 * s),
            xy * (9 * s), xz * (9 * s), yz * (9 * s)]


def next_coefficients(c):
    return [c[0] - c[1] + c[4], c[2] - c[7], c[3] - c[8], c[5], c[6], c[9]]


def rebuild_next(c):
    out = []
    for cy in (-1, 0, 1):
        base = c[0] + (cy * c[1] + c[3] if cy else 0.0)
        lin = c[2] + cy * c[5] if cy else c[2]
        for cz in (-1, 0, 1):
            out.append(base + cz * lin + c[4] if cz else base)
    return out


def rebuild(c):
    out = []
    for cx in (-1, 0, 1):
        base = c[0] + cx * c[1] + c[4] if cx else c[0]
        liny = c[2] + cx * c[7] if cx else c[2]
        linz = c[3] + cx * c[8] if cx else c[3]
        out += rebuild_next([base, liny, linz, c[5], c[6], c[9]])
    return out


def first_kernel(rates_hbm, pop_hbm, pre_hbm, send_hbm, xa_ref, xb_ref, ya_ref, yb_ref, pre_ref, edge_ref, side_ref,
                 rates_ref, send_ref, sems):
    copies = [pltpu.make_async_copy(pre_hbm.at[:, p], pre_ref.at[:, p], sems.at[p]) for p in range(2)]
    for n, x in enumerate((0, XW - 1)):
        copies.append(pltpu.make_async_copy(pop_hbm.at[:, x], edge_ref.at[:, n], sems.at[2 + n]))
    copies.append(pltpu.make_async_copy(rates_hbm, rates_ref, sems.at[4]))
    for n, y in enumerate((0, YW - 1)):
        copies.append(pltpu.make_async_copy(pop_hbm.at[:, :, y, :], side_ref.at[n], sems.at[5 + n]))
    for copy in copies:
        copy.start()
    send_ref[LO_OWN:, :, :] = jnp.zeros((NDEV - LO_OWN, 8, Z), F32)
    for p in range(2):
        copies[p].wait()
        for q in range(4):
            c = precursor_coefficients([pre_ref[i, p, 8 * q:8 * q + 8, :] for i in range(27)])
            for k in range(10):
                send_ref[OWN + (2 * k + p) * 4 + q, :, :] = c[k]
                row = 2 * k + p
                if q == 3:
                    send_ref[LO_OWN + row // 8, row % 8:row % 8 + 1, :] = c[k][7:8, :]
                if q == 0:
                    send_ref[HI_OWN + row // 8, row % 8:row % 8 + 1, :] = c[k][0:1, :]
            if p == 0:
                c = next_coefficients(c)
                for k in range(6):
                    send_ref[NEXT + 4 * k + q, :, :] = c[k]
                    if q == 3:
                        send_ref[LO_NEXT, k:k + 1, :] = c[k][7:8, :]
                    if q == 0:
                        send_ref[HI_NEXT, k:k + 1, :] = c[k][0:1, :]
    sends = [pltpu.make_async_copy(send_ref.at[0:LO_OWN], send_hbm.at[0:LO_OWN], sems.at[7]),
             pltpu.make_async_copy(send_ref.at[LO_OWN:NDEV], send_hbm.at[LO_OWN:NDEV], sems.at[8])]
    sends[0].start()
    copies[4].wait()
    lane = lax.broadcasted_iota(jnp.int32, (8, Z), 1)
    odd_x = (lax.axis_index("gx") & 1) == 1
    for n, cx in enumerate((-1, 1)):
        copies[2 + n].wait()
        for q in range(4):
            rows = slice(8 * q, 8 * q + 8)
            post = z_stream(collide([edge_ref[i, n, rows, :] for i in range(27)], lambda i: rates_ref[i]), lane)
            for k in range(9):
                value = post[9 * (cx + 1) + k]
                if cx < 0:
                    xa_ref[k, rows, :] = value
                else:
                    keep = xa_ref[k, rows, :]
                    xa_ref[k, rows, :] = jnp.where(odd_x, keep, value)
                    xb_ref[k, rows, :] = jnp.where(odd_x, value, keep)
    odd_y = (lax.axis_index("gy") & 1) == 1
    for n, cy in enumerate((-1, 1)):
        copies[5 + n].wait()
        post = z_stream(collide([side_ref[n, i] for i in range(27)], lambda i: rates_ref[i]), lane)
        for cx in (-1, 0, 1):
            for cz in (-1, 0, 1):
                k = 3 * (cx + 1) + cz + 1
                value = post[slot(cx, cy, cz)]
                if cy < 0:
                    ya_ref[k, :, :] = value
                else:
                    keep = ya_ref[k, :, :]
                    ya_ref[k, :, :] = jnp.where(odd_y, keep, value)
                    yb_ref[k, :, :] = jnp.where(odd_y, value, keep)
                if cx:
                    at = 0 if cx < 0 else XW - 1
                    send_ref[CORNER + CORNERS.index((cx, cy)), cz + 1:cz + 2, :] = value[at:at + 1, :]
    sends[1].start()
    for copy in sends:
        copy.wait()


def before_exchange(rates, populations, precursor):
    return pl.pallas_call(
        first_kernel,
        in_specs=[HBM, HBM, HBM],
        out_specs=[HBM] + [VMEM] * 4,
        out_shape=[pltpu.HBM((NDEV, 8, Z), F32)] + [pltpu.VMEM((9, n, Z), F32) for n in (YW, YW, XW, XW)],
        scratch_shapes=[
            pltpu.VMEM((27, 2, YW, Z), F32),
            pltpu.VMEM((27, 2, YW, Z), F32),
            pltpu.VMEM((2, 27, XW, Z), F32),
            pltpu.SMEM((27,), F32),
            pltpu.VMEM((NDEV, 8, Z), F32),
            pltpu.SemaphoreType.DMA((9,)),
        ],
        name="before_exchange",
        compiler_params=pltpu.CompilerParams(vmem_limit_bytes=4 << 20),
    )(far(rates), far(populations), far(precursor))


def sums_kernel(cols_ref, turb_ref, pop_hbm, w_ref, disc_ref, pop_ref, in_sems):
    def copy_in(x):
        return pltpu.make_async_copy(pop_hbm.at[:, x], pop_ref.at[:, x], in_sems.at[x])

    for x in range(XW):
        copy_in(x).start()
    gx = lax.axis_index("gx")
    gy = lax.axis_index("gy")
    rows = lax.broadcasted_iota(jnp.int32, (W_ROWS, SLOTS), 0)
    lo = rows - 320
    main = rows < 320
    xx = jnp.where(main, rows >> 5, jnp.where(lo < 16, lo, lo - 16))
    yy = jnp.where(main, rows & 31, jnp.where(lo < 16, -1, YW))
    col = ((gx * XW + xx - 1) & (NX_ALL - 1)) * NY_ALL + ((gy * YW + yy) & (NY_ALL - 1))
    valid = main | ((lo & 15) < 10)
    hit = ((col == cols_ref[...]) & valid & (lo < 32)) | (lo >= 32)
    owner = lax.broadcasted_iota(jnp.int32, (128, SLOTS), 0) == turb_ref[...]
    w_ref[...] = lax.dot_general(
        jnp.where(hit, 1.0, 0.0).astype(jnp.bfloat16),
        jnp.where(owner, 1.0, 0.0).astype(jnp.bfloat16),
        (((1,), (1,)), ((), ())), preferred_element_type=F32)
    disc_ref[...] = jnp.zeros_like(disc_ref)
    profile = profile_row()

    def plane(x, carry):
        copy_in(x).wait()
        for q in range(4):
            rows = slice(8 * q, 8 * q + 8)
            part = []
            for cx in range(3):
                total = None
                for cy in range(3):
                    b = 9 * cx + 3 * cy
                    t = pop_ref[b, x, rows, :] + pop_ref[b + 2, x, rows, :] + 4.0 * pop_ref[b + 1, x, rows, :]
                    t = 4.0 * t if cy == 1 else t
                    total = t if total is None else total + t
                part.append(total)
            ends = part[0] + part[2]
            ux = (part[2] - part[0]) / (ends + 4.0 * part[1])
            sums = jnp.sum(ux * profile, axis=1, keepdims=True)
            disc_ref[...] += sums * w_ref[pl.ds(pl.multiple_of((x + 1) * YW + 8 * q, 8), 8), :]
        return carry

    lax.fori_loop(0, XW, plane, 0)


def disc_sums(cols, turb, populations):
    return pl.pallas_call(
        sums_kernel,
        in_specs=[VMEM, VMEM, HBM],
        out_specs=[VMEM] * 2,
        out_shape=[pltpu.VMEM((W_ROWS, 128), F32), pltpu.VMEM((8, 128), F32)],
        scratch_shapes=[pltpu.VMEM((27, XW, YW, Z), F32), pltpu.SemaphoreType.DMA((XW,))],
        name="disc_sums",
        compiler_params=pltpu.CompilerParams(vmem_limit_bytes=8 << 20),
    )(cols, turb, far(populations))


def route_kernel(pairing_ref, got_ref, disc_ref, send_hbm, send_ref, sems):
    me = lax.axis_index("gx") * GY + lax.axis_index("gy")
    is_next = ((me >= NEXT) & (me < LO_OWN)) | (me == LO_NEXT) | (me == HI_NEXT)
    corner = me - CORNER
    is_corner = (corner >= 0) & (corner < 4)
    low = ((me >= LO_OWN) & (me < HI_OWN)) | (me == LO_NEXT)
    high = ((me >= HI_OWN) & (me < LO_NEXT)) | (me == HI_NEXT)
    from_x = jnp.where(corner < 2, 1, -1)
    from_y = jnp.where(is_corner, jnp.where((corner & 1) == 0, 1, -1), jnp.where(low, -1, jnp.where(high, 1, 0)))
    ahead = jnp.where(is_next, 1, 0)
    lanes = [(t + from_y) & (GY - 1) for t in range(GY)]
    part = jnp.sum(disc_ref[...], axis=0, keepdims=True)
    copies = []
    for d in range(GX):
        tile = pairing_ref[(d + ahead) & (GX - 1)]
        tile = jnp.where(is_corner, (d + from_x) & (GX - 1), tile) * GY
        for t in range(GY):
            at = (d * GY + t) * PIECE
            send_ref[at:at + 8, :] = got_ref[tile + lanes[t], :, :]
            send_ref[at + 8:at + 9, :] = part
        if d % 8 == 7:
            rows = slice((d - 7) * GY * PIECE, (d + 1) * GY * PIECE)
            copies.append(pltpu.make_async_copy(send_ref.at[rows], send_hbm.at[rows], sems.at[d // 8]))
            copies[-1].start()
    for copy in copies:
        copy.wait()


def route(pairing, got, disc):
    return pl.pallas_call(
        route_kernel,
        in_specs=[SMEM, VMEM, VMEM],
        out_specs=HBM,
        out_shape=pltpu.HBM((NDEV * PIECE, Z), F32),
        scratch_shapes=[pltpu.VMEM((NDEV * PIECE, Z), F32), pltpu.SemaphoreType.DMA((GX // 8,))],
        name="route",
        compiler_params=pltpu.CompilerParams(vmem_limit_bytes=3 << 20),
    )(pairing, near(got), near(disc))


def changed(used_ref, p):
    return (p == 0) | (p == 1) | (p == XW) | (used_ref[p + 1] > 0)


def late(used_ref, x, cx):
    if cx == 0:
        return x < len(BLEND)
    return changed(used_ref, x) | changed(used_ref, x - cx)


def stream_group(rp, low_scr, high_scr, out_scr, x, cx):
    lane = lax.broadcasted_iota(jnp.int32, (YW, Z), 1)
    row = lax.broadcasted_iota(jnp.int32, (YW, Z), 0)
    at = x + 1 - cx
    for cy in (-1, 0, 1):
        for cz in (-1, 0, 1):
            i = slot(cx, cy, cz)
            k = 3 * (cx + 1) + cz + 1
            value = rp[i, at, 8 - cy:40 - cy, :]
            if cy == 1:
                value = jnp.where(row == 0, low_scr[k, pl.ds(at, 1), :], value)
            elif cy == -1:
                value = jnp.where(row == YW - 1, high_scr[k, pl.ds(at, 1), :], value)
            if cz != 0 and (cx != 0 or cy != 0):
                value = jnp.where(lane == (0 if cz == 1 else Z - 1), rp[i, x + 1, 8:40, :], value)
            out_scr[i, x, :, :] = value


def group_copy(out_scr, out_hbm, sems, x, cx):
    group = slice(9 * (cx + 1), 9 * (cx + 2))
    return pltpu.make_async_copy(out_scr.at[group, x], out_hbm.at[group, x], sems.at[x, cx + 1])


HELD = (0, 1, 2, XW - 1)


def early_kernel(rates_ref, pop_hbm, w_ref, xa_ref, xb_ref, ya_ref, yb_ref, out_hbm, r_hbm, xm_ref, xp_ref, ym_ref,
                 yp_ref, held_ref, used_ref, rp, low_scr, high_scr, out_scr, pop_ref, in_sems, r_sems, sems):
    first = len(BLEND)

    def copy_in(x):
        return pltpu.make_async_copy(pop_hbm.at[:, x], pop_ref.at[:, x], in_sems.at[x])

    def copy_r(x):
        return pltpu.make_async_copy(rp.at[:, x + 1, 8:40, :], r_hbm.at[:, x], r_sems.at[x])

    for x in range(XW):
        copy_in(x).start()
    lane = lax.broadcasted_iota(jnp.int32, (8, Z), 1)

    def collide_plane(x):
        copy_in(x).wait()
        for q in range(4):
            rows = slice(8 * q, 8 * q + 8)
            post = z_stream(collide([pop_ref[i, x, rows, :] for i in range(27)], lambda i: rates_ref[i]), lane)
            for i in range(27):
                rp[i, x + 1, 8 * q + 8:8 * q + 16, :] = post[i]

    for p in range(XW + 2):
        beside = jnp.max(w_ref[320 + p:321 + p, :] + w_ref[336 + p:337 + p, :])
        used_ref[p] = jnp.where(jnp.max(w_ref[YW * p:YW * p + YW, :]) + beside > 0.0, 1, 0)
    odd_x = (lax.axis_index("gx") & 1) == 1
    odd_y = (lax.axis_index("gy") & 1) == 1
    for k in range(9):
        xm_ref[k] = jnp.where(odd_x, xb_ref[k], xa_ref[k])
        xp_ref[k] = jnp.where(odd_x, xa_ref[k], xb_ref[k])
        high = jnp.where(odd_y, yb_ref[k], ya_ref[k])
        low = jnp.where(odd_y, ya_ref[k], yb_ref[k])
        ym_ref[k] = high
        yp_ref[k] = low
        high_scr[k, 1:9, :] = high
        low_scr[k, 1:9, :] = low
    def prepare(x, carry):
        collide_plane(x)
        return carry

    lax.fori_loop(0, first + 1, prepare, 0)

    def plane(x, carry):
        @pl.when(x + 1 < XW)
        def _():
            collide_plane(jnp.minimum(x + 1, XW - 1))

        for cx in (-1, 0, 1):
            @pl.when(jnp.logical_not(late(used_ref, x, cx)))
            def _():
                stream_group(rp, low_scr, high_scr, out_scr, x, cx)
                group_copy(out_scr, out_hbm, sems, x, cx).start()
        return carry

    lax.fori_loop(first, XW, plane, 0)
    for x in range(3, XW - 1):
        copy_r(x).start()
    for n, x in enumerate(HELD):
        held_ref[:, n, :, :] = rp[:, x + 1, 8:40, :]
    for x in range(3, XW - 1):
        copy_r(x).wait()
    for x in range(first, XW):
        for cx in (-1, 0, 1):
            @pl.when(jnp.logical_not(late(used_ref, x, cx)))
            def _():
                group_copy(out_scr, out_hbm, sems, x, cx).wait()


def stream_early(rates, populations, w, *borders):
    return pl.pallas_call(
        early_kernel,
        in_specs=[SMEM, HBM, VMEM] + [VMEM] * 4,
        out_specs=[HBM, HBM] + [VMEM] * 5 + [SMEM],
        out_shape=[pltpu.HBM((27, XW, YW, Z), F32)] * 2 + [pltpu.VMEM(b.shape, F32) for b in borders]
        + [pltpu.VMEM((27, len(HELD), YW, Z), F32), jax.ShapeDtypeStruct((XW + 2,), jnp.int32)],
        scratch_shapes=[
            pltpu.VMEM((27, XW + 2, 48, Z), F32),
            pltpu.VMEM((9, 16, Z), F32),
            pltpu.VMEM((9, 16, Z), F32),
            pltpu.VMEM((27, XW, YW, Z), F32),
            pltpu.VMEM((27, XW, YW, Z), F32),
            pltpu.SemaphoreType.DMA((XW,)),
            pltpu.SemaphoreType.DMA((XW,)),
            pltpu.SemaphoreType.DMA((XW, 3)),
        ],
        name="stream_early",
        compiler_params=pltpu.CompilerParams(vmem_limit_bytes=20 << 20),
        cost_estimate=pl.CostEstimate(flops=7 * 10**9, transcendentals=0, bytes_accessed=10**6),
    )(rates, far(populations), near(w), *[near(b) for b in borders])


def last_kernel(got_ref, w_ref, loading_ref, r_hbm, xm_ref, xp_ref, ym_ref, yp_ref, held_ref, used_ref, early_hbm,
                out_hbm, speed_ref,
                rp, force, load_scr, lo_scr, hi_scr, yp_scr, ym_scr, r_ref, out_scr, in_sems, sems):
    def copy_in(x):
        return pltpu.make_async_copy(r_hbm.at[:, x], r_ref.at[:, x], in_sems.at[x])

    def needed(p):
        return changed(used_ref, p - 1) | changed(used_ref, p) | changed(used_ref, p + 1)

    for x in range(3, XW - 1):
        @pl.when(needed(x))
        def _():
            copy_in(x).start()

    lane = lax.broadcasted_iota(jnp.int32, (8, Z), 1)
    profile = profile_row()
    up = jnp.where(lane == 0, -profile, pltpu.roll(profile, 1, 1))
    down = jnp.where(lane == Z - 1, -profile, pltpu.roll(profile, Z - 1, 1))
    along = (3.0 * down, 3.0 * profile, 3.0 * up)

    def got(tile, a=0, b=8):
        return got_ref[PIECE * tile + a:PIECE * tile + b, :]

    def pushes(f):
        return [f * a for a in along]

    def push(value, i, fs):
        cx = i // 9 - 1
        return value if cx == 0 else (value + fs[i % 3] if cx > 0 else value - fs[i % 3])

    load_scr[...] = jnp.zeros_like(load_scr)
    load_scr[0:1, 0:TURBINES] = loading_ref[...]
    counts = w_ref[352:360, :]
    totals = jnp.broadcast_to(jnp.sum(got_ref[pl.ds(8, NDEV, stride=PIECE), :], axis=0, keepdims=True), (8, 128))
    k = lax.broadcasted_iota(jnp.int32, (8, 128), 1)
    speed = jnp.where(k < TURBINES, totals / (jnp.where(k < TURBINES, counts, 1.0) * PROFILE_SUM), 0.0)
    speed_ref[...] = speed[0:1, 0:TURBINES]
    thrust = (0.5 * jnp.broadcast_to(load_scr[0:1, :], (8, 128))) * speed * jnp.abs(speed)
    force[...] = -lax.dot_general(
        w_ref[0:352, :] * thrust[0:1, :], jnp.ones((128, Z), F32), (((1,), (0,)), ((), ())),
        precision=lax.Precision.HIGHEST, preferred_element_type=F32)
    for scr, tile, nxt, halo, frow, cy, out in (
        (lo_scr, LO_OWN, LO_NEXT, yp_ref, 320, 1, yp_scr),
        (hi_scr, HI_OWN, HI_NEXT, ym_ref, 336, -1, ym_scr),
    ):
        scr[...] = jnp.zeros_like(scr)
        for c in range(10):
            r = 2 * c
            scr[c, 0:2, :] = got(tile + r // 8, r % 8, r % 8 + 2)
        built = rebuild([scr[c] for c in range(10)])
        ahead = rebuild_next([got(nxt, c, c + 1) for c in range(6)])
        row = lax.broadcasted_iota(jnp.int32, (8, Z), 0)
        blend = jnp.where(row == 0, BLEND[0], jnp.where(row == 1, BLEND[1], 0.0))
        fs = pushes(force[frow + 1:frow + 9, :])
        for cx in (-1, 0, 1):
            for cz in (-1, 0, 1):
                k = 3 * (cx + 1) + cz + 1
                i = slot(cx, cy, cz)
                b = built[i]
                b = b if cz == 0 else pltpu.roll(b, cz % Z, 1)
                out[k, 1:9, :] = (1.0 - blend) * push(halo[k], i, fs) + blend * b
        for cz in (-1, 0, 1):
            n = CORNERS.index((1, cy))
            out[6 + cz + 1, 0:1, :] = got(CORNER + n, cz + 1, cz + 2) + (
                force[frow:frow + 1, :] * along[cz + 1][0:1, :])
            n = CORNERS.index((-1, cy))
            value = got(CORNER + n, cz + 1, cz + 2) - force[frow + 9:frow + 10, :] * along[cz + 1][0:1, :]
            b = ahead[3 * (cy + 1) + cz + 1]
            b = b if cz == 0 else pltpu.roll(jnp.broadcast_to(b, (8, Z)), cz % Z, 1)[0:1, :]
            out[cz + 1, 9:10, :] = (1.0 - BLEND[0]) * value + BLEND[0] * b

    for q in range(4):
        rows = slice(8 * q, 8 * q + 8)
        into = slice(8 * q + 8, 8 * q + 16)
        fs = pushes(force[rows, :])
        for k in range(9):
            rp[18 + k, 0, into, :] = push(xp_ref[k, rows, :], 18 + k, fs)
        for p in range(2):
            built = z_stream(rebuild([got(OWN + (2 * k + p) * 4 + q) for k in range(10)]), lane)
            fs = pushes(force[YW * (p + 1) + 8 * q:YW * (p + 1) + 8 * q + 8, :])
            for i in range(27):
                rp[i, p + 1, into, :] = (1.0 - BLEND[p]) * push(held_ref[i, p, rows, :], i, fs) + BLEND[p] * built[i]
        for n in range(2, len(HELD)):
            x = HELD[n]
            fs = pushes(force[YW * (x + 1) + 8 * q:YW * (x + 1) + 8 * q + 8, :])
            for i in range(27):
                rp[i, x + 1, into, :] = push(held_ref[i, n, rows, :], i, fs)
        fs = pushes(force[YW * (XW + 1) + 8 * q:YW * (XW + 1) + 8 * q + 8, :])
        built = rebuild_next([got(NEXT + 4 * k + q) for k in range(6)])
        for k in range(9):
            cz = k % 3 - 1
            b = built[k] if cz == 0 else pltpu.roll(built[k], cz % Z, 1)
            rp[k, XW + 1, into, :] = (1.0 - BLEND[0]) * push(xm_ref[k, rows, :], k, fs) + BLEND[0] * b

    for x in range(3, XW - 1):
        @pl.when(needed(x))
        def _():
            copy_in(x).wait()
            for q in range(4):
                rows = slice(8 * q, 8 * q + 8)
                into = slice(8 * q + 8, 8 * q + 16)
                fs = pushes(force[YW * (x + 1) + 8 * q:YW * (x + 1) + 8 * q + 8, :])
                for i in range(27):
                    rp[i, x + 1, into, :] = push(r_ref[i, x, rows, :], i, fs)

    def plane(x, carry):
        for cx in (-1, 0, 1):
            @pl.when(late(used_ref, x, cx))
            def _():
                stream_group(rp, yp_scr, ym_scr, out_scr, x, cx)
                group_copy(out_scr, out_hbm, sems, x, cx).start()
        return carry

    lax.fori_loop(0, XW, plane, 0)
    for x in range(XW):
        for cx in (-1, 0, 1):
            @pl.when(late(used_ref, x, cx))
            def _():
                group_copy(out_scr, out_hbm, sems, x, cx).wait()


def after_exchange(*args):
    return pl.pallas_call(
        last_kernel,
        in_specs=[HBM if n in (3, 10) else SMEM if n == 9 else VMEM for n in range(len(args))],
        input_output_aliases={10: 0},
        out_specs=[HBM, VMEM],
        out_shape=[pltpu.HBM((27, XW, YW, Z), F32), jax.ShapeDtypeStruct((1, TURBINES), F32)],
        scratch_shapes=[
            pltpu.VMEM((27, XW + 2, 48, Z), F32),
            pltpu.VMEM((352, Z), F32),
            pltpu.VMEM((8, 128), F32),
            pltpu.VMEM((10, 8, Z), F32),
            pltpu.VMEM((10, 8, Z), F32),
            pltpu.VMEM((9, 16, Z), F32),
            pltpu.VMEM((9, 16, Z), F32),
            pltpu.VMEM((27, XW, YW, Z), F32),
            pltpu.VMEM((27, XW, YW, Z), F32),
            pltpu.SemaphoreType.DMA((XW,)),
            pltpu.SemaphoreType.DMA((XW, 3)),
        ],
        name="after_exchange",
        compiler_params=pltpu.CompilerParams(vmem_limit_bytes=24 << 20),
    )(*[far(a) if n in (3, 10) else a if n == 9 else near(a) for n, a in enumerate(args)])


def body(populations, precursor, pairing, rates, loading, disc_cols, disc_turb):
    both = ("gx", "gy")
    inner = lambda n: [(i, i ^ 1) for i in range(n)]
    outer = lambda n: [(i, (i + (1 if i % 2 else -1)) % n) for i in range(n)]
    send, xa, xb, ya, yb = before_exchange(rates, populations, precursor)
    got = lax.all_to_all(send, both, 0, 0, tiled=True)
    w, disc = disc_sums(disc_cols.reshape(1, SLOTS), disc_turb.reshape(1, SLOTS), populations)
    xb = lax.ppermute(xb, "gx", outer(GX))
    xa = lax.ppermute(xa, "gx", inner(GX))
    yb = lax.ppermute(yb, "gy", outer(GY))
    ya = lax.ppermute(ya, "gy", inner(GY))
    send = route(pairing, got, disc)
    send = send.reshape(NDEV, PIECE, 1, Z)
    got = lax.all_to_all(send, both, 0, 0, tiled=True).reshape(NDEV * PIECE, Z)
    read, r, *rest = stream_early(rates, populations, w, xa, xb, ya, yb)
    read, speed = after_exchange(got, w, loading.reshape(1, TURBINES), r, *rest, read)
    return read, speed.reshape(TURBINES)


def solution(mesh):
    in_specs = (P(None, "gx", "gy", None), P(None, "gx", "gy", None), P(), P(), P(), P(), P())
    out_specs = (P(None, "gx", "gy", None), P())
    return jax.shard_map(body, mesh=mesh, in_specs=in_specs, out_specs=out_specs, check_vma=False)
```

```python
import jax
import jax.numpy as jnp
import numpy as np
from jax import lax
from jax.experimental import pallas as pl
from jax.experimental.pallas import tpu as pltpu
from jax.sharding import PartitionSpec as P

GX, GY = 32, 4
NDEV = GX * GY
XW, YW, Z = 8, 32, 128
NY_ALL, NX_ALL = 128, 256
SLOTS = 512
TURBINES = 32
F32 = jnp.float32

OWN, NEXT, LO_OWN, HI_OWN, LO_NEXT, HI_NEXT, CORNER = 0, 80, 104, 107, 110, 111, 112
PIECE = 9
CORNERS = ((-1, -1), (-1, 1), (1, -1), (1, 1))
W_ROWS = 360
BLEND = (0.5, 0.25)

PROFILE_SUM = float(np.sum(np.exp(-np.square((np.arange(Z) - Z / 3.0) / (Z / 6.0)))))


HBM = pl.BlockSpec(memory_space=pltpu.HBM)
SMEM = pl.BlockSpec(memory_space=pltpu.SMEM)
VMEM = pl.BlockSpec(memory_space=pltpu.VMEM)


def near(array):
    return pltpu.with_memory_space_constraint(array, pltpu.VMEM)


def far(array):
    return pltpu.with_memory_space_constraint(array, pltpu.HBM)


def slot(cx, cy, cz):
    return 9 * (cx + 1) + 3 * (cy + 1) + (cz + 1)


def profile_row():
    heights = lax.broadcasted_iota(jnp.int32, (8, Z), 1).astype(F32)
    return jnp.exp(-jnp.square((heights - Z / 3.0) * (6.0 / Z)))


def forward(g):
    for stride in (1, 3, 9):
        out = list(g)
        for i in range(27):
            if (i // stride) % 3 == 0:
                a, b, c = g[i], g[i + stride], g[i + 2 * stride]
                s = c + a
                out[i] = s + 4.0 * b
                out[i + stride] = c - a
                out[i + 2 * stride] = s
        g = out
    return g


def backward(m):
    for stride in (9, 3, 1):
        out = list(m)
        for i in range(27):
            if (i // stride) % 3 == 0:
                a, b, c = m[i], m[i + stride], m[i + 2 * stride]
                out[i] = c - b
                out[i + stride] = 0.5 * (a - c)
                out[i + 2 * stride] = c + b
        m = out
    return m


def collide(g, rates):
    return relax(forward(g), rates)


def relax(m, rates):
    density = m[0] * (1.0 / 216.0)
    inv = 1.0 / m[0]
    u = (m[9] * inv, m[3] * inv, m[1] * inv)
    j = (m[9] * (1.0 / 216.0), m[3] * (1.0 / 216.0), m[1] * (1.0 / 216.0))
    ju = {}
    for a in range(3):
        for b in range(a, 3):
            ju[(a, b)] = j[a] * u[b]
    out = []
    for i in range(27):
        order = (i // 9, i // 3 % 3, i % 3)
        ones = [d for d in range(3) if order[d] == 1]
        twos = [d for d in range(3) if order[d] == 2]
        if i in (0, 1, 3, 9):
            out.append(m[i] * 0.125)
            continue
        r = rates(i)
        keep = m[i] * ((1.0 - r) * 0.125)
        if len(ones) == 3:
            out.append(keep)
            continue
        scale = r * (27.0 / 3.0 ** len(twos))
        if len(ones) == 0:
            eq = ju[(twos[0], twos[0])]
            for d in twos[1:]:
                eq = eq + ju[(d, d)]
            eq = density + 3.0 * eq
        elif len(ones) == 1:
            eq = j[ones[0]]
        else:
            eq = ju[(ones[0], ones[1])]
        out.append(keep + eq * scale)
    return backward(out)


def z_stream(p, lane):
    out = []
    for i in range(27):
        cz = i % 3 - 1
        if cz == 0:
            out.append(p[i])
        elif cz == 1:
            out.append(jnp.where(lane == 0, p[26 - i], pltpu.roll(p[i], 1, 1)))
        else:
            out.append(jnp.where(lane == Z - 1, p[26 - i], pltpu.roll(p[i], Z - 1, 1)))
    return out


def precursor_coefficients(g):
    m = forward(g)
    rho, jx, jy, jz = m[0], m[9], m[3], m[1]
    xx, yy, zz, xy, xz, yz = m[18], m[6], m[2], m[12], m[10], m[4]
    third = rho * (1.0 / 3.0)
    pxx, pyy, pzz = xx - third, yy - third, zz - third
    s = 1.0 / 216.0
    k0 = (rho - 1.5 * (pxx + pyy + pzz)) * s
    return [k0, jx * (3 * s), jy * (3 * s), jz * (3 * s), pxx * (4.5 * s), pyy * (4.5 * s), pzz * (4.5 * s),
            xy * (9 * s), xz * (9 * s), yz * (9 * s)]


def next_coefficients(c):
    return [c[0] - c[1] + c[4], c[2] - c[7], c[3] - c[8], c[5], c[6], c[9]]


def rebuild_next(c):
    out = []
    for cy in (-1, 0, 1):
        base = c[0] + (cy * c[1] + c[3] if cy else 0.0)
        lin = c[2] + cy * c[5] if cy else c[2]
        for cz in (-1, 0, 1):
            out.append(base + cz * lin + c[4] if cz else base)
    return out


def rebuild(c):
    out = []
    for cx in (-1, 0, 1):
        base = c[0] + cx * c[1] + c[4] if cx else c[0]
        liny = c[2] + cx * c[7] if cx else c[2]
        linz = c[3] + cx * c[8] if cx else c[3]
        out += rebuild_next([base, liny, linz, c[5], c[6], c[9]])
    return out


def first_kernel(rates_hbm, pop_hbm, pre_hbm, send_hbm, xa_ref, xb_ref, ya_ref, yb_ref, pre_ref, edge_ref, side_ref,
                 rates_ref, send_ref, sems):
    copies = [pltpu.make_async_copy(pre_hbm.at[:, p], pre_ref.at[:, p], sems.at[p]) for p in range(2)]
    for n, x in enumerate((0, XW - 1)):
        copies.append(pltpu.make_async_copy(pop_hbm.at[:, x], edge_ref.at[:, n], sems.at[2 + n]))
    copies.append(pltpu.make_async_copy(rates_hbm, rates_ref, sems.at[4]))
    for n, y in enumerate((0, YW - 1)):
        copies.append(pltpu.make_async_copy(pop_hbm.at[:, :, y, :], side_ref.at[n], sems.at[5 + n]))
    for copy in copies:
        copy.start()
    send_ref[LO_OWN:, :, :] = jnp.zeros((NDEV - LO_OWN, 8, Z), F32)
    for p in range(2):
        copies[p].wait()
        for q in range(4):
            c = precursor_coefficients([pre_ref[i, p, 8 * q:8 * q + 8, :] for i in range(27)])
            for k in range(10):
                send_ref[OWN + (2 * k + p) * 4 + q, :, :] = c[k]
                row = 2 * k + p
                if q == 3:
                    send_ref[LO_OWN + row // 8, row % 8:row % 8 + 1, :] = c[k][7:8, :]
                if q == 0:
                    send_ref[HI_OWN + row // 8, row % 8:row % 8 + 1, :] = c[k][0:1, :]
            if p == 0:
                c = next_coefficients(c)
                for k in range(6):
                    send_ref[NEXT + 4 * k + q, :, :] = c[k]
                    if q == 3:
                        send_ref[LO_NEXT, k:k + 1, :] = c[k][7:8, :]
                    if q == 0:
                        send_ref[HI_NEXT, k:k + 1, :] = c[k][0:1, :]
    sends = [pltpu.make_async_copy(send_ref.at[0:LO_OWN], send_hbm.at[0:LO_OWN], sems.at[7]),
             pltpu.make_async_copy(send_ref.at[LO_OWN:NDEV], send_hbm.at[LO_OWN:NDEV], sems.at[8])]
    sends[0].start()
    copies[4].wait()
    lane = lax.broadcasted_iota(jnp.int32, (8, Z), 1)
    odd_x = (lax.axis_index("gx") & 1) == 1
    for n, cx in enumerate((-1, 1)):
        copies[2 + n].wait()
        for q in range(4):
            rows = slice(8 * q, 8 * q + 8)
            post = z_stream(collide([edge_ref[i, n, rows, :] for i in range(27)], lambda i: rates_ref[i]), lane)
            for k in range(9):
                value = post[9 * (cx + 1) + k]
                if cx < 0:
                    xa_ref[k, rows, :] = value
                else:
                    keep = xa_ref[k, rows, :]
                    xa_ref[k, rows, :] = jnp.where(odd_x, keep, value)
                    xb_ref[k, rows, :] = jnp.where(odd_x, value, keep)
    odd_y = (lax.axis_index("gy") & 1) == 1
    for n, cy in enumerate((-1, 1)):
        copies[5 + n].wait()
        post = z_stream(collide([side_ref[n, i] for i in range(27)], lambda i: rates_ref[i]), lane)
        for cx in (-1, 0, 1):
            for cz in (-1, 0, 1):
                k = 3 * (cx + 1) + cz + 1
                value = post[slot(cx, cy, cz)]
                if cy < 0:
                    ya_ref[k, :, :] = value
                else:
                    keep = ya_ref[k, :, :]
                    ya_ref[k, :, :] = jnp.where(odd_y, keep, value)
                    yb_ref[k, :, :] = jnp.where(odd_y, value, keep)
                if cx:
                    at = 0 if cx < 0 else XW - 1
                    send_ref[CORNER + CORNERS.index((cx, cy)), cz + 1:cz + 2, :] = value[at:at + 1, :]
    sends[1].start()
    for copy in sends:
        copy.wait()


def before_exchange(rates, populations, precursor):
    return pl.pallas_call(
        first_kernel,
        in_specs=[HBM, HBM, HBM],
        out_specs=[HBM] + [VMEM] * 4,
        out_shape=[pltpu.HBM((NDEV, 8, Z), F32)] + [pltpu.VMEM((9, n, Z), F32) for n in (YW, YW, XW, XW)],
        scratch_shapes=[
            pltpu.VMEM((27, 2, YW, Z), F32),
            pltpu.VMEM((27, 2, YW, Z), F32),
            pltpu.VMEM((2, 27, XW, Z), F32),
            pltpu.SMEM((27,), F32),
            pltpu.VMEM((NDEV, 8, Z), F32),
            pltpu.SemaphoreType.DMA((9,)),
        ],
        name="before_exchange",
        compiler_params=pltpu.CompilerParams(vmem_limit_bytes=4 << 20),
    )(far(rates), far(populations), far(precursor))


def collide_kernel(rates_ref, cols_ref, turb_ref, pop_hbm, out_hbm, w_ref, disc_ref,
                   pop_ref, out_ref, in_sems, out_sems):
    def copy_in(x):
        return pltpu.make_async_copy(pop_hbm.at[:, x], pop_ref.at[:, x], in_sems.at[x])

    def copy_out(x):
        return pltpu.make_async_copy(out_ref.at[:, x], out_hbm.at[:, x], out_sems.at[x])

    for x in range(XW):
        copy_in(x).start()
    gx = lax.axis_index("gx")
    gy = lax.axis_index("gy")
    rows = lax.broadcasted_iota(jnp.int32, (W_ROWS, SLOTS), 0)
    lo = rows - 320
    main = rows < 320
    xx = jnp.where(main, rows >> 5, jnp.where(lo < 16, lo, lo - 16))
    yy = jnp.where(main, rows & 31, jnp.where(lo < 16, -1, YW))
    col = ((gx * XW + xx - 1) & (NX_ALL - 1)) * NY_ALL + ((gy * YW + yy) & (NY_ALL - 1))
    valid = main | ((lo & 15) < 10)
    hit = ((col == cols_ref[...]) & valid & (lo < 32)) | (lo >= 32)
    owner = lax.broadcasted_iota(jnp.int32, (128, SLOTS), 0) == turb_ref[...]
    w_ref[...] = lax.dot_general(
        jnp.where(hit, 1.0, 0.0).astype(jnp.bfloat16),
        jnp.where(owner, 1.0, 0.0).astype(jnp.bfloat16),
        (((1,), (1,)), ((), ())), preferred_element_type=F32)
    disc_ref[...] = jnp.zeros_like(disc_ref)
    lane = lax.broadcasted_iota(jnp.int32, (8, Z), 1)
    profile = profile_row()

    def plane(x, carry):
        copy_in(x).wait()
        for q in range(4):
            rows = slice(8 * q, 8 * q + 8)
            m = forward([pop_ref[i, x, rows, :] for i in range(27)])
            sums = jnp.sum(m[9] / m[0] * profile, axis=1, keepdims=True)
            disc_ref[...] += sums * w_ref[pl.ds(pl.multiple_of((x + 1) * YW + 8 * q, 8), 8), :]
            post = z_stream(relax(m, lambda i: rates_ref[i]), lane)
            for i in range(27):
                out_ref[i, x, rows, :] = post[i]
        copy_out(x).start()
        return carry

    lax.fori_loop(0, XW, plane, 0)
    for x in range(XW):
        copy_out(x).wait()


def collision(rates, cols, turb, populations):
    shapes = ((27, XW, YW, Z), (W_ROWS, 128), (8, 128))
    return pl.pallas_call(
        collide_kernel,
        in_specs=[SMEM, VMEM, VMEM, HBM],
        out_specs=[HBM] + [VMEM] * (len(shapes) - 1),
        out_shape=[pltpu.HBM(shapes[0], F32)] + [pltpu.VMEM(shape, F32) for shape in shapes[1:]],
        scratch_shapes=[
            pltpu.VMEM(shapes[0], F32),
            pltpu.VMEM(shapes[0], F32),
            pltpu.SemaphoreType.DMA((XW,)),
            pltpu.SemaphoreType.DMA((XW,)),
        ],
        name="collision",
        compiler_params=pltpu.CompilerParams(vmem_limit_bytes=12 << 20),
    )(rates, cols, turb, far(populations))


def route_kernel(pairing_ref, got_ref, disc_ref, send_hbm, send_ref, sems):
    me = lax.axis_index("gx") * GY + lax.axis_index("gy")
    is_next = ((me >= NEXT) & (me < LO_OWN)) | (me == LO_NEXT) | (me == HI_NEXT)
    corner = me - CORNER
    is_corner = (corner >= 0) & (corner < 4)
    low = ((me >= LO_OWN) & (me < HI_OWN)) | (me == LO_NEXT)
    high = ((me >= HI_OWN) & (me < LO_NEXT)) | (me == HI_NEXT)
    from_x = jnp.where(corner < 2, 1, -1)
    from_y = jnp.where(is_corner, jnp.where((corner & 1) == 0, 1, -1), jnp.where(low, -1, jnp.where(high, 1, 0)))
    ahead = jnp.where(is_next, 1, 0)
    lanes = [(t + from_y) & (GY - 1) for t in range(GY)]
    part = jnp.sum(disc_ref[...], axis=0, keepdims=True)
    copies = []
    for d in range(GX):
        tile = pairing_ref[(d + ahead) & (GX - 1)]
        tile = jnp.where(is_corner, (d + from_x) & (GX - 1), tile) * GY
        for t in range(GY):
            at = (d * GY + t) * PIECE
            send_ref[at:at + 8, :] = got_ref[tile + lanes[t], :, :]
            send_ref[at + 8:at + 9, :] = part
        if d % 8 == 7:
            rows = slice((d - 7) * GY * PIECE, (d + 1) * GY * PIECE)
            copies.append(pltpu.make_async_copy(send_ref.at[rows], send_hbm.at[rows], sems.at[d // 8]))
            copies[-1].start()
    for copy in copies:
        copy.wait()


def route(pairing, got, disc):
    return pl.pallas_call(
        route_kernel,
        in_specs=[SMEM, VMEM, VMEM],
        out_specs=HBM,
        out_shape=pltpu.HBM((NDEV * PIECE, Z), F32),
        scratch_shapes=[pltpu.VMEM((NDEV * PIECE, Z), F32), pltpu.SemaphoreType.DMA((GX // 8,))],
        name="route",
        compiler_params=pltpu.CompilerParams(vmem_limit_bytes=3 << 20),
    )(pairing, near(got), near(disc))


def changed(used_ref, p):
    return (p == 0) | (p == 1) | (p == XW) | (used_ref[p + 1] > 0)


def late(used_ref, x, cx):
    if cx == 0:
        return x < len(BLEND)
    return changed(used_ref, x) | changed(used_ref, x - cx)


def stream_group(rp, low_scr, high_scr, out_scr, x, cx):
    lane = lax.broadcasted_iota(jnp.int32, (YW, Z), 1)
    row = lax.broadcasted_iota(jnp.int32, (YW, Z), 0)
    at = x + 1 - cx
    for cy in (-1, 0, 1):
        for cz in (-1, 0, 1):
            i = slot(cx, cy, cz)
            k = 3 * (cx + 1) + cz + 1
            value = rp[i, at, 8 - cy:40 - cy, :]
            if cy == 1:
                value = jnp.where(row == 0, low_scr[k, pl.ds(at, 1), :], value)
            elif cy == -1:
                value = jnp.where(row == YW - 1, high_scr[k, pl.ds(at, 1), :], value)
            if cz != 0 and (cx != 0 or cy != 0):
                value = jnp.where(lane == (0 if cz == 1 else Z - 1), rp[i, x + 1, 8:40, :], value)
            out_scr[i, x, :, :] = value


def group_copy(out_scr, out_hbm, sems, x, cx):
    group = slice(9 * (cx + 1), 9 * (cx + 2))
    return pltpu.make_async_copy(out_scr.at[group, x], out_hbm.at[group, x], sems.at[x, cx + 1])


HELD = (0, 1, 2, XW - 1)


def early_kernel(w_ref, r_hbm, xa_ref, xb_ref, ya_ref, yb_ref, out_hbm, xm_ref, xp_ref, ym_ref, yp_ref, held_ref,
                 used_ref, rp, low_scr, high_scr, out_scr, in_sems, held_sems, sems):
    first = len(BLEND)

    def copy_in(x):
        return pltpu.make_async_copy(r_hbm.at[:, x], rp.at[:, x + 1, 8:40, :], in_sems.at[x])

    for x in range(first, XW):
        copy_in(x).start()
    holds = [pltpu.make_async_copy(r_hbm.at[:, x], held_ref.at[:, n], held_sems.at[n]) for n, x in enumerate(HELD)]
    for copy in holds:
        copy.start()
    for p in range(XW + 2):
        beside = jnp.max(w_ref[320 + p:321 + p, :] + w_ref[336 + p:337 + p, :])
        used_ref[p] = jnp.where(jnp.max(w_ref[YW * p:YW * p + YW, :]) + beside > 0.0, 1, 0)
    odd_x = (lax.axis_index("gx") & 1) == 1
    odd_y = (lax.axis_index("gy") & 1) == 1
    for k in range(9):
        xm_ref[k] = jnp.where(odd_x, xb_ref[k], xa_ref[k])
        xp_ref[k] = jnp.where(odd_x, xa_ref[k], xb_ref[k])
        high = jnp.where(odd_y, yb_ref[k], ya_ref[k])
        low = jnp.where(odd_y, ya_ref[k], yb_ref[k])
        ym_ref[k] = high
        yp_ref[k] = low
        high_scr[k, 1:9, :] = high
        low_scr[k, 1:9, :] = low
    copy_in(first).wait()

    def plane(x, carry):
        @pl.when(x + 1 < XW)
        def _():
            copy_in(jnp.minimum(x + 1, XW - 1)).wait()

        for cx in (-1, 0, 1):
            @pl.when(jnp.logical_not(late(used_ref, x, cx)))
            def _():
                stream_group(rp, low_scr, high_scr, out_scr, x, cx)
                group_copy(out_scr, out_hbm, sems, x, cx).start()
        return carry

    lax.fori_loop(first, XW, plane, 0)
    for copy in holds:
        copy.wait()
    for x in range(first, XW):
        for cx in (-1, 0, 1):
            @pl.when(jnp.logical_not(late(used_ref, x, cx)))
            def _():
                group_copy(out_scr, out_hbm, sems, x, cx).wait()


def stream_early(w, r, *borders):
    return pl.pallas_call(
        early_kernel,
        in_specs=[VMEM, HBM] + [VMEM] * 4,
        out_specs=[HBM] + [VMEM] * 5 + [SMEM],
        out_shape=[pltpu.HBM((27, XW, YW, Z), F32)] + [pltpu.VMEM(b.shape, F32) for b in borders]
        + [pltpu.VMEM((27, len(HELD), YW, Z), F32), jax.ShapeDtypeStruct((XW + 2,), jnp.int32)],
        scratch_shapes=[
            pltpu.VMEM((27, XW + 2, 48, Z), F32),
            pltpu.VMEM((9, 16, Z), F32),
            pltpu.VMEM((9, 16, Z), F32),
            pltpu.VMEM((27, XW, YW, Z), F32),
            pltpu.SemaphoreType.DMA((XW,)),
            pltpu.SemaphoreType.DMA((len(HELD),)),
            pltpu.SemaphoreType.DMA((XW, 3)),
        ],
        name="stream_early",
        compiler_params=pltpu.CompilerParams(vmem_limit_bytes=16 << 20),
        cost_estimate=pl.CostEstimate(flops=7 * 10**9, transcendentals=0, bytes_accessed=10**6),
    )(near(w), far(r), *[near(b) for b in borders])


def last_kernel(got_ref, w_ref, loading_ref, r_hbm, xm_ref, xp_ref, ym_ref, yp_ref, held_ref, used_ref, early_hbm,
                out_hbm, speed_ref,
                rp, force, load_scr, lo_scr, hi_scr, yp_scr, ym_scr, r_ref, out_scr, in_sems, sems):
    def copy_in(x):
        return pltpu.make_async_copy(r_hbm.at[:, x], r_ref.at[:, x], in_sems.at[x])

    def needed(p):
        return changed(used_ref, p - 1) | changed(used_ref, p) | changed(used_ref, p + 1)

    for x in range(3, XW - 1):
        @pl.when(needed(x))
        def _():
            copy_in(x).start()

    lane = lax.broadcasted_iota(jnp.int32, (8, Z), 1)
    profile = profile_row()
    up = jnp.where(lane == 0, -profile, pltpu.roll(profile, 1, 1))
    down = jnp.where(lane == Z - 1, -profile, pltpu.roll(profile, Z - 1, 1))
    along = (3.0 * down, 3.0 * profile, 3.0 * up)

    def got(tile, a=0, b=8):
        return got_ref[PIECE * tile + a:PIECE * tile + b, :]

    def pushes(f):
        return [f * a for a in along]

    def push(value, i, fs):
        cx = i // 9 - 1
        return value if cx == 0 else (value + fs[i % 3] if cx > 0 else value - fs[i % 3])

    load_scr[...] = jnp.zeros_like(load_scr)
    load_scr[0:1, 0:TURBINES] = loading_ref[...]
    counts = w_ref[352:360, :]
    totals = jnp.broadcast_to(jnp.sum(got_ref[pl.ds(8, NDEV, stride=PIECE), :], axis=0, keepdims=True), (8, 128))
    k = lax.broadcasted_iota(jnp.int32, (8, 128), 1)
    speed = jnp.where(k < TURBINES, totals / (jnp.where(k < TURBINES, counts, 1.0) * PROFILE_SUM), 0.0)
    speed_ref[...] = speed[0:1, 0:TURBINES]
    thrust = (0.5 * jnp.broadcast_to(load_scr[0:1, :], (8, 128))) * speed * jnp.abs(speed)
    force[...] = -lax.dot_general(
        w_ref[0:352, :] * thrust[0:1, :], jnp.ones((128, Z), F32), (((1,), (0,)), ((), ())),
        precision=lax.Precision.HIGHEST, preferred_element_type=F32)
    for scr, tile, nxt, halo, frow, cy, out in (
        (lo_scr, LO_OWN, LO_NEXT, yp_ref, 320, 1, yp_scr),
        (hi_scr, HI_OWN, HI_NEXT, ym_ref, 336, -1, ym_scr),
    ):
        scr[...] = jnp.zeros_like(scr)
        for c in range(10):
            r = 2 * c
            scr[c, 0:2, :] = got(tile + r // 8, r % 8, r % 8 + 2)
        built = rebuild([scr[c] for c in range(10)])
        ahead = rebuild_next([got(nxt, c, c + 1) for c in range(6)])
        row = lax.broadcasted_iota(jnp.int32, (8, Z), 0)
        blend = jnp.where(row == 0, BLEND[0], jnp.where(row == 1, BLEND[1], 0.0))
        fs = pushes(force[frow + 1:frow + 9, :])
        for cx in (-1, 0, 1):
            for cz in (-1, 0, 1):
                k = 3 * (cx + 1) + cz + 1
                i = slot(cx, cy, cz)
                b = built[i]
                b = b if cz == 0 else pltpu.roll(b, cz % Z, 1)
                out[k, 1:9, :] = (1.0 - blend) * push(halo[k], i, fs) + blend * b
        for cz in (-1, 0, 1):
            n = CORNERS.index((1, cy))
            out[6 + cz + 1, 0:1, :] = got(CORNER + n, cz + 1, cz + 2) + (
                force[frow:frow + 1, :] * along[cz + 1][0:1, :])
            n = CORNERS.index((-1, cy))
            value = got(CORNER + n, cz + 1, cz + 2) - force[frow + 9:frow + 10, :] * along[cz + 1][0:1, :]
            b = ahead[3 * (cy + 1) + cz + 1]
            b = b if cz == 0 else pltpu.roll(jnp.broadcast_to(b, (8, Z)), cz % Z, 1)[0:1, :]
            out[cz + 1, 9:10, :] = (1.0 - BLEND[0]) * value + BLEND[0] * b

    for q in range(4):
        rows = slice(8 * q, 8 * q + 8)
        into = slice(8 * q + 8, 8 * q + 16)
        fs = pushes(force[rows, :])
        for k in range(9):
            rp[18 + k, 0, into, :] = push(xp_ref[k, rows, :], 18 + k, fs)
        for p in range(2):
            built = z_stream(rebuild([got(OWN + (2 * k + p) * 4 + q) for k in range(10)]), lane)
            fs = pushes(force[YW * (p + 1) + 8 * q:YW * (p + 1) + 8 * q + 8, :])
            for i in range(27):
                rp[i, p + 1, into, :] = (1.0 - BLEND[p]) * push(held_ref[i, p, rows, :], i, fs) + BLEND[p] * built[i]
        for n in range(2, len(HELD)):
            x = HELD[n]
            fs = pushes(force[YW * (x + 1) + 8 * q:YW * (x + 1) + 8 * q + 8, :])
            for i in range(27):
                rp[i, x + 1, into, :] = push(held_ref[i, n, rows, :], i, fs)
        fs = pushes(force[YW * (XW + 1) + 8 * q:YW * (XW + 1) + 8 * q + 8, :])
        built = rebuild_next([got(NEXT + 4 * k + q) for k in range(6)])
        for k in range(9):
            cz = k % 3 - 1
            b = built[k] if cz == 0 else pltpu.roll(built[k], cz % Z, 1)
            rp[k, XW + 1, into, :] = (1.0 - BLEND[0]) * push(xm_ref[k, rows, :], k, fs) + BLEND[0] * b

    for x in range(3, XW - 1):
        @pl.when(needed(x))
        def _():
            copy_in(x).wait()
            for q in range(4):
                rows = slice(8 * q, 8 * q + 8)
                into = slice(8 * q + 8, 8 * q + 16)
                fs = pushes(force[YW * (x + 1) + 8 * q:YW * (x + 1) + 8 * q + 8, :])
                for i in range(27):
                    rp[i, x + 1, into, :] = push(r_ref[i, x, rows, :], i, fs)

    def plane(x, carry):
        for cx in (-1, 0, 1):
            @pl.when(late(used_ref, x, cx))
            def _():
                stream_group(rp, yp_scr, ym_scr, out_scr, x, cx)
                group_copy(out_scr, out_hbm, sems, x, cx).start()
        return carry

    lax.fori_loop(0, XW, plane, 0)
    for x in range(XW):
        for cx in (-1, 0, 1):
            @pl.when(late(used_ref, x, cx))
            def _():
                group_copy(out_scr, out_hbm, sems, x, cx).wait()


def after_exchange(*args):
    return pl.pallas_call(
        last_kernel,
        in_specs=[HBM if n in (3, 10) else SMEM if n == 9 else VMEM for n in range(len(args))],
        input_output_aliases={10: 0},
        out_specs=[HBM, VMEM],
        out_shape=[pltpu.HBM((27, XW, YW, Z), F32), jax.ShapeDtypeStruct((1, TURBINES), F32)],
        scratch_shapes=[
            pltpu.VMEM((27, XW + 2, 48, Z), F32),
            pltpu.VMEM((352, Z), F32),
            pltpu.VMEM((8, 128), F32),
            pltpu.VMEM((10, 8, Z), F32),
            pltpu.VMEM((10, 8, Z), F32),
            pltpu.VMEM((9, 16, Z), F32),
            pltpu.VMEM((9, 16, Z), F32),
            pltpu.VMEM((27, XW, YW, Z), F32),
            pltpu.VMEM((27, XW, YW, Z), F32),
            pltpu.SemaphoreType.DMA((XW,)),
            pltpu.SemaphoreType.DMA((XW, 3)),
        ],
        name="after_exchange",
        compiler_params=pltpu.CompilerParams(vmem_limit_bytes=24 << 20),
    )(*[far(a) if n in (3, 10) else a if n == 9 else near(a) for n, a in enumerate(args)])


def body(populations, precursor, pairing, rates, loading, disc_cols, disc_turb):
    both = ("gx", "gy")
    inner = lambda n: [(i, i ^ 1) for i in range(n)]
    outer = lambda n: [(i, (i + (1 if i % 2 else -1)) % n) for i in range(n)]
    send, xa, xb, ya, yb = before_exchange(rates, populations, precursor)
    got = lax.all_to_all(send, both, 0, 0, tiled=True)
    r, w, disc = collision(
        rates, disc_cols.reshape(1, SLOTS), disc_turb.reshape(1, SLOTS), populations)
    xb = lax.ppermute(xb, "gx", outer(GX))
    disc, xa = lax.optimization_barrier((disc, xa))
    xa = lax.ppermute(xa, "gx", inner(GX))
    yb = lax.ppermute(yb, "gy", outer(GY))
    ya = lax.ppermute(ya, "gy", inner(GY))
    send = route(pairing, got, disc).reshape(NDEV, PIECE, 1, Z)
    got = lax.all_to_all(send, both, 0, 0, tiled=True).reshape(NDEV * PIECE, Z)
    read, *rest = stream_early(w, r, xa, xb, ya, yb)
    read, speed = after_exchange(got, w, loading.reshape(1, TURBINES), r, *rest, read)
    return read, speed.reshape(TURBINES)


def solution(mesh):
    in_specs = (P(None, "gx", "gy", None), P(None, "gx", "gy", None), P(), P(), P(), P(), P())
    out_specs = (P(None, "gx", "gy", None), P())
    return jax.shard_map(body, mesh=mesh, in_specs=in_specs, out_specs=out_specs, check_vma=False)
```
